32 devices in a mesh: dp: 8 (over z, x), code: 4 (over y, core).
Axes of the slice: x: 2, y: 2, z: 4, core: 2. Of those that a mesh axis runs over, the one named last changes fastest.
Arguments:
- tokens: int32 [2, 8, 4, 256], P(None, 'dp'), may hold values from 0 to 1023
- masked: int32 [2, 8, 4, 256], P(None, 'dp'), may hold values from 0 to 1, as said below
- small_grid: int32 [2, 8], P(None, 'dp'), may hold values from 0 to 1, as said below
- domains: int32 [2, 8, 4], P(None, 'dp'), may hold values from 0 to 3, as said below
- attend_in: float32 [2, 1024, 3072], P(None, ('dp', 'code')), may hold values from -0.1875 to 0.1875
- attend_out: float32 [2, 1024, 1024], P(None, ('dp', 'code')), may hold values from -0.75 to 0.75
- expand: float32 [1024, 4096], P(('dp', 'code')), may hold values from -0.1875 to 0.1875
- contract: float32 [4096, 1024], P(('dp', 'code')), may hold values from -0.09375 to 0.09375
- gains: float32 [5, 1024], P(None, ('dp', 'code')), may hold values from 0.1 to 1.9
- tables: float32 [2, 1024, 1024], P(None, 'code'), may hold values from -0.1875 to 0.1875
- mean_in: float32 [2, 1024, 3072], P(None, ('dp', 'code')), may hold values from -7.1525574e-07 to 7.1525574e-07
- mean_out: float32 [2, 1024, 1024], P(None, ('dp', 'code')), may hold values from -7.1525574e-07 to 7.1525574e-07
- mean_expand: float32 [1024, 4096], P(('dp', 'code')), may hold values from -7.1525574e-07 to 7.1525574e-07
- mean_contract: float32 [4096, 1024], P(('dp', 'code')), may hold values from -7.1525574e-07 to 7.1525574e-07
- mean_gains: float32 [5, 1024], P(None, ('dp', 'code')), may hold values from -7.6293945e-06 to 7.6293945e-06
- mean_tables: float32 [2, 1024, 1024], P(None, 'code'), may hold values from -7.1525574e-07 to 7.1525574e-07
- square_in: float32 [2, 1024, 3072], P(None, ('dp', 'code')), may hold values from 6.965231e-14 to 2.7874166e-13
- square_out: float32 [2, 1024, 1024], P(None, ('dp', 'code')), may hold values from 6.965231e-14 to 2.7874166e-13
- square_expand: float32 [1024, 4096], P(('dp', 'code')), may hold values from 6.965231e-14 to 2.7874166e-13
- square_contract: float32 [4096, 1024], P(('dp', 'code')), may hold values from 6.965231e-14 to 2.7874166e-13
- square_gains: float32 [5, 1024], P(None, ('dp', 'code')), may hold values from 6.9652313e-12 to 2.7874167e-11
- square_tables: float32 [2, 1024, 1024], P(None, 'code'), may hold values from 6.965231e-14 to 2.7874166e-13
Outputs:
- total_loss: float32 [], replicated
- gradient_norm: float32 [], replicated
- updated_in: float32 [2, 1024, 3072], P(None, ('dp', 'code'))
- updated_out: float32 [2, 1024, 1024], P(None, ('dp', 'code'))
- updated_expand: float32 [1024, 4096], P(('dp', 'code'))
- updated_contract: float32 [4096, 1024], P(('dp', 'code'))
- updated_gains: float32 [5, 1024], P(None, ('dp', 'code'))
- updated_tables: float32 [2, 1024, 1024], P(None, 'code')
- averaged_in: float32 [2, 1024, 3072], P(None, ('dp', 'code'))
- averaged_out: float32 [2, 1024, 1024], P(None, ('dp', 'code'))
- averaged_expand: float32 [1024, 4096], P(('dp', 'code'))
- averaged_contract: float32 [4096, 1024], P(('dp', 'code'))
- averaged_gains: float32 [5, 1024], P(None, ('dp', 'code'))
- averaged_tables: float32 [2, 1024, 1024], P(None, 'code')
- squared_in: float32 [2, 1024, 3072], P(None, ('dp', 'code'))
- squared_out: float32 [2, 1024, 1024], P(None, ('dp', 'code'))
- squared_expand: float32 [1024, 4096], P(('dp', 'code'))
- squared_contract: float32 [4096, 1024], P(('dp', 'code'))
- squared_gains: float32 [5, 1024], P(None, ('dp', 'code'))
- squared_tables: float32 [2, 1024, 1024], P(None, 'code')
The draws below stay inside these ranges and needn't reach their ends.
Inputs may be any that keep to these rules, and one draw needn't show every extreme that they name: In micro-batch 1 no token whose clip has domain 3 is masked. `small_grid`: group 0 holds four small clips in micro-batch 0 and one large clip in micro-batch 1. `domains`: clip 0 of group 0 in micro-batch 1 has domain 3.
All inputs are finite; a program needn't handle non-finite values.
Results may differ from the reference program's by a relative error of at most 0.0065.
The reference program's roundings to bfloat16 on the way count: a program that leaves them out, or rounds other values in their place, can miss the bound.
Values may be sent and summed in bfloat16 or wider, within the bound.
No kernel may reach another device: no remote copies, remote signals or barrier semaphores. Data moves between devices by JAX's collectives and lax.ppermute only.
A program may use at most 320 MiB of HBM per device.

```python
import math
import jax
import jax.numpy as jnp
from jax import lax

D = 1024
HEADS = 16
HEAD = 64
FF = 4096
V = 1024
FRAMES = 4
SLOTS = 256
SMALL_TOKENS = 64
CLIPS = 4
DOMAINS = 4
MICRO = 2
STEP = 10
GROUPS = 8


def layout_draw(key):
    base = jax.random.fold_in(key, 71)
    key_grid, key_dom, key_mask = jax.random.split(base, 3)
    micro_ids = jnp.arange(MICRO)
    group_ids = jnp.arange(GROUPS)
    small = (jax.random.randint(key_grid, (MICRO, GROUPS), 0, 3) == 0).astype(jnp.int32)
    small = jnp.where((micro_ids[:, None] == 0) & (group_ids[None, :] == 0), 1, small)
    small = jnp.where((micro_ids[:, None] == MICRO - 1) & (group_ids[None, :] == 0), 0, small)
    doms = jax.random.randint(key_dom, (MICRO, GROUPS, CLIPS), 0, DOMAINS)
    first_clip = (micro_ids[:, None, None] == MICRO - 1) & (group_ids[None, :, None] == 0) & (jnp.arange(CLIPS)[None, None, :] == 0)
    doms = jnp.where(first_clip, DOMAINS - 1, doms).astype(jnp.int32)
    slot_ids = jnp.arange(SLOTS)
    clip_of = jnp.where(small[:, :, None] > 0, slot_ids[None, None, :] // SMALL_TOKENS, 0).astype(jnp.int32)
    dom_slot = jnp.take_along_axis(doms, clip_of, axis=2)
    blocked = (micro_ids[:, None, None] == MICRO - 1) & (dom_slot == DOMAINS - 1)
    hidden = jax.random.randint(key_mask, (MICRO, GROUPS, FRAMES, SLOTS), 0, 2)
    hidden = jnp.where(blocked[:, :, None, :], 0, hidden).astype(jnp.int32)
    return (small.astype(jnp.int32), doms, hidden)


def draw_masked(key, part):
    return layout_draw(key)[2]


def draw_small_grid(key, part):
    return layout_draw(key)[0]


def draw_domains(key, part):
    return layout_draw(key)[1]


def touch_ends(result, stream_key, least, high):
    index_at = [jax.random.randint(jax.random.fold_in(stream_key, axis), (), 0, length) for axis, length in enumerate(result.shape)]
    longest = result.shape.index(max(result.shape))
    next_to = index_at[:longest] + [(index_at[longest] + 1) % result.shape[longest]] + index_at[longest + 1:]
    return result.at[tuple(index_at)].set(least).at[tuple(next_to)].set(high)


def shard_levels(key, dims, shards, least, largest):
    level = 1.0
    for position, blocks in shards:
        draws = jax.random.uniform(jax.random.fold_in(jax.random.fold_in(key, 6), position), (blocks,), jnp.float32, least / len(shards), largest / len(shards))
        level = level * jnp.repeat(jnp.exp(draws), dims[position] // blocks).reshape((-1,) + (1,) * (len(dims) - 1 - position))
    return level


def normal_values(key, shape, spread, bound, cuts=(), held_as=jnp.bfloat16):
    drawn = spread * jax.random.normal(key, shape, jnp.float32)
    if cuts:
        drawn = drawn * shard_levels(key, shape, cuts, -0.22, 0.18)
    return jnp.clip(drawn, -bound, bound).astype(held_as)


def setup_inputs(seed: int = 0) -> dict:
    seeds = jax.random.split(jax.random.key(seed), 23)
    return {
        "tokens": touch_ends(jax.random.randint(seeds[0], (MICRO, GROUPS, FRAMES, SLOTS), 0, V), jax.random.fold_in(seeds[0], 1), 0, V - 1).astype(jnp.int32),
        "masked": draw_masked(jax.random.fold_in(seeds[22], 71), 0),
        "small_grid": draw_small_grid(jax.random.fold_in(seeds[22], 71), 0),
        "domains": draw_domains(jax.random.fold_in(seeds[22], 71), 0),
        "attend_in": normal_values(seeds[4], (2, D, 3 * D), D ** -0.5, 0.1875, ((1, 32),), jnp.float32),
        "attend_out": normal_values(seeds[5], (2, D, D), (D // 16) ** -0.5, 0.75, ((1, 32),), jnp.float32),
        "expand": normal_values(seeds[6], (D, FF), D ** -0.5, 0.1875, ((0, 32),), jnp.float32),
        "contract": normal_values(seeds[7], (FF, D), FF ** -0.5, 0.09375, ((0, 32),), jnp.float32),
        "gains": jnp.clip(1.0 + 0.18 * jax.random.normal(seeds[8], (5, D), jnp.float32), 0.1, 1.9),
        "tables": normal_values(seeds[9], (2, V, D), D ** -0.5, 0.1875, ((1, 4),), jnp.float32),
        "mean_in": normal_values(seeds[10], (2, D, 3 * D), (0.1111 * 0.005 * (8*D*D + 2*D*FF + 2*V*D + 5*D) ** -0.5), 7.152557373046875e-07, ((1, 32),), jnp.float32),
        "mean_out": normal_values(seeds[11], (2, D, D), (0.1111 * 0.005 * (8*D*D + 2*D*FF + 2*V*D + 5*D) ** -0.5), 7.152557373046875e-07, ((1, 32),), jnp.float32),
        "mean_expand": normal_values(seeds[12], (D, FF), (0.1111 * 0.005 * (8*D*D + 2*D*FF + 2*V*D + 5*D) ** -0.5), 7.152557373046875e-07, ((0, 32),), jnp.float32),
        "mean_contract": normal_values(seeds[13], (FF, D), (0.1111 * 0.005 * (8*D*D + 2*D*FF + 2*V*D + 5*D) ** -0.5), 7.152557373046875e-07, ((0, 32),), jnp.float32),
        "mean_gains": normal_values(seeds[14], (5, D), (1.111 * 0.005 * (8*D*D + 2*D*FF + 2*V*D + 5*D) ** -0.5), 7.62939453125e-06, ((1, 32),), jnp.float32),
        "mean_tables": normal_values(seeds[15], (2, V, D), (0.1111 * 0.005 * (8*D*D + 2*D*FF + 2*V*D + 5*D) ** -0.5), 7.152557373046875e-07, ((1, 4),), jnp.float32),
        "square_in": jnp.clip(jnp.exp(math.log(2.787416564925538e-13) - 1.3867695 * jax.random.uniform(seeds[16], (2, D, 3 * D), jnp.float32) ** shard_levels(seeds[16], (2, D, 3 * D), ((1, 32),), -0.2, 0.2)), 6.965231207555975e-14, 2.787416564925538e-13),
        "square_out": jnp.clip(jnp.exp(math.log(2.787416564925538e-13) - 1.3867695 * jax.random.uniform(seeds[17], (2, D, D), jnp.float32) ** shard_levels(seeds[17], (2, D, D), ((1, 32),), -0.2, 0.2)), 6.965231207555975e-14, 2.787416564925538e-13),
        "square_expand": jnp.clip(jnp.exp(math.log(2.787416564925538e-13) - 1.3867695 * jax.random.uniform(seeds[18], (D, FF), jnp.float32) ** shard_levels(seeds[18], (D, FF), ((0, 32),), -0.2, 0.2)), 6.965231207555975e-14, 2.787416564925538e-13),
        "square_contract": jnp.clip(jnp.exp(math.log(2.787416564925538e-13) - 1.3867695 * jax.random.uniform(seeds[19], (FF, D), jnp.float32) ** shard_levels(seeds[19], (FF, D), ((0, 32),), -0.2, 0.2)), 6.965231207555975e-14, 2.787416564925538e-13),
        "square_gains": jnp.clip(jnp.exp(math.log(2.7874166516617116e-11) - 1.3867695 * jax.random.uniform(seeds[20], (5, D), jnp.float32) ** shard_levels(seeds[20], (5, D), ((1, 32),), -0.2, 0.2)), 6.965231343081246e-12, 2.7874166516617116e-11),
        "square_tables": jnp.clip(jnp.exp(math.log(2.787416564925538e-13) - 1.3867695 * jax.random.uniform(seeds[21], (2, V, D), jnp.float32) ** shard_levels(seeds[21], (2, V, D), ((1, 4),), -0.2, 0.2)), 6.965231207555975e-14, 2.787416564925538e-13),
    }


EPS = 1e-05
NEG = -1e+30
BETA_ONE = 0.9
BETA_TWO = 0.95
ADAM_EPS = 1e-08
DECAY = 0.1
RATE = 0.02
RATE_SMALL = 0.2
CLIP = 0.005
HIGH = lax.Precision.HIGHEST

@jax.custom_vjp
def low(v):
    return lax.optimization_barrier(v.astype(jnp.bfloat16)).astype(jnp.float32)

@jax.custom_vjp
def low_back(v):
    return v

def low_keep(v):
    return (low(v), None)

def low_pass(kept, grad):
    return (grad,)

def back_keep(v):
    return (v, None)

def back_low(kept, grad):
    return (low(grad),)
low.defvjp(low_keep, low_pass)
low_back.defvjp(back_keep, back_low)

def norm_rows(values, gain):
    return values * lax.rsqrt(lax.optimization_barrier(jnp.mean(values * values, axis=-1, keepdims=True)) + EPS) * gain

def attend(normed, w_in, w_out, allowed, row, col):
    first, second = (normed.shape[0], normed.shape[1])
    packed = low_back(low(jnp.einsum('abd,dn->abn', normed, w_in, precision=HIGH)))
    parts = packed.reshape(first, second, 3, HEADS, HEAD)
    query, key, value = (parts[:, :, 0], parts[:, :, 1], parts[:, :, 2])
    scores = low_back(jnp.einsum(row + 'he,' + col + 'he->bhqk', query, key, precision=HIGH)) * HEAD ** (-0.5)
    scores = jnp.where(allowed, scores, NEG)
    top = lax.optimization_barrier(jnp.max(scores, axis=-1, keepdims=True))
    expd = jnp.exp(scores - top)
    probs = low(expd / lax.optimization_barrier(jnp.sum(expd, axis=-1, keepdims=True)))
    mixed = jnp.einsum('bhqk,' + col + 'he->' + row + 'he', probs, value, precision=HIGH)
    mixed = low_back(low(mixed.reshape(first, second, D)))
    return low_back(jnp.einsum('abd,dn->abn', mixed, w_out, precision=HIGH))

def group_loss(params, codes, hidden_mask, weight, small):
    w_in, w_out, w_up, w_down, gain_all, table_all = [low(p) for p in params]
    slot_ids = jnp.arange(SLOTS)
    segment = jnp.where(small > 0, slot_ids // SMALL_TOKENS, 0)
    within = segment[:, None] == segment[None, :]
    frame_ids = jnp.arange(FRAMES)
    causal = frame_ids[None, :] <= frame_ids[:, None]
    embedded = jnp.take(table_all[0], codes, axis=0)
    start = jnp.where(hidden_mask[:, :, None] > 0, gain_all[4], embedded)
    after_space = start + attend(low(norm_rows(start, gain_all[0])), w_in[0], w_out[0], within, 'bq', 'bk')
    after_time = after_space + attend(low(norm_rows(after_space, gain_all[1])), w_in[1], w_out[1], causal, 'qb', 'kb')
    pre = low_back(jnp.einsum('abd,dn->abn', low(norm_rows(after_time, gain_all[2])), w_up, precision=HIGH))
    after_ffn = after_time + low_back(jnp.einsum('abn,nd->abd', low(jax.nn.gelu(pre, approximate=True)), w_down, precision=HIGH))
    final = low(norm_rows(after_ffn, gain_all[3])).reshape(FRAMES * SLOTS, D)
    logits = low_back(jnp.dot(final, table_all[1].T, precision=HIGH))
    top = lax.optimization_barrier(jnp.max(logits, axis=1, keepdims=True))
    log_total = top[:, 0] + jnp.log(lax.optimization_barrier(jnp.sum(jnp.exp(logits - top), axis=1)))
    target = jnp.take_along_axis(logits, codes.reshape(-1, 1), axis=1)[:, 0]
    return jnp.sum(weight.reshape(-1) * (log_total - target))

def adamw(weight, grad, first, second, rate, decay):
    first_new = BETA_ONE * first + (1.0 - BETA_ONE) * grad
    second_new = BETA_TWO * second + (1.0 - BETA_TWO) * grad * grad
    unbiased_first = first_new / (1.0 - BETA_ONE ** STEP)
    unbiased_second = second_new / (1.0 - BETA_TWO ** STEP)
    updated = weight - rate * (unbiased_first / (jnp.sqrt(unbiased_second) + ADAM_EPS) + decay * weight)
    return (updated, first_new, second_new)

def reference(tokens, masked, small_grid, domains, attend_in, attend_out, expand, contract, gains, tables, mean_in, mean_out, mean_expand, mean_contract, mean_gains, mean_tables, square_in, square_out, square_expand, square_contract, square_gains, square_tables):
    slot_ids = jnp.arange(SLOTS)
    clip_of = jnp.where(small_grid[:, :, None] > 0, slot_ids[None, None, :] // SMALL_TOKENS, 0).astype(jnp.int32)
    dom_slot = jnp.take_along_axis(domains, clip_of, axis=2)
    domain_hot = (dom_slot[..., None] == jnp.arange(DOMAINS)[None, None, None, :]).astype(jnp.float32)
    mask_f = masked.astype(jnp.float32)
    counts = jnp.einsum('mgfs,mgsd->md', mask_f, domain_hot, precision=HIGH)
    scale = 1.0 / (MICRO * DOMAINS * jnp.maximum(counts, 1.0))
    token_scale = jnp.einsum('mgsd,md->mgs', domain_hot, scale, precision=HIGH)
    weight = mask_f * token_scale[:, :, None, :]

    def flat(values):
        return values.reshape((MICRO * GROUPS,) + values.shape[2:])
    params = (attend_in, attend_out, expand, contract, gains, tables)

    def total(*pieces):
        checked = jax.checkpoint(group_loss)

        def step(carry, item):
            codes, hidden_mask, token_weight, small = item
            return (carry + checked(pieces, codes, hidden_mask, token_weight, small), None)
        summed, _ = lax.scan(step, jnp.zeros((), jnp.float32), (flat(tokens), flat(mask_f), flat(weight), small_grid.reshape(-1)))
        return summed
    loss, pull = jax.vjp(total, *params)
    grads = pull(jnp.ones((), loss.dtype))
    square_sum = sum((jnp.sum(g * g) for g in grads))
    norm = jnp.sqrt(square_sum)
    factor = jnp.minimum(1.0, CLIP / (norm + 1e-06))
    firsts = (mean_in, mean_out, mean_expand, mean_contract, mean_gains, mean_tables)
    seconds = (square_in, square_out, square_expand, square_contract, square_gains, square_tables)
    rates = (RATE, RATE, RATE, RATE, RATE_SMALL, RATE)
    decays = (DECAY, DECAY, DECAY, DECAY, 0.0, DECAY)
    results = [adamw(p, factor * g, f, s, r, k) for p, g, f, s, r, k in zip(params, grads, firsts, seconds, rates, decays)]
    return (loss, norm, results[0][0], results[1][0], results[2][0], results[3][0], results[4][0], results[5][0], results[0][1], results[1][1], results[2][1], results[3][1], results[4][1], results[5][1], results[0][2], results[1][2], results[2][2], results[3][2], results[4][2], results[5][2])
```

```python
import jax
import jax.numpy as jnp
from jax import lax
from jax.sharding import Mesh, PartitionSpec as P

D = 1024
HEADS = 16
HEAD = 64
FRAMES = 4
SLOTS = 256
SMALL_TOKENS = 64
CLIPS = 4
DOMAINS = 4
MICRO = 2
STEP = 10


EPS = 1e-05
NEG = -1e30
BETA_ONE = 0.9
BETA_TWO = 0.95
ADAM_EPS = 1e-08
DECAY = 0.1
RATE = 0.02
RATE_SMALL = 0.2
CLIP = 0.005
HIGH = lax.Precision.HIGHEST
LOW = jnp.bfloat16
WIDE = jnp.float32
ALL = ("z", "r", "m", "h")


def shifted(part, axis, shift):
    n = lax.axis_size(axis)
    return lax.ppermute(part, axis, [((i + shift) % n, i) for i in range(n)])


def gather_axis(part, axis, dim):
    n = lax.axis_size(axis)
    mine = lax.axis_index(axis)
    whole = jnp.broadcast_to(
        jnp.expand_dims(part, dim), part.shape[:dim] + (n,) + part.shape[dim:]
    )
    for shift in range(1, n):
        other = shifted(part, axis, shift)
        whole = lax.dynamic_update_index_in_dim(whole, other, (mine + shift) % n, dim)
    return whole


def scatter_axis(parts, axis, dim, sent=LOW):
    n = lax.axis_size(axis)
    mine = lax.axis_index(axis)
    total = lax.dynamic_index_in_dim(parts, mine, dim, keepdims=False).astype(WIDE)
    for shift in range(1, n):
        piece = lax.dynamic_index_in_dim(parts, (mine + shift) % n, dim, keepdims=False)
        total = total + shifted(piece.astype(sent), axis, n - shift).astype(WIDE)
    return total


def gather_rows(shard):
    low = shard.astype(LOW)
    half = low.shape[1] // 2
    first = gather_axis(low[:, :half], "z", 0)
    first = gather_axis(first, "r", 1)
    first = gather_axis(first, "m", 2)
    second = gather_axis(low[:, half:], "z", 0)
    second = gather_axis(second, "m", 1)
    second = gather_axis(second, "r", 1)
    first = gather_axis(first, "h", 3)
    second = gather_axis(second, "h", 3)
    return jnp.concatenate([first, second], axis=-1).reshape(-1, low.shape[1])


def gather_table(shard):
    low = shard.astype(LOW)
    return gather_axis(gather_axis(low, "m", 0), "h", 1).reshape(-1, low.shape[1])


def split_pair(lhs, lead, tail):
    pair = lax.axis_size("h")
    mine = lax.axis_index("h")
    seen = lhs.reshape(lhs.shape[0], lead, pair, tail)
    return [
        lax.dynamic_index_in_dim(seen, (mine + shift) % pair, 2, keepdims=False).reshape(
            lhs.shape[0], lead * tail
        )
        for shift in range(1, pair)
    ] + [lax.dynamic_index_in_dim(seen, mine, 2, keepdims=False).reshape(lhs.shape[0], lead * tail)]


def pair_product(others, own, rhs):
    pair = lax.axis_size("h")
    arrived = []
    for shift, lhs in zip(range(1, pair), others):
        term = lax.dot_general(lhs, rhs, (((0,), (0,)), ((), ())), preferred_element_type=WIDE)
        arrived.append(shifted(term.astype(LOW), "h", pair - shift))
    total = lax.dot_general(own, rhs, (((0,), (0,)), ((), ())), preferred_element_type=WIDE)
    total = total.astype(LOW).astype(WIDE)
    for term in arrived:
        total = total + term.astype(WIDE)
    return total


def scatter_product(lhs, rhs):
    zs, rs, ms, hs = (lax.axis_size(axis) for axis in ALL)
    tail = lhs.shape[1] // (zs * rs * ms * hs)
    *others, own = split_pair(lhs, zs * rs * ms, tail)
    total = pair_product(others, own, rhs).reshape(zs, rs, ms, tail, rhs.shape[1])
    half = rhs.shape[1] // 2
    first = scatter_axis(total[..., :half], "r", 1)
    first = scatter_axis(first, "m", 1)
    first = scatter_axis(first, "z", 0)
    second = scatter_axis(total[..., half:], "m", 2)
    second = scatter_axis(second, "r", 1)
    second = scatter_axis(second, "z", 0)
    return jnp.concatenate([first, second], axis=-1)


def scatter_table(others, own, rhs):
    zs, rs, ms, hs = (lax.axis_size(axis) for axis in ALL)
    total = pair_product(others, own, rhs)
    total = total.reshape(ms, rs, zs, -1, rhs.shape[1])
    total = scatter_axis(total, "m", 0)
    total = scatter_axis(total, "r", 0)
    return scatter_axis(total, "z", 0)


def norm_forward(values, gain):
    return values * lax.rsqrt(jnp.mean(values * values, axis=-1, keepdims=True) + EPS) * gain


def norm_backward(values, gain, upstream):
    factor = lax.rsqrt(jnp.mean(values * values, axis=-1, keepdims=True) + EPS)
    scaled = upstream * gain
    inward = factor * scaled - values * factor**3 * jnp.mean(
        scaled * values, axis=-1, keepdims=True
    )
    gain_grad = jnp.sum((upstream * values * factor).reshape(-1, values.shape[-1]), axis=0)
    return (inward, gain_grad)


def project(left, right):
    return jnp.dot(left, right, preferred_element_type=WIDE)


def project_back(left, right):
    return lax.dot_general(left, right, (((1,), (1,)), ((), ())), preferred_element_type=WIDE)


def split_heads(packed, first, second):
    parts = packed.reshape(first, second, 3, HEADS, HEAD)
    return (parts[:, :, 0], parts[:, :, 1], parts[:, :, 2])


def masked_scores(query, key, allowed, row, col):
    scores = jnp.einsum(
        row + "he," + col + "he->bhqk", query, key, preferred_element_type=WIDE
    ) * HEAD ** (-0.5)
    return jnp.where(allowed, scores, NEG)


def attend_forward(normed, shape, w_in, w_out, allowed, row, col):
    packed = project(normed, w_in).astype(LOW)
    query, key, value = split_heads(packed, *shape)
    scores = masked_scores(query, key, allowed, row, col)
    top = jnp.max(scores, axis=-1, keepdims=True)
    expd = jnp.exp(scores - top)
    summed = jnp.sum(expd, axis=-1, keepdims=True)
    probs = (expd / summed).astype(LOW)
    mixed = jnp.einsum(
        "bhqk," + col + "he->" + row + "he", probs, value, preferred_element_type=WIDE
    )
    mixed = mixed.reshape(-1, D).astype(LOW)
    return (project(mixed, w_out), (packed, mixed, top + jnp.log(summed)))


def attend_backward(normed, shape, w_in, w_out, allowed, row, col, kept, upstream):
    packed, mixed, log_total = kept
    up_low = upstream.astype(LOW)
    grad_out = scatter_product(mixed, up_low)
    grad_mixed = project_back(up_low, w_out)
    grad_mixed = grad_mixed.astype(LOW).reshape(shape + (HEADS, HEAD))
    query, key, value = split_heads(packed, *shape)
    probs = jnp.exp(masked_scores(query, key, allowed, row, col) - log_total)
    grad_value = jnp.einsum(
        "bhqk," + row + "he->" + col + "he",
        probs.astype(LOW),
        grad_mixed,
        preferred_element_type=WIDE,
    )
    grad_probs = jnp.einsum(
        row + "he," + col + "he->bhqk", grad_mixed, value, preferred_element_type=WIDE
    )
    grad_scores = (
        probs * (grad_probs - jnp.sum(probs * grad_probs, axis=-1, keepdims=True)) * HEAD ** (-0.5)
    )
    grad_scores = grad_scores.astype(LOW)
    grad_query = jnp.einsum(
        "bhqk," + col + "he->" + row + "he", grad_scores, key, preferred_element_type=WIDE
    )
    grad_key = jnp.einsum(
        "bhqk," + row + "he->" + col + "he", grad_scores, query, preferred_element_type=WIDE
    )
    grad_packed = jnp.concatenate(
        [piece.reshape(-1, D) for piece in (grad_query, grad_key, grad_value)], axis=-1
    ).astype(LOW)
    grad_normed = project_back(grad_packed, w_in)
    grad_in = scatter_product(normed, grad_packed)
    return (grad_normed, grad_in, grad_out)


def adamw(weight, grad, first, second, rate, decay):
    first_new = BETA_ONE * first + (1.0 - BETA_ONE) * grad
    second_new = BETA_TWO * second + (1.0 - BETA_TWO) * grad * grad
    unbiased_first = first_new / (1.0 - BETA_ONE**STEP)
    unbiased_second = second_new / (1.0 - BETA_TWO**STEP)
    updated = weight - rate * (
        unbiased_first / (jnp.sqrt(unbiased_second) + ADAM_EPS) + decay * weight
    )
    return (updated, first_new, second_new)


def swap_frames(values):
    hs = lax.axis_size("h")
    frames = values.shape[0]
    seen = values.reshape(frames, hs, SLOTS // hs, D)
    mine = lax.axis_index("h")
    whole = jnp.broadcast_to(
        lax.dynamic_index_in_dim(seen, mine, 1, keepdims=False)[None],
        (hs, frames, SLOTS // hs, D),
    )
    for shift in range(1, hs):
        piece = lax.dynamic_index_in_dim(seen, (mine + shift) % hs, 1, keepdims=False)
        other = shifted(piece, "h", hs - shift)
        whole = lax.dynamic_update_index_in_dim(whole, other, (mine + hs - shift) % hs, 0)
    return whole.reshape(hs * frames, SLOTS // hs, D)


def swap_slots(values):
    hs = lax.axis_size("h")
    frames = values.shape[0] // hs
    seen = values.reshape(hs, frames, SLOTS // hs, D)
    mine = lax.axis_index("h")
    own = lax.dynamic_index_in_dim(seen, mine, 0, keepdims=False)
    whole = jnp.broadcast_to(own[:, None], (frames, hs, SLOTS // hs, D))
    for shift in range(1, hs):
        piece = lax.dynamic_index_in_dim(seen, (mine + shift) % hs, 0, keepdims=False)
        other = shifted(piece, "h", hs - shift)
        whole = lax.dynamic_update_index_in_dim(whole, other, (mine + hs - shift) % hs, 1)
    return whole.reshape(frames, SLOTS, D)


def on_device(
    tokens,
    masked,
    small_grid,
    domains,
    attend_in,
    attend_out,
    expand,
    contract,
    gains,
    tables,
    mean_in,
    mean_out,
    mean_expand,
    mean_contract,
    mean_gains,
    mean_tables,
    square_in,
    square_out,
    square_expand,
    square_contract,
    square_gains,
    square_tables,
):
    zs, rs, ms, hs = (lax.axis_size(axis) for axis in ALL)
    micro = lax.axis_index("m")
    half = lax.axis_index("h")

    def of_micro(array):
        return lax.dynamic_index_in_dim(array[:, 0], micro, 0, keepdims=False)

    codes = of_micro(tokens)
    hidden_mask = of_micro(masked).astype(WIDE)
    small = of_micro(small_grid)
    doms = of_micro(domains)

    table_in = gather_table(tables[0])
    gain_low = gains.astype(LOW)
    gain_all = gather_axis(
        gather_axis(gather_axis(gather_axis(gain_low, "z", 0), "r", 1), "m", 2), "h", 3
    )
    gain_all = jnp.moveaxis(gain_all, 4, 0).reshape(gains.shape[0], D).astype(WIDE)
    w_in = [gather_rows(attend_in[0]), None]
    w_out = [gather_rows(attend_out[0]), None]
    w_in[1] = gather_rows(attend_in[1])
    w_out[1] = gather_rows(attend_out[1])
    w_up = gather_rows(expand)
    w_down = gather_rows(contract)
    table_out = gather_table(tables[1])

    slot_ids = jnp.arange(SLOTS)
    frame_ids = jnp.arange(FRAMES)
    causal = frame_ids[None, :] <= frame_ids[:, None]
    segment = jnp.where(small > 0, slot_ids // SMALL_TOKENS, 0)
    within = segment[:, None] == segment[None, :]
    dom_slot = jnp.sum((segment[:, None] == jnp.arange(CLIPS)[None, :]) * doms[None, :], axis=-1)
    domain_hot = (dom_slot[:, None] == jnp.arange(DOMAINS)[None, :]).astype(WIDE)
    counts = jnp.sum(jnp.sum(hidden_mask, axis=0)[:, None] * domain_hot, axis=0)[None, :]
    counts = jnp.sum(gather_axis(counts, "z", 0), axis=0)
    counts = jnp.sum(gather_axis(counts, "r", 0), axis=0)[0]
    scale = 1.0 / (MICRO * DOMAINS * jnp.maximum(counts, 1.0))
    slot_scale = jnp.sum(domain_hot * scale[None, :], axis=1)

    frames = FRAMES // hs
    slots = SLOTS // hs
    space = (frames, SLOTS)
    time = (FRAMES, slots)
    code_ids = jnp.arange(table_in.shape[0])

    space_codes = lax.dynamic_slice_in_dim(codes, half * frames, frames, 0).reshape(-1)
    space_mask = lax.dynamic_slice_in_dim(hidden_mask, half * frames, frames, 0).reshape(-1)
    time_codes = lax.dynamic_slice_in_dim(codes, half * slots, slots, 1).reshape(-1)
    time_weight = (
        lax.dynamic_slice_in_dim(hidden_mask, half * slots, slots, 1)
        * lax.dynamic_slice_in_dim(slot_scale, half * slots, slots, 0)[None, :]
    ).reshape(-1)

    picked = project((space_codes[:, None] == code_ids[None, :]).astype(LOW), table_in)
    start = jnp.where(space_mask[:, None] > 0, gain_all[4], picked)
    normed_space = norm_forward(start, gain_all[0]).astype(LOW)
    branch_space, kept_space = attend_forward(
        normed_space, space, w_in[0], w_out[0], within, "bq", "bk"
    )
    after_space = swap_frames((start + branch_space).reshape(space + (D,))).reshape(-1, D)
    normed_time = norm_forward(after_space, gain_all[1]).astype(LOW)
    branch_time, kept_time = attend_forward(
        normed_time, time, w_in[1], w_out[1], causal, "qb", "kb"
    )
    after_time = after_space + branch_time
    normed_ffn = norm_forward(after_time, gain_all[2]).astype(LOW)
    pre = project(normed_ffn, w_up)
    activ = jax.nn.gelu(pre, approximate=True).astype(LOW)
    after_ffn = after_time + project(activ, w_down)
    final = norm_forward(after_ffn, gain_all[3]).astype(LOW)
    logits = project_back(final, table_out)
    hits = time_codes[:, None] == code_ids[None, :]
    top = jnp.max(logits, axis=1, keepdims=True)
    log_total = top + jnp.log(jnp.sum(jnp.exp(logits - top), axis=1, keepdims=True))
    target = jnp.sum(jnp.where(hits, logits, 0.0), axis=1)
    loss_part = jnp.sum(time_weight * (log_total[:, 0] - target))
    grad_logits = (time_weight[:, None] * (jnp.exp(logits - log_total) - hits)).astype(LOW)

    *others, own = split_pair(grad_logits, ms, tables.shape[1])
    head_grad = scatter_table(others, own, final)
    grad_final = project(grad_logits, table_out)
    grad_ffn, gain_three = norm_backward(after_ffn, gain_all[3], grad_final)
    up_low = grad_ffn.astype(LOW)
    grad_down = scatter_product(activ, up_low)
    grad_activ = project_back(up_low, w_down)
    grad_pre = jax.vjp(lambda inner: jax.nn.gelu(inner, approximate=True), pre)[1](grad_activ)[
        0
    ].astype(LOW)
    grad_up = scatter_product(normed_ffn, grad_pre)
    inward, gain_two = norm_backward(after_time, gain_all[2], project_back(grad_pre, w_up))
    grad_time = grad_ffn + inward
    grad_normed, grad_in_time, grad_out_time = attend_backward(
        normed_time, time, w_in[1], w_out[1], causal, "qb", "kb", kept_time, grad_time
    )
    inward, gain_one = norm_backward(after_space, gain_all[1], grad_normed)
    grad_space = swap_slots((grad_time + inward).reshape(time + (D,))).reshape(-1, D)
    grad_normed, grad_in_space, grad_out_space = attend_backward(
        normed_space, space, w_in[0], w_out[0], within, "bq", "bk", kept_space, grad_space
    )
    inward, gain_zero = norm_backward(start, gain_all[0], grad_normed)
    grad_start = grad_space + inward
    mask_grad = jnp.sum(grad_start * space_mask[:, None], axis=0)
    seen_codes = jnp.where(space_mask > 0, -1, space_codes)
    rows = tables.shape[1]
    chosen = []
    for shift in list(range(1, hs)) + [0]:
        ids = (jnp.arange(ms)[:, None] * hs + (half + shift) % hs) * rows + jnp.arange(rows)[None, :]
        chosen.append((seen_codes[:, None] == ids.reshape(1, -1)).astype(LOW))
    embed_grad = scatter_table(chosen[:-1], chosen[-1], grad_start.astype(LOW))

    gain_grads = jnp.stack([gain_zero, gain_one, gain_two, gain_three, mask_grad])
    gain_grads = jnp.moveaxis(gain_grads.reshape(-1, zs, rs, ms, hs, gains.shape[1]), 0, 4)
    gain_grads = scatter_axis(gain_grads, "h", 3, WIDE)
    gain_grads = scatter_axis(gain_grads, "r", 1, WIDE)
    gain_grads = scatter_axis(gain_grads, "m", 1, WIDE)
    gain_grads = scatter_axis(gain_grads, "z", 0, WIDE)

    layer_grads = (
        jnp.stack([grad_in_space, grad_in_time]),
        jnp.stack([grad_out_space, grad_out_time]),
        grad_up,
        grad_down,
        gain_grads,
    )
    owned = sum((jnp.sum(g * g) for g in layer_grads + (embed_grad, head_grad)))
    sums = lax.all_gather(jnp.stack([owned, loss_part]).reshape(1, 2), ALL, axis=0, tiled=True)
    square_sum, loss = jnp.sum(sums, axis=0)
    norm = jnp.sqrt(square_sum)
    factor = jnp.minimum(1.0, CLIP / (norm + 1e-06))

    def spread(grad):
        grad = gather_axis(gather_axis(grad.astype(LOW), "z", 0), "r", 0)
        return grad.reshape(rows, D).astype(WIDE)

    table_grad = jnp.stack([spread(embed_grad), spread(head_grad)])
    params = (attend_in, attend_out, expand, contract, gains, tables)
    grads = layer_grads + (table_grad,)
    firsts = (mean_in, mean_out, mean_expand, mean_contract, mean_gains, mean_tables)
    seconds = (square_in, square_out, square_expand, square_contract, square_gains, square_tables)
    rates = (RATE, RATE, RATE, RATE, RATE_SMALL, RATE)
    decays = (DECAY, DECAY, DECAY, DECAY, 0.0, DECAY)
    results = [
        adamw(p, factor * g, f, s, r, k)
        for p, g, f, s, r, k in zip(params, grads, firsts, seconds, rates, decays)
    ]
    return (loss, norm) + tuple(result[k] for k in range(3) for result in results)


def solution(mesh):
    dp, code = mesh.shape["dp"], mesh.shape["code"]
    deep = next(n for n in (4, 2, 1) if dp % n == 0)
    fine = Mesh(mesh.devices.reshape(deep, dp // deep, MICRO, code // MICRO), ALL)
    group = ("z", "r")
    weights = (
        P(None, ALL, None),
        P(None, ALL, None),
        P(ALL, None),
        P(ALL, None),
        P(None, ALL),
        P(None, ("m", "h"), None),
    )
    return jax.shard_map(
        on_device,
        mesh=fine,
        in_specs=(
            P(None, group, None, None),
            P(None, group, None, None),
            P(None, group),
            P(None, group, None),
        )
        + weights * 3,
        out_specs=(P(), P()) + weights * 3,
        check_vma=False,
    )
```

```python
import functools

import jax
import jax.numpy as jnp
from jax import lax
from jax.experimental import pallas as pl
from jax.experimental.pallas import tpu as pltpu
from jax.sharding import Mesh, PartitionSpec as P

D = 1024
HEADS = 16
HEAD = 64
FRAMES = 4
SLOTS = 256
SMALL_TOKENS = 64
CLIPS = 4
DOMAINS = 4
MICRO = 2
STEP = 10


EPS = 1e-05
NEG = -1e30
BETA_ONE = 0.9
BETA_TWO = 0.95
ADAM_EPS = 1e-08
DECAY = 0.1
RATE = 0.02
RATE_SMALL = 0.2
CLIP = 0.005
LOW = jnp.bfloat16
WIDE = jnp.float32
ALL = ("z", "r", "m", "h")
GROUP = 256
LANES = 128


def shifted(part, axis, shift):
    n = lax.axis_size(axis)
    return lax.ppermute(part, axis, [((i + shift) % n, i) for i in range(n)])


def at(array, index, dim):
    return lax.dynamic_index_in_dim(array, index, dim, keepdims=False)


def sent_around(part, axis):
    return [shifted(part, axis, shift) for shift in range(1, lax.axis_size(axis))]


def placed(part, others, axis, dim):
    n = lax.axis_size(axis)
    mine = lax.axis_index(axis)
    whole = jnp.broadcast_to(
        jnp.expand_dims(part, dim), part.shape[:dim] + (n,) + part.shape[dim:]
    )
    for shift, other in zip(range(1, n), others):
        whole = lax.dynamic_update_index_in_dim(whole, other, (mine + shift) % n, dim)
    return whole


def gather_axis(part, axis, dim):
    return placed(part, sent_around(part, axis), axis, dim)


def halves(array, dim):
    size = array.shape[dim] // lax.axis_size("h")
    half = lax.axis_index("h")
    return [
        lax.dynamic_slice_in_dim(array, start * size, size, dim) for start in (half, 1 - half)
    ]


class Job:
    def __init__(self, steps):
        self.steps = steps
        self.result = None
        self.flight = next(steps)

    def resume(self, arrived):
        try:
            self.flight = self.steps.send(arrived)
        except StopIteration as stop:
            self.flight, self.result = None, stop.value

    def finish(self):
        while self.flight is not None:
            self.resume(self.flight)
        return self.result


def advance(value, *jobs):
    jobs = [job for job in jobs if job.flight is not None]
    value, flights = lax.optimization_barrier((value, [job.flight for job in jobs]))
    for job, flight in zip(jobs, flights):
        job.resume(flight)
    return value


def gather_half(part):
    others = yield sent_around(part, "z")
    first, second = jnp.split(placed(part, others, "z", 0), 2, axis=-1)
    one = sent_around(first, "m")
    two = sent_around(second, "r")
    one, two = yield (one, two)
    first, second = placed(first, one, "m", 1), placed(second, two, "r", 1)
    one = sent_around(first, "r")
    two = sent_around(second, "m")
    one, two = yield (one, two)
    first, second = placed(first, one, "r", 1), placed(second, two, "m", 2)
    own = jnp.concatenate([first, second], axis=-1)
    own = own.reshape(-1, own.shape[-1])
    (other,) = yield [shifted(own, "h", 1)]
    return (own, other)


def by_owner(array, block):
    seen = array.reshape(array.shape[0], -1, 2, block)
    half = lax.axis_index("h")
    return [at(seen, which, 2).reshape(array.shape[0], -1) for which in (half, 1 - half)]


def gather_columns(part, block):
    mine, other = by_owner(part, block)
    (other,) = yield [shifted(other, "h", 1)]
    pair = placed(mine, [other], "h", 0)
    result = yield from gather_half(pair.reshape(-1, mine.shape[1]))
    return result


def reduce_rows(other, own, names, order):
    (arrived,) = yield [shifted(other, "h", 1)]
    total = (own() + arrived.astype(WIDE)).astype(LOW)
    names = list(names)
    total = total.reshape(
        tuple(lax.axis_size(name) for name in names) + (-1, total.shape[-1])
    )
    for axis in order:
        dim = names.index(axis)
        n = lax.axis_size(axis)
        mine = lax.axis_index(axis)
        pieces = [
            shifted(at(total, (mine + shift) % n, dim), axis, n - shift) for shift in range(1, n)
        ]
        pieces = yield pieces
        total = at(total, mine, dim).astype(WIDE)
        for piece in pieces:
            total = total + piece.astype(WIDE)
        names.pop(dim)
        if names:
            total = total.astype(LOW)
            if names == ["h"]:
                total = total.astype(WIDE)
    return total


def swap_rows(total):
    seen = total.reshape(2, -1, total.shape[-1])
    half = lax.axis_index("h")
    (other,) = yield [shifted(at(seen, 1 - half, 0), "h", 1)]
    return (at(seen, half, 0), other)


def reduce_layer(other, own, order, block=None):
    total = yield from reduce_rows(other, own, ("z", "r", "m"), order)
    total = total.reshape(-1, total.shape[-1])
    square = jnp.sum(total * total)
    mine, other = yield from swap_rows(total)
    rows = mine.shape[0]
    if block is None:
        return (placed(mine, [other], "h", 1).reshape(rows, -1), square)
    mine, other = (half.reshape(rows, -1, block) for half in (mine, other))
    return (placed(mine, [other], "h", 2).reshape(rows, -1), square)


def reduce_owned(other, own, order):
    total = yield from reduce_rows(other, own, ("z", "r", "m"), order)
    return (total.reshape(-1, total.shape[-1]), jnp.sum(total * total))


def reduce_table(other, own):
    total = yield from reduce_rows(other, own, ("m", "h", "r", "z"), ("m", "r", "z"))
    square = jnp.sum(total * total)
    total = total.astype(LOW)
    others = yield sent_around(total, "z")
    total = placed(total, others, "z", 1)
    others = yield sent_around(total, "r")
    total = placed(total, others, "r", 1)
    mine, other = yield from swap_rows(total.reshape(-1, total.shape[-1]))
    return (placed(mine, [other], "h", 1).reshape(mine.shape[0], -1).astype(WIDE), square)


def summed_over(part, axes):
    for axis in axes:
        shift = lax.axis_size(axis) // 2
        while shift:
            part = part + shifted(part, axis, shift)
            shift //= 2
    return part


def norm_forward(values, gain):
    return values * lax.rsqrt(jnp.mean(values * values, axis=-1, keepdims=True) + EPS) * gain


def norm_backward(values, gain, upstream):
    factor = lax.rsqrt(jnp.mean(values * values, axis=-1, keepdims=True) + EPS)
    scaled = upstream * gain
    inward = factor * scaled - values * factor**3 * jnp.mean(
        scaled * values, axis=-1, keepdims=True
    )
    gain_grad = jnp.sum(upstream * values * factor, axis=0)
    return (inward, gain_grad)


def dot_nt(left, right):
    return lax.dot_general(left, right, (((1,), (1,)), ((), ())), preferred_element_type=WIDE)


def dot_tn(left, right):
    return lax.dot_general(left, right, (((0,), (0,)), ((), ())), preferred_element_type=WIDE)


def dot_nn(left, right):
    return jnp.dot(left, right, preferred_element_type=WIDE)


def allowed_pairs(kind, scalar, count):
    row = lax.broadcasted_iota(jnp.int32, (count, count), 0)
    col = lax.broadcasted_iota(jnp.int32, (count, count), 1)
    if kind == "space":
        return (scalar == 0) | (row // SMALL_TOKENS == col // SMALL_TOKENS)
    lanes = count // FRAMES
    own = FRAMES // 2
    row_frame, col_frame = row // lanes, col // lanes
    row_at = row_frame + jnp.where(scalar == 0, 0, jnp.where(row_frame < own, own, -own))
    col_at = col_frame + jnp.where(scalar == 0, 0, jnp.where(col_frame < own, own, -own))
    return (row % lanes == col % lanes) & (col_at <= row_at)


def softmax_rows(query, key, allowed):
    scores = jnp.where(allowed, dot_nt(query, key) * HEAD ** (-0.5), NEG)
    expd = jnp.exp(scores - jnp.max(scores, axis=-1, keepdims=True))
    return expd / jnp.sum(expd, axis=-1, keepdims=True)


def block_of(ref, start, kind):
    if kind == "space":
        return ref[:, pl.ds(start, LANES)]
    part = ref[:, :, pl.ds(start, LANES)]
    return part.reshape(-1, LANES)


def store_to(ref, start, kind, value):
    if kind == "space":
        ref[:, pl.ds(start, LANES)] = value
    else:
        ref[:, :, pl.ds(start, LANES)] = value.reshape(FRAMES, -1, LANES)


def forward_body(kind, scalar_ref, packed_ref, mixed_ref):
    allowed = allowed_pairs(kind, scalar_ref[0], GROUP)
    first = lax.broadcasted_iota(jnp.int32, (GROUP, LANES), 1) < HEAD

    def turn(pair, _):
        start = pl.multiple_of(pair * LANES, LANES)
        query = block_of(packed_ref, start, kind)
        key = block_of(packed_ref, pl.multiple_of(D + start, LANES), kind)
        value = block_of(packed_ref, pl.multiple_of(2 * D + start, LANES), kind)
        zero = jnp.zeros_like(query)
        one = dot_nn(softmax_rows(jnp.where(first, query, zero), key, allowed).astype(LOW), value)
        two = dot_nn(softmax_rows(jnp.where(first, zero, query), key, allowed).astype(LOW), value)
        store_to(mixed_ref, start, kind, jnp.where(first, one, two).astype(LOW))
        return 0

    lax.fori_loop(0, D // LANES, turn, 0, unroll=4)


def backward_body(kind, scalar_ref, packed_ref, up_ref, out_ref):
    allowed = allowed_pairs(kind, scalar_ref[0], GROUP)
    first = lax.broadcasted_iota(jnp.int32, (GROUP, LANES), 1) < HEAD

    def turn(pair, _):
        start = pl.multiple_of(pair * LANES, LANES)
        key_at = pl.multiple_of(D + start, LANES)
        value_at = pl.multiple_of(2 * D + start, LANES)
        query = block_of(packed_ref, start, kind)
        key = block_of(packed_ref, key_at, kind)
        value = block_of(packed_ref, value_at, kind)
        up = block_of(up_ref, start, kind)
        zero = jnp.zeros_like(query)
        grads = []
        for mine in (first, ~first):
            probs = softmax_rows(jnp.where(mine, query, zero), key, allowed)
            inner = dot_nt(jnp.where(mine, up, zero), value)
            total = jnp.sum(probs * inner, axis=-1, keepdims=True)
            scores = (probs * (inner - total) * HEAD ** (-0.5)).astype(LOW)
            grads.append((dot_nn(scores, key), dot_tn(scores, query), dot_tn(probs.astype(LOW), up)))
        for place, one, two in zip((start, key_at, value_at), *grads):
            store_to(out_ref, place, kind, jnp.where(first, one, two).astype(LOW))
        return 0

    lax.fori_loop(0, D // LANES, turn, 0, unroll=2)


def attention(kind, scalar, packed, up=None):
    shape = packed.shape[:-1]
    if kind == "space":
        grid, block, where = (shape[0] // GROUP,), (GROUP,), lambda g, s: (g, 0)
    else:
        grid, block, where = (FRAMES * shape[1] // GROUP,), (FRAMES, GROUP // FRAMES), lambda g, s: (0, g, 0)
    wide = pl.BlockSpec(block + (3 * D,), where)
    narrow = pl.BlockSpec(block + (D,), where)
    body, last, ins = forward_body, D, (packed,)
    if up is not None:
        body, last, ins = backward_body, 3 * D, (packed, up.reshape(shape + (D,)))
    return pl.pallas_call(
        functools.partial(body, kind),
        out_shape=jax.ShapeDtypeStruct(shape + (last,), LOW),
        grid_spec=pltpu.PrefetchScalarGridSpec(
            num_scalar_prefetch=1,
            grid=grid,
            in_specs=[wide, narrow][: len(ins)],
            out_specs=narrow if up is None else wide,
        ),
    )(scalar.reshape(1).astype(jnp.int32), *ins)


def adamw(weight, grad, first, second, rate, decay):
    first_new = BETA_ONE * first + (1.0 - BETA_ONE) * grad
    second_new = BETA_TWO * second + (1.0 - BETA_TWO) * grad * grad
    unbiased_first = first_new / (1.0 - BETA_ONE**STEP)
    unbiased_second = second_new / (1.0 - BETA_TWO**STEP)
    updated = weight - rate * (
        unbiased_first / (jnp.sqrt(unbiased_second) + ADAM_EPS) + decay * weight
    )
    return (updated, first_new, second_new)


def gelu(values):
    return jax.nn.gelu(values, approximate=True)


def gelu_backward(values, upstream):
    return jax.vjp(gelu, values)[1](upstream)[0]


def swap_slots(values):
    mine, other = halves(values, 1)
    return jnp.concatenate([mine, shifted(other, "h", 1)], axis=0)


def swap_frames(values):
    half = lax.axis_index("h")
    mine, other = jnp.split(values, 2, axis=0)
    other = shifted(other, "h", 1)
    return jnp.where(
        half == 0,
        jnp.concatenate([mine, other], axis=1),
        jnp.concatenate([other, mine], axis=1),
    )


def on_device(
    tokens,
    masked,
    small_grid,
    domains,
    attend_in,
    attend_out,
    expand,
    contract,
    gains,
    tables,
    mean_in,
    mean_out,
    mean_expand,
    mean_contract,
    mean_gains,
    mean_tables,
    square_in,
    square_out,
    square_expand,
    square_contract,
    square_gains,
    square_tables,
):
    micro = lax.axis_index("m")
    half = lax.axis_index("h")
    frames = FRAMES // lax.axis_size("h")
    block = contract.shape[0]
    kinds = gains.shape[0]

    def of_micro(array):
        return at(array[:, 0], micro, 0)

    codes = of_micro(tokens)
    hidden_mask = of_micro(masked).astype(WIDE)
    small = of_micro(small_grid)
    doms = of_micro(domains)

    turned = jnp.pad(gains.T, ((0, 0), (0, LANES - kinds)))
    layer_one = jnp.concatenate([attend_in[0], attend_out[0], turned], axis=1).astype(LOW)
    layer_two = jnp.concatenate([attend_in[1], attend_out[1]], axis=1).astype(LOW)
    layer_one = lax.all_gather(layer_one, ALL, axis=0, tiled=True)
    layer_two = lax.all_gather(layer_two, ALL, axis=0, tiled=True)
    low_in, low_out = tables.astype(LOW)
    table_in = gather_axis(gather_axis(low_in, "m", 0), "h", 1).reshape(-1, D)
    up_job = Job(gather_columns(expand.astype(LOW), block))
    down_job = Job(gather_half(contract.astype(LOW)))
    table_out = gather_axis(gather_axis(low_out, "m", 0), "h", 1).reshape(-1, D)

    w_in = (layer_one[:, : 3 * D], layer_two[:, : 3 * D])
    w_out = (layer_one[:, 3 * D : 4 * D], layer_two[:, 3 * D :])
    gain_all = layer_one[:, 4 * D :].T[:kinds].astype(WIDE)

    slot_ids = jnp.arange(SLOTS)
    segment = jnp.where(small > 0, slot_ids // SMALL_TOKENS, 0)
    dom_slot = jnp.sum((segment[:, None] == jnp.arange(CLIPS)[None, :]) * doms[None, :], axis=-1)
    domain_hot = (dom_slot[:, None] == jnp.arange(DOMAINS)[None, :]).astype(WIDE)
    counts = jnp.sum(jnp.sum(hidden_mask, axis=0)[:, None] * domain_hot, axis=0)[None, :]
    counts = summed_over(counts, ("r", "z"))[0]
    scale = 1.0 / (MICRO * DOMAINS * jnp.maximum(counts, 1.0))
    slot_scale = jnp.sum(domain_hot * scale[None, :], axis=1)
    code_ids = jnp.arange(table_in.shape[0])

    def own_frames(array):
        return lax.dynamic_slice_in_dim(array, half * frames, frames, 0)

    def time_order(array):
        mine = halves(array, 1)[0]
        return jnp.concatenate(halves(mine, 0), axis=0).reshape(-1)

    space_codes = own_frames(codes).reshape(-1)
    space_mask = own_frames(hidden_mask).reshape(-1)
    time_codes = time_order(codes)
    time_weight = time_order(hidden_mask * slot_scale[None, :])

    picked = dot_nn((space_codes[:, None] == code_ids[None, :]).astype(LOW), table_in)
    start = jnp.where(space_mask[:, None] > 0, gain_all[4], picked)
    normed_space = norm_forward(start, gain_all[0]).astype(LOW)
    normed_space = advance(normed_space, up_job)
    normed_space = advance(normed_space, up_job, down_job)
    packed_space = dot_nn(normed_space, w_in[0]).astype(LOW)
    mixed_space = attention("space", small, packed_space)
    mixed_space = advance(mixed_space, up_job, down_job)
    after_space = start + dot_nn(mixed_space, w_out[0])
    after_space = swap_slots(after_space.reshape(frames, SLOTS, D)).reshape(-1, D)
    normed_time = norm_forward(after_space, gain_all[1]).astype(LOW)
    normed_time = advance(normed_time, up_job, down_job)
    packed_time = dot_nn(normed_time, w_in[1]).astype(LOW).reshape(FRAMES, -1, 3 * D)
    mixed_time = attention("time", half, packed_time).reshape(-1, D)
    after_time = after_space + dot_nn(mixed_time, w_out[1])
    normed_ffn = norm_forward(after_time, gain_all[2]).astype(LOW)
    ups, downs = up_job.finish(), down_job.finish()
    pres = [dot_nn(normed_ffn, up) for up in ups]
    activs = [gelu(pre).astype(LOW) for pre in pres]
    after_ffn = after_time + dot_nn(activs[0], downs[0]) + dot_nn(activs[1], downs[1])
    final = norm_forward(after_ffn, gain_all[3]).astype(LOW)
    logits = dot_nt(final, table_out)
    hits = time_codes[:, None] == code_ids[None, :]
    top = jnp.max(logits, axis=1, keepdims=True)
    log_total = top + jnp.log(jnp.sum(jnp.exp(logits - top), axis=1, keepdims=True))
    target = jnp.sum(jnp.where(hits, logits, 0.0), axis=1)
    loss_part = jnp.sum(time_weight * (log_total[:, 0] - target))
    grad_logits = (time_weight[:, None] * (jnp.exp(logits - log_total) - hits)).astype(LOW)

    def product(make, left, mine, other, *rest):
        return Job(make(dot_tn(left, other).astype(LOW), lambda: dot_tn(left, mine), *rest))

    head_job = product(reduce_table, grad_logits, *halves(final, 1))
    grad_final = dot_nn(grad_logits, table_out)
    grad_ffn, gain_three = norm_backward(after_ffn, gain_all[3], grad_final)
    up_low = grad_ffn.astype(LOW)
    contract_job = Job(
        reduce_owned(
            dot_tn(activs[1], up_low).astype(LOW),
            lambda: dot_tn(activs[0], up_low),
            ("m", "r", "z"),
        )
    )
    grad_activs = [dot_nt(up_low, down) for down in downs]
    grad_pres = [gelu_backward(pre, grad).astype(LOW) for pre, grad in zip(pres, grad_activs)]
    grad_pres = advance(grad_pres, head_job, contract_job)
    expand_job = product(
        reduce_layer, normed_ffn, grad_pres[0], grad_pres[1], ("r", "m", "z"), block
    )
    grad_normed = dot_nt(grad_pres[0], ups[0]) + dot_nt(grad_pres[1], ups[1])
    inward, gain_two = norm_backward(after_time, gain_all[2], grad_normed)
    grad_time = grad_ffn + inward
    up_low = grad_time.astype(LOW)
    up_low = advance(up_low, head_job, expand_job)
    out_job = product(reduce_layer, mixed_time, *halves(up_low, 1), ("m", "r", "z"))
    grad_mixed = dot_nt(up_low, w_out[1]).astype(LOW)
    grad_packed = attention("time", half, packed_time, grad_mixed).reshape(-1, 3 * D)
    grad_packed = advance(grad_packed, head_job, contract_job, out_job)
    in_job = product(reduce_layer, normed_time, *halves(grad_packed, 1), ("m", "r", "z"))
    grad_normed = dot_nt(grad_packed, w_in[1])
    inward, gain_one = norm_backward(after_space, gain_all[1], grad_normed)
    grad_space = swap_frames((grad_time + inward).reshape(FRAMES, -1, D)).reshape(-1, D)
    up_low = grad_space.astype(LOW)
    up_low = advance(up_low, head_job, contract_job, expand_job, out_job, in_job)
    first_out_job = product(reduce_layer, mixed_space, *halves(up_low, 1), ("r", "m", "z"))
    grad_mixed = dot_nt(up_low, w_out[0]).astype(LOW)
    grad_packed = attention("space", small, packed_space, grad_mixed)
    grad_packed = advance(
        grad_packed, head_job, contract_job, expand_job, out_job, first_out_job
    )
    first_in_job = product(reduce_layer, normed_space, *halves(grad_packed, 1), ("r", "m", "z"))
    grad_normed = dot_nt(grad_packed, w_in[0])
    inward, gain_zero = norm_backward(start, gain_all[0], grad_normed)
    grad_start = grad_space + inward
    mask_grad = jnp.sum(grad_start * space_mask[:, None], axis=0)
    chosen = (jnp.where(space_mask > 0, -1, space_codes)[:, None] == code_ids[None, :]).astype(LOW)
    start_low = grad_start.astype(LOW)
    embed_job = product(reduce_table, chosen, *halves(start_low, 1))

    gain_grads = jnp.stack([gain_zero, gain_one, gain_two, gain_three, mask_grad])
    gain_grads = summed_over(gain_grads, ("h", "r", "m", "z"))
    owner = jnp.int32(0)
    for axis in ALL:
        owner = owner * lax.axis_size(axis) + lax.axis_index(axis)
    width = gains.shape[1]
    gain_grads = lax.dynamic_slice_in_dim(gain_grads, owner * width, width, 1)

    jobs = (in_job, first_in_job, out_job, first_out_job, expand_job, contract_job)
    jobs = jobs + (embed_job, head_job)
    while any(job.flight is not None for job in jobs):
        for job in jobs:
            if job.flight is not None:
                job.resume(job.flight)
    results = [job.result for job in jobs]
    owned = sum(square for _, square in results) + jnp.sum(gain_grads * gain_grads)
    sums = summed_over(jnp.stack([owned, loss_part]).reshape(1, 2), ("h", "m", "r", "z"))
    square_sum, loss = sums[0, 0], sums[0, 1]
    norm = jnp.sqrt(square_sum)
    factor = jnp.minimum(1.0, CLIP / (norm + 1e-06))

    made = [grad for grad, _ in results]
    grads = (
        jnp.stack([made[1], made[0]]),
        jnp.stack([made[3], made[2]]),
        made[4],
        made[5],
        gain_grads,
        jnp.stack([made[6], made[7]]),
    )
    params = (attend_in, attend_out, expand, contract, gains, tables)
    firsts = (mean_in, mean_out, mean_expand, mean_contract, mean_gains, mean_tables)
    seconds = (square_in, square_out, square_expand, square_contract, square_gains, square_tables)
    rates = (RATE, RATE, RATE, RATE, RATE_SMALL, RATE)
    decays = (DECAY, DECAY, DECAY, DECAY, 0.0, DECAY)
    results = [
        adamw(p, factor * g, f, s, r, k)
        for p, g, f, s, r, k in zip(params, grads, firsts, seconds, rates, decays)
    ]
    return (loss, norm) + tuple(result[k] for k in range(3) for result in results)


def solution(mesh):
    dp, code = mesh.shape["dp"], mesh.shape["code"]
    deep = next(n for n in (4, 2, 1) if dp % n == 0)
    fine = Mesh(mesh.devices.reshape(deep, dp // deep, MICRO, code // MICRO), ALL)
    group = ("z", "r")
    weights = (
        P(None, ALL, None),
        P(None, ALL, None),
        P(ALL, None),
        P(ALL, None),
        P(None, ALL),
        P(None, ("m", "h"), None),
    )
    return jax.shard_map(
        on_device,
        mesh=fine,
        in_specs=(
            P(None, group, None, None),
            P(None, group, None, None),
            P(None, group),
            P(None, group, None),
        )
        + weights * 3,
        out_specs=(P(), P()) + weights * 3,
        check_vma=False,
    )
```

```python
import functools

import jax
import jax.numpy as jnp
from jax import lax
from jax.experimental import pallas as pl
from jax.experimental.pallas import tpu as pltpu
from jax.sharding import Mesh, PartitionSpec as P

D = 1024
HEADS = 16
HEAD = 64
FRAMES = 4
SLOTS = 256
SMALL_TOKENS = 64
CLIPS = 4
DOMAINS = 4
MICRO = 2
STEP = 10


EPS = 1e-05
NEG = -1e30
BETA_ONE = 0.9
BETA_TWO = 0.95
ADAM_EPS = 1e-08
DECAY = 0.1
RATE = 0.02
RATE_SMALL = 0.2
CLIP = 0.005
LOW = jnp.bfloat16
WIDE = jnp.float32
ALL = ("z", "r", "m", "h")
GROUP = 256
LANES = 128


def shifted(part, axis, shift):
    n = lax.axis_size(axis)
    return lax.ppermute(part, axis, [((i + shift) % n, i) for i in range(n)])


def at(array, index, dim):
    return lax.dynamic_index_in_dim(array, index, dim, keepdims=False)


def sent_around(part, axis):
    return [shifted(part, axis, shift) for shift in range(1, lax.axis_size(axis))]


def placed(part, others, axis, dim):
    n = lax.axis_size(axis)
    mine = lax.axis_index(axis)
    whole = jnp.broadcast_to(
        jnp.expand_dims(part, dim), part.shape[:dim] + (n,) + part.shape[dim:]
    )
    for shift, other in zip(range(1, n), others):
        whole = lax.dynamic_update_index_in_dim(whole, other, (mine + shift) % n, dim)
    return whole


def gather_axis(part, axis, dim):
    return placed(part, sent_around(part, axis), axis, dim)


def halves(array, dim):
    size = array.shape[dim] // lax.axis_size("h")
    half = lax.axis_index("h")
    return [
        lax.dynamic_slice_in_dim(array, start * size, size, dim) for start in (half, 1 - half)
    ]


class Job:
    def __init__(self, steps):
        self.steps = steps
        self.result = None
        self.flight = next(steps)

    def resume(self, arrived):
        try:
            self.flight = self.steps.send(arrived)
        except StopIteration as stop:
            self.flight, self.result = None, stop.value

    def finish(self):
        while self.flight is not None:
            self.resume(self.flight)
        return self.result


def advance(value, *jobs):
    jobs = [job for job in jobs if job.flight is not None]
    value, flights = lax.optimization_barrier((value, [job.flight for job in jobs]))
    for job, flight in zip(jobs, flights):
        job.resume(flight)
    return value


def gather_half(part):
    others = yield sent_around(part, "z")
    first, second = jnp.split(placed(part, others, "z", 0), 2, axis=-1)
    one = sent_around(first, "m")
    two = sent_around(second, "r")
    one, two = yield (one, two)
    first, second = placed(first, one, "m", 1), placed(second, two, "r", 1)
    one = sent_around(first, "r")
    two = sent_around(second, "m")
    one, two = yield (one, two)
    first, second = placed(first, one, "r", 1), placed(second, two, "m", 2)
    own = jnp.concatenate([first, second], axis=-1)
    own = own.reshape(-1, own.shape[-1])
    (other,) = yield [shifted(own, "h", 1)]
    return (own, other)


def by_owner(array, block):
    seen = array.reshape(array.shape[0], -1, 2, block)
    half = lax.axis_index("h")
    return [at(seen, which, 2).reshape(array.shape[0], -1) for which in (half, 1 - half)]


def gather_columns(part, block):
    mine, other = by_owner(part, block)
    (other,) = yield [shifted(other, "h", 1)]
    pair = placed(mine, [other], "h", 0)
    result = yield from gather_half(pair.reshape(-1, mine.shape[1]))
    return result


def pieces_of(total, dim, axis):
    n = lax.axis_size(axis)
    mine = lax.axis_index(axis)
    return [
        shifted(at(total, (mine + shift) % n, dim), axis, n - shift) for shift in range(1, n)
    ]


def added(total, dim, axis, pieces):
    total = at(total, lax.axis_index(axis), dim).astype(WIDE)
    for piece in pieces:
        total = total + piece.astype(WIDE)
    return total


def reduce_rows(other, own, names, order, parts=1):
    (arrived,) = yield [shifted(other, "h", 1)]
    total = (own() + arrived.astype(WIDE)).astype(LOW)
    names = list(names)
    total = total.reshape(
        tuple(lax.axis_size(name) for name in names) + (-1, total.shape[-1])
    )
    totals = jnp.split(total, parts, axis=-1)
    orders = [list(order), [order[1], order[0]] + list(order[2:])][:parts]
    left = [list(names) for _ in totals]
    for step in range(2):
        dims = [names.index(axes[step]) for names, axes in zip(left, orders)]
        steps = list(zip(totals, dims, [axes[step] for axes in orders]))
        pieces = yield [pieces_of(*each) for each in steps]
        totals = [added(*each, arrived).astype(LOW) for each, arrived in zip(steps, pieces)]
        for names, dim in zip(left, dims):
            names.pop(dim)
    total = totals[0] if parts == 1 else jnp.concatenate(totals, axis=-1)
    dim = left[0].index(order[2])
    pieces = yield pieces_of(total, dim, order[2])
    return added(total, dim, order[2], pieces)


def swap_rows(total):
    seen = total.reshape(2, -1, total.shape[-1])
    half = lax.axis_index("h")
    (other,) = yield [shifted(at(seen, 1 - half, 0), "h", 1)]
    return (at(seen, half, 0), other)


def in_order(mine, other, dim):
    first = lax.axis_index("h") == 0
    return jnp.concatenate(
        [jnp.where(first, mine, other), jnp.where(first, other, mine)], axis=dim
    )


def reduce_layer(other, own, order, block=None, parts=1):
    total = yield from reduce_rows(other, own, ("z", "r", "m"), order, parts)
    total = total.reshape(-1, total.shape[-1])
    square = jnp.sum(total * total)
    mine, other = yield from swap_rows(total)
    if block is None:
        return (in_order(mine, other, 1), square)
    rows = mine.shape[0]
    mine, other = (half.reshape(rows, -1, 1, block) for half in (mine, other))
    return (in_order(mine, other, 2).reshape(rows, -1), square)


def reduce_owned(other, own, order):
    total = yield from reduce_rows(other, own, ("z", "r", "m"), order)
    return (total.reshape(-1, total.shape[-1]), jnp.sum(total * total))


def reduce_table(other, own):
    total = yield from reduce_rows(other, own, ("m", "h", "r", "z"), ("m", "r", "z"))
    square = jnp.sum(total * total)
    total = total.astype(LOW)
    others = yield sent_around(total, "z")
    total = placed(total, others, "z", 1)
    others = yield sent_around(total, "r")
    total = placed(total, others, "r", 1)
    mine, other = yield from swap_rows(total.reshape(-1, total.shape[-1]))
    return (in_order(mine, other, 1).astype(WIDE), square)


def sum_over(part, axes):
    for axis in axes:
        n = lax.axis_size(axis)
        if n == 4:
            others = yield sent_around(part, axis)
            part = jnp.sum(placed(part, others, axis, 0), axis=0)
            continue
        shift = n // 2
        while shift:
            (other,) = yield [shifted(part, axis, shift)]
            part = part + other
            shift //= 2
    return part


def norm_forward(values, gain):
    return values * lax.rsqrt(jnp.mean(values * values, axis=-1, keepdims=True) + EPS) * gain


def norm_backward(values, gain, upstream):
    factor = lax.rsqrt(jnp.mean(values * values, axis=-1, keepdims=True) + EPS)
    scaled = upstream * gain
    inward = factor * scaled - values * factor**3 * jnp.mean(
        scaled * values, axis=-1, keepdims=True
    )
    gain_grad = jnp.sum(upstream * values * factor, axis=0)
    return (inward, gain_grad)


def dot_nt(left, right):
    return lax.dot_general(left, right, (((1,), (1,)), ((), ())), preferred_element_type=WIDE)


def dot_tn(left, right):
    return lax.dot_general(left, right, (((0,), (0,)), ((), ())), preferred_element_type=WIDE)


def dot_nn(left, right):
    return jnp.dot(left, right, preferred_element_type=WIDE)


def allowed_pairs(kind, scalar, count):
    row = lax.broadcasted_iota(jnp.int32, (count, count), 0)
    col = lax.broadcasted_iota(jnp.int32, (count, count), 1)
    if kind == "space":
        return (scalar == 0) | (row // SMALL_TOKENS == col // SMALL_TOKENS)
    lanes = count // FRAMES
    own = FRAMES // 2
    row_frame, col_frame = row // lanes, col // lanes
    row_at = row_frame + jnp.where(scalar == 0, 0, jnp.where(row_frame < own, own, -own))
    col_at = col_frame + jnp.where(scalar == 0, 0, jnp.where(col_frame < own, own, -own))
    return (row % lanes == col % lanes) & (col_at <= row_at)


def softmax_rows(query, key, allowed):
    scores = jnp.where(allowed, dot_nt(query, key) * HEAD ** (-0.5), NEG)
    expd = jnp.exp(scores - jnp.max(scores, axis=-1, keepdims=True))
    return expd / jnp.sum(expd, axis=-1, keepdims=True)


def block_of(ref, start, kind):
    if kind == "space":
        return ref[:, pl.ds(start, LANES)]
    part = ref[:, :, pl.ds(start, LANES)]
    return part.reshape(-1, LANES)


def store_to(ref, start, kind, value):
    if kind == "space":
        ref[:, pl.ds(start, LANES)] = value
    else:
        ref[:, :, pl.ds(start, LANES)] = value.reshape(FRAMES, -1, LANES)


def forward_body(kind, scalar_ref, packed_ref, mixed_ref):
    allowed = allowed_pairs(kind, scalar_ref[0], GROUP)
    first = lax.broadcasted_iota(jnp.int32, (GROUP, LANES), 1) < HEAD

    def turn(pair, _):
        start = pl.multiple_of(pair * LANES, LANES)
        query = block_of(packed_ref, start, kind)
        key = block_of(packed_ref, pl.multiple_of(D + start, LANES), kind)
        value = block_of(packed_ref, pl.multiple_of(2 * D + start, LANES), kind)
        zero = jnp.zeros_like(query)
        one = dot_nn(softmax_rows(jnp.where(first, query, zero), key, allowed).astype(LOW), value)
        two = dot_nn(softmax_rows(jnp.where(first, zero, query), key, allowed).astype(LOW), value)
        store_to(mixed_ref, start, kind, jnp.where(first, one, two).astype(LOW))
        return 0

    lax.fori_loop(0, D // LANES, turn, 0, unroll=4)


def backward_body(kind, scalar_ref, packed_ref, up_ref, out_ref):
    allowed = allowed_pairs(kind, scalar_ref[0], GROUP)
    first = lax.broadcasted_iota(jnp.int32, (GROUP, LANES), 1) < HEAD

    def turn(pair, _):
        start = pl.multiple_of(pair * LANES, LANES)
        key_at = pl.multiple_of(D + start, LANES)
        value_at = pl.multiple_of(2 * D + start, LANES)
        query = block_of(packed_ref, start, kind)
        key = block_of(packed_ref, key_at, kind)
        value = block_of(packed_ref, value_at, kind)
        up = block_of(up_ref, start, kind)
        zero = jnp.zeros_like(query)
        grads = []
        for mine in (first, ~first):
            probs = softmax_rows(jnp.where(mine, query, zero), key, allowed)
            inner = dot_nt(jnp.where(mine, up, zero), value)
            total = jnp.sum(probs * inner, axis=-1, keepdims=True)
            scores = (probs * (inner - total) * HEAD ** (-0.5)).astype(LOW)
            grads.append((dot_nn(scores, key), dot_tn(scores, query), dot_tn(probs.astype(LOW), up)))
        for place, one, two in zip((start, key_at, value_at), *grads):
            store_to(out_ref, place, kind, jnp.where(first, one, two).astype(LOW))
        return 0

    lax.fori_loop(0, D // LANES, turn, 0, unroll=2)


def attention(kind, scalar, packed, up=None):
    shape = packed.shape[:-1]
    if kind == "space":
        grid, block, where = (shape[0] // GROUP,), (GROUP,), lambda g, s: (g, 0)
    else:
        grid, block, where = (FRAMES * shape[1] // GROUP,), (FRAMES, GROUP // FRAMES), lambda g, s: (0, g, 0)
    wide = pl.BlockSpec(block + (3 * D,), where)
    narrow = pl.BlockSpec(block + (D,), where)
    body, last, ins = forward_body, D, (packed,)
    if up is not None:
        body, last, ins = backward_body, 3 * D, (packed, up.reshape(shape + (D,)))
    return pl.pallas_call(
        functools.partial(body, kind),
        out_shape=jax.ShapeDtypeStruct(shape + (last,), LOW),
        grid_spec=pltpu.PrefetchScalarGridSpec(
            num_scalar_prefetch=1,
            grid=grid,
            in_specs=[wide, narrow][: len(ins)],
            out_specs=narrow if up is None else wide,
        ),
    )(scalar.reshape(1).astype(jnp.int32), *ins)


def adamw(weight, grad, first, second, rate, decay):
    first_new = BETA_ONE * first + (1.0 - BETA_ONE) * grad
    second_new = BETA_TWO * second + (1.0 - BETA_TWO) * grad * grad
    unbiased_first = first_new / (1.0 - BETA_ONE**STEP)
    unbiased_second = second_new / (1.0 - BETA_TWO**STEP)
    updated = weight - rate * (
        unbiased_first / (jnp.sqrt(unbiased_second) + ADAM_EPS) + decay * weight
    )
    return (updated, first_new, second_new)


def gelu(values):
    return jax.nn.gelu(values, approximate=True)


def gelu_backward(values, upstream):
    return jax.vjp(gelu, values)[1](upstream)[0]


def swap_slots(values):
    mine, other = halves(values, 1)
    return jnp.concatenate([mine, shifted(other, "h", 1)], axis=0)


def swap_frames(values):
    half = lax.axis_index("h")
    mine, other = jnp.split(values, 2, axis=0)
    other = shifted(other, "h", 1)
    return jnp.where(
        half == 0,
        jnp.concatenate([mine, other], axis=1),
        jnp.concatenate([other, mine], axis=1),
    )


def on_device(
    tokens,
    masked,
    small_grid,
    domains,
    attend_in,
    attend_out,
    expand,
    contract,
    gains,
    tables,
    mean_in,
    mean_out,
    mean_expand,
    mean_contract,
    mean_gains,
    mean_tables,
    square_in,
    square_out,
    square_expand,
    square_contract,
    square_gains,
    square_tables,
):
    micro = lax.axis_index("m")
    half = lax.axis_index("h")
    frames = FRAMES // lax.axis_size("h")
    block = contract.shape[0]
    kinds = gains.shape[0]

    def of_micro(array):
        return at(array[:, 0], micro, 0)

    codes = of_micro(tokens)
    hidden_mask = of_micro(masked).astype(WIDE)
    small = of_micro(small_grid)
    doms = of_micro(domains)

    turned = jnp.pad(gains.T, ((0, 0), (0, LANES - kinds)))
    layer_one = jnp.concatenate([attend_in[0], attend_out[0], turned], axis=1).astype(LOW)
    layer_two = jnp.concatenate([attend_in[1], attend_out[1]], axis=1).astype(LOW)
    layer_one = lax.all_gather(layer_one, ALL, axis=0, tiled=True)
    layer_two = lax.all_gather(layer_two, ALL, axis=0, tiled=True)
    low_in, low_out = tables.astype(LOW)
    table_in = gather_axis(gather_axis(low_in, "m", 0), "h", 1).reshape(-1, D)
    up_job = Job(gather_columns(expand.astype(LOW), block))
    down_job = Job(gather_half(contract.astype(LOW)))
    table_in = advance(table_in, up_job)
    table_out = gather_axis(gather_axis(low_out, "m", 0), "h", 1).reshape(-1, D)

    code_ids = jnp.arange(table_in.shape[0])

    def own_frames(array):
        return lax.dynamic_slice_in_dim(array, half * frames, frames, 0)

    space_codes = own_frames(codes).reshape(-1)
    picked = dot_nn((space_codes[:, None] == code_ids[None, :]).astype(LOW), table_in)
    picked = advance(picked, up_job, down_job)
    layer_one = advance(layer_one, up_job, down_job)
    w_in = (layer_one[:, : 3 * D], layer_two[:, : 3 * D])
    w_out = (layer_one[:, 3 * D : 4 * D], layer_two[:, 3 * D :])
    gain_all = layer_one[:, 4 * D :].T[:kinds].astype(WIDE)

    slot_ids = jnp.arange(SLOTS)
    segment = jnp.where(small > 0, slot_ids // SMALL_TOKENS, 0)
    dom_slot = jnp.sum((segment[:, None] == jnp.arange(CLIPS)[None, :]) * doms[None, :], axis=-1)
    domain_hot = (dom_slot[:, None] == jnp.arange(DOMAINS)[None, :]).astype(WIDE)
    counts = jnp.sum(jnp.sum(hidden_mask, axis=0)[:, None] * domain_hot, axis=0)[None, :]
    counts = Job(sum_over(counts, ("r", "z"))).finish()[0]
    scale = 1.0 / (MICRO * DOMAINS * jnp.maximum(counts, 1.0))
    slot_scale = jnp.sum(domain_hot * scale[None, :], axis=1)

    def time_order(array):
        mine = halves(array, 1)[0]
        return jnp.concatenate(halves(mine, 0), axis=0).reshape(-1)

    space_mask = own_frames(hidden_mask).reshape(-1)
    time_codes = time_order(codes)
    time_weight = time_order(hidden_mask * slot_scale[None, :])

    start = jnp.where(space_mask[:, None] > 0, gain_all[4], picked)
    normed_space = norm_forward(start, gain_all[0]).astype(LOW)
    packed_space = dot_nn(normed_space, w_in[0]).astype(LOW)
    mixed_space = attention("space", small, packed_space)
    after_space = start + dot_nn(mixed_space, w_out[0])
    after_space = swap_slots(after_space.reshape(frames, SLOTS, D)).reshape(-1, D)
    normed_time = norm_forward(after_space, gain_all[1]).astype(LOW)
    normed_time = advance(normed_time, up_job, down_job)
    packed_time = dot_nn(normed_time, w_in[1]).astype(LOW).reshape(FRAMES, -1, 3 * D)
    mixed_time = attention("time", half, packed_time).reshape(-1, D)
    after_time = after_space + dot_nn(mixed_time, w_out[1])
    normed_ffn = norm_forward(after_time, gain_all[2]).astype(LOW)
    ups, downs = up_job.finish(), down_job.finish()
    pres = [dot_nn(normed_ffn, up) for up in ups]
    activs = [gelu(pre).astype(LOW) for pre in pres]
    after_ffn = after_time + dot_nn(activs[0], downs[0]) + dot_nn(activs[1], downs[1])
    final = norm_forward(after_ffn, gain_all[3]).astype(LOW)
    logits = dot_nt(final, table_out)
    hits = time_codes[:, None] == code_ids[None, :]
    top = jnp.max(logits, axis=1, keepdims=True)
    log_total = top + jnp.log(jnp.sum(jnp.exp(logits - top), axis=1, keepdims=True))
    target = jnp.sum(jnp.where(hits, logits, 0.0), axis=1)
    loss_part = jnp.sum(time_weight * (log_total[:, 0] - target))
    grad_logits = (time_weight[:, None] * (jnp.exp(logits - log_total) - hits)).astype(LOW)

    def product(make, left, mine, other, *rest):
        return Job(make(dot_tn(left, other).astype(LOW), lambda: dot_tn(left, mine), *rest))

    head_job = product(reduce_table, grad_logits, *halves(final, 1))
    grad_final = dot_nn(grad_logits, table_out)
    grad_ffn, gain_three = norm_backward(after_ffn, gain_all[3], grad_final)
    up_low = grad_ffn.astype(LOW)
    contract_job = Job(
        reduce_owned(
            dot_tn(activs[1], up_low).astype(LOW),
            lambda: dot_tn(activs[0], up_low),
            ("m", "r", "z"),
        )
    )
    grad_activs = [dot_nt(up_low, down) for down in downs]
    grad_pres = [gelu_backward(pre, grad).astype(LOW) for pre, grad in zip(pres, grad_activs)]
    grad_pres = advance(grad_pres, head_job, contract_job)
    expand_job = product(
        reduce_layer, normed_ffn, grad_pres[0], grad_pres[1], ("r", "m", "z"), block
    )
    grad_normed = dot_nt(grad_pres[0], ups[0]) + dot_nt(grad_pres[1], ups[1])
    inward, gain_two = norm_backward(after_time, gain_all[2], grad_normed)
    grad_time = grad_ffn + inward
    up_low = grad_time.astype(LOW)
    up_low = advance(up_low, head_job, expand_job)
    out_job = product(reduce_layer, mixed_time, *halves(up_low, 1), ("m", "r", "z"))
    grad_mixed = dot_nt(up_low, w_out[1]).astype(LOW)
    grad_packed = attention("time", half, packed_time, grad_mixed).reshape(-1, 3 * D)
    grad_packed = advance(grad_packed, head_job, contract_job, out_job)
    in_job = product(reduce_layer, normed_time, *halves(grad_packed, 1), ("m", "r", "z"))
    grad_normed = dot_nt(grad_packed, w_in[1])
    inward, gain_one = norm_backward(after_space, gain_all[1], grad_normed)
    grad_space = swap_frames((grad_time + inward).reshape(FRAMES, -1, D)).reshape(-1, D)
    up_low = grad_space.astype(LOW)
    up_low = advance(up_low, head_job, out_job, in_job)
    first_out_job = product(reduce_layer, mixed_space, *halves(up_low, 1), ("r", "m", "z"))
    grad_mixed = dot_nt(up_low, w_out[0]).astype(LOW)
    grad_packed = attention("space", small, packed_space, grad_mixed)
    grad_packed = advance(
        grad_packed, head_job, contract_job, expand_job, out_job, in_job, first_out_job
    )
    first_in_job = product(
        reduce_layer, normed_space, *halves(grad_packed, 1), ("r", "m", "z"), None, 2
    )
    grad_normed = dot_nt(grad_packed, w_in[0])
    grad_normed = advance(grad_normed, first_in_job, head_job, out_job)
    inward, gain_zero = norm_backward(start, gain_all[0], grad_normed)
    grad_start = grad_space + inward
    mask_grad = jnp.sum(grad_start * space_mask[:, None], axis=0)
    chosen = (jnp.where(space_mask > 0, -1, space_codes)[:, None] == code_ids[None, :]).astype(LOW)
    start_low = grad_start.astype(LOW)
    embed_job = product(reduce_table, chosen, *halves(start_low, 1))

    gain_grads = jnp.stack([gain_zero, gain_one, gain_two, gain_three, mask_grad])
    gain_job = Job(sum_over(gain_grads, ("h", "m", "r", "z")))
    token = jnp.zeros((), WIDE)
    late = (expand_job, contract_job, in_job, first_out_job)
    token = advance(token, embed_job, gain_job, head_job, out_job, *late)
    token = advance(token, first_in_job)
    token = advance(token, embed_job, gain_job, first_out_job)
    token = advance(token, first_in_job)
    token = advance(token, embed_job, gain_job, expand_job, in_job, first_out_job)
    token = advance(token, first_in_job, embed_job, gain_job)

    jobs = (in_job, first_in_job, out_job, first_out_job, expand_job, contract_job)
    jobs = jobs + (embed_job, head_job)
    owner = jnp.int32(0)
    for axis in ALL:
        owner = owner * lax.axis_size(axis) + lax.axis_index(axis)
    width = gains.shape[1]
    gain_grads = lax.dynamic_slice_in_dim(gain_job.finish(), owner * width, width, 1)
    results = [job.finish() for job in jobs]
    owned = sum(square for _, square in results) + jnp.sum(gain_grads * gain_grads)
    sums = jnp.stack([owned, loss_part]).reshape(1, 2)
    sums = Job(sum_over(sums, ("h", "m", "r", "z"))).finish()
    square_sum, loss = sums[0, 0], sums[0, 1]
    norm = jnp.sqrt(square_sum)
    factor = jnp.minimum(1.0, CLIP / (norm + 1e-06))

    made = [grad for grad, _ in results]
    grads = (
        jnp.stack([made[1], made[0]]),
        jnp.stack([made[3], made[2]]),
        made[4],
        made[5],
        gain_grads,
        jnp.stack([made[6], made[7]]),
    )
    params = (attend_in, attend_out, expand, contract, gains, tables)
    firsts = (mean_in, mean_out, mean_expand, mean_contract, mean_gains, mean_tables)
    seconds = (square_in, square_out, square_expand, square_contract, square_gains, square_tables)
    rates = (RATE, RATE, RATE, RATE, RATE_SMALL, RATE)
    decays = (DECAY, DECAY, DECAY, DECAY, 0.0, DECAY)
    results = [
        adamw(p, factor * g, f, s, r, k)
        for p, g, f, s, r, k in zip(params, grads, firsts, seconds, rates, decays)
    ]
    return (loss, norm) + tuple(result[k] for k in range(3) for result in results)


def solution(mesh):
    dp, code = mesh.shape["dp"], mesh.shape["code"]
    deep = next(n for n in (4, 2, 1) if dp % n == 0)
    fine = Mesh(mesh.devices.reshape(deep, dp // deep, MICRO, code // MICRO), ALL)
    group = ("z", "r")
    weights = (
        P(None, ALL, None),
        P(None, ALL, None),
        P(ALL, None),
        P(ALL, None),
        P(None, ALL),
        P(None, ("m", "h"), None),
    )
    return jax.shard_map(
        on_device,
        mesh=fine,
        in_specs=(
            P(None, group, None, None),
            P(None, group, None, None),
            P(None, group),
            P(None, group, None),
        )
        + weights * 3,
        out_specs=(P(), P()) + weights * 3,
        check_vma=False,
    )
```

```python
import functools

import jax
import jax.numpy as jnp
from jax import lax
from jax.experimental import pallas as pl
from jax.experimental.pallas import tpu as pltpu
from jax.sharding import Mesh, PartitionSpec as P

D = 1024
HEADS = 16
HEAD = 64
FRAMES = 4
SLOTS = 256
SMALL_TOKENS = 64
CLIPS = 4
DOMAINS = 4
MICRO = 2
STEP = 10


EPS = 1e-05
NEG = -1e30
BETA_ONE = 0.9
BETA_TWO = 0.95
ADAM_EPS = 1e-08
DECAY = 0.1
RATE = 0.02
RATE_SMALL = 0.2
CLIP = 0.005
LOW = jnp.bfloat16
WIDE = jnp.float32
ALL = ("z", "r", "m", "h")
GROUP = 256
LANES = 128
HALF = D // 2


def shifted(part, axis, shift):
    n = lax.axis_size(axis)
    return lax.ppermute(part, axis, [((i + shift) % n, i) for i in range(n)])


def at(array, index, dim):
    return lax.dynamic_index_in_dim(array, index, dim, keepdims=False)


def sent_around(part, axis):
    return [shifted(part, axis, shift) for shift in range(1, lax.axis_size(axis))]


def placed(part, others, axis, dim):
    n = lax.axis_size(axis)
    mine = lax.axis_index(axis)
    whole = jnp.broadcast_to(
        jnp.expand_dims(part, dim), part.shape[:dim] + (n,) + part.shape[dim:]
    )
    for shift, other in zip(range(1, n), others):
        whole = lax.dynamic_update_index_in_dim(whole, other, (mine + shift) % n, dim)
    return whole


def gather_axis(part, axis, dim):
    return placed(part, sent_around(part, axis), axis, dim)


def halves(array, dim):
    size = array.shape[dim] // lax.axis_size("h")
    half = lax.axis_index("h")
    return [
        lax.dynamic_slice_in_dim(array, start * size, size, dim) for start in (half, 1 - half)
    ]


class Job:
    def __init__(self, steps):
        self.steps = steps
        self.result = None
        self.flight = next(steps)

    def resume(self, arrived):
        try:
            self.flight = self.steps.send(arrived)
        except StopIteration as stop:
            self.flight, self.result = None, stop.value

    def finish(self):
        while self.flight is not None:
            self.resume(self.flight)
        return self.result


def advance(value, *jobs):
    jobs = [job for job in jobs if job.flight is not None]
    value, flights = lax.optimization_barrier((value, [job.flight for job in jobs]))
    for job, flight in zip(jobs, flights):
        job.resume(flight)
    return value


def split_columns(array):
    cut = array.shape[-1] // (2 * LANES) * LANES
    return array[..., :cut], array[..., cut:]


def gather_deep(part):
    if lax.axis_size("z") != 4:
        others = yield sent_around(part, "z")
        return placed(part, others, "z", 0)
    above, below = yield [shifted(part, "z", 1), shifted(part, "z", 3)]
    first, second = split_columns(above)[0], split_columns(below)[1]
    first, second = yield [shifted(first, "z", 1), shifted(second, "z", 3)]
    mine = lax.axis_index("z")
    whole = jnp.broadcast_to(part[None], (4,) + part.shape)
    whole = lax.dynamic_update_index_in_dim(whole, above, (mine + 1) % 4, 0)
    whole = lax.dynamic_update_index_in_dim(whole, below, (mine + 3) % 4, 0)
    zero = jnp.int32(0)
    place = [(mine + 2) % 4] + [zero] * part.ndim
    whole = lax.dynamic_update_slice(whole, first[None], place)
    place[-1] = jnp.int32(first.shape[-1])
    return lax.dynamic_update_slice(whole, second[None], place)


def gather_flat(part, dim):
    first, second = split_columns(part)
    one, two = yield (sent_around(first, "m"), sent_around(second, "r"))
    first, second = placed(first, one, "m", dim), placed(second, two, "r", dim)
    one, two = yield (sent_around(first, "r"), sent_around(second, "m"))
    first, second = placed(first, one, "r", dim), placed(second, two, "m", dim + 1)
    return jnp.concatenate([first, second], axis=-1)


def exchanged(own):
    own = own.reshape(-1, own.shape[-1])
    (other,) = yield [shifted(own, "h", 1)]
    return (own, other)


def gather_half(part):
    whole = yield from gather_deep(part)
    whole = yield from gather_flat(whole, 1)
    return (yield from exchanged(whole))


def gather_pair(mine, other):
    (other,) = yield [shifted(other, "h", 1)]
    pair = placed(mine, [other], "h", 0)
    return pair.reshape(-1, mine.shape[1])


def by_owner(array, block):
    seen = array.reshape(array.shape[0], -1, 2, block)
    half = lax.axis_index("h")
    return [at(seen, which, 2).reshape(array.shape[0], -1) for which in (half, 1 - half)]


def gather_columns(part, block):
    pair = yield from gather_pair(*by_owner(part, block))
    return (yield from gather_half(pair))


def gather_layer(w_in, w_out, *rest):
    parts = [by_owner(array, HALF) for array in (w_in, w_out)]
    mine, other = (jnp.concatenate(part + rest, axis=1).astype(LOW) for part in zip(*parts))
    pair = yield from gather_pair(mine, other)
    whole = yield from gather_flat(pair, 0)
    whole = yield from gather_deep(whole)
    return (yield from exchanged(whole))


def gather_table(part):
    others = yield sent_around(part, "m")
    part = placed(part, others, "m", 0)
    others = yield sent_around(part, "h")
    return placed(part, others, "h", 1).reshape(-1, part.shape[-1])


def pieces_of(total, dim, axis):
    n = lax.axis_size(axis)
    mine = lax.axis_index(axis)
    return [
        shifted(at(total, (mine + shift) % n, dim), axis, n - shift) for shift in range(1, n)
    ]


def added(total, dim, axis, pieces):
    total = at(total, lax.axis_index(axis), dim).astype(WIDE)
    for piece in pieces:
        total = total + piece.astype(WIDE)
    return total


def reduce_rows(other, own, names, order, parts=1):
    (arrived,) = yield [shifted(other, "h", 1)]
    total = (own() + arrived.astype(WIDE)).astype(LOW)
    names = list(names)
    total = total.reshape(
        tuple(lax.axis_size(name) for name in names) + (-1, total.shape[-1])
    )
    totals = jnp.split(total, parts, axis=-1)
    orders = [list(order), [order[1], order[0]] + list(order[2:])][:parts]
    left = [list(names) for _ in totals]
    for step in range(2):
        dims = [names.index(axes[step]) for names, axes in zip(left, orders)]
        steps = list(zip(totals, dims, [axes[step] for axes in orders]))
        pieces = yield [pieces_of(*each) for each in steps]
        totals = [added(*each, arrived).astype(LOW) for each, arrived in zip(steps, pieces)]
        for names, dim in zip(left, dims):
            names.pop(dim)
    total = totals[0] if parts == 1 else jnp.concatenate(totals, axis=-1)
    dim = left[0].index(order[2])
    pieces = yield pieces_of(total, dim, order[2])
    return added(total, dim, order[2], pieces)


def swap_rows(total):
    seen = total.reshape(2, -1, total.shape[-1])
    half = lax.axis_index("h")
    (other,) = yield [shifted(at(seen, 1 - half, 0), "h", 1)]
    return (at(seen, half, 0), other)


def in_order(mine, other, dim):
    first = lax.axis_index("h") == 0
    return jnp.concatenate(
        [jnp.where(first, mine, other), jnp.where(first, other, mine)], axis=dim
    )


def reduce_layer(other, own, order, block=None, parts=1):
    total = yield from reduce_rows(other, own, ("z", "r", "m"), order, parts)
    total = total.reshape(-1, total.shape[-1])
    square = jnp.sum(total * total)
    mine, other = yield from swap_rows(total)
    if block is None:
        return (in_order(mine, other, 1), square)
    rows = mine.shape[0]
    mine, other = (half.reshape(rows, -1, 1, block) for half in (mine, other))
    return (in_order(mine, other, 2).reshape(rows, -1), square)


def reduce_owned(other, own, order):
    total = yield from reduce_rows(other, own, ("z", "r", "m"), order)
    return (total.reshape(-1, total.shape[-1]), jnp.sum(total * total))


def reduce_table(other, own):
    total = yield from reduce_rows(other, own, ("m", "h", "r", "z"), ("m", "r", "z"))
    square = jnp.sum(total * total)
    total = total.astype(LOW)
    others = yield sent_around(total, "z")
    total = placed(total, others, "z", 1)
    others = yield sent_around(total, "r")
    total = placed(total, others, "r", 1)
    mine, other = yield from swap_rows(total.reshape(-1, total.shape[-1]))
    return (in_order(mine, other, 1).astype(WIDE), square)


def sum_over(part, axes):
    for axis in axes:
        n = lax.axis_size(axis)
        if n == 4:
            others = yield sent_around(part, axis)
            part = jnp.sum(placed(part, others, axis, 0), axis=0)
            continue
        shift = n // 2
        while shift:
            (other,) = yield [shifted(part, axis, shift)]
            part = part + other
            shift //= 2
    return part


def norm_forward(values, gain):
    return values * lax.rsqrt(jnp.mean(values * values, axis=-1, keepdims=True) + EPS) * gain


def norm_backward(values, gain, upstream):
    factor = lax.rsqrt(jnp.mean(values * values, axis=-1, keepdims=True) + EPS)
    scaled = upstream * gain
    inward = factor * scaled - values * factor**3 * jnp.mean(
        scaled * values, axis=-1, keepdims=True
    )
    gain_grad = jnp.sum(upstream * values * factor, axis=0)
    return (inward, gain_grad)


def dot_nt(left, right):
    return lax.dot_general(left, right, (((1,), (1,)), ((), ())), preferred_element_type=WIDE)


def dot_tn(left, right):
    return lax.dot_general(left, right, (((0,), (0,)), ((), ())), preferred_element_type=WIDE)


def dot_nn(left, right):
    return jnp.dot(left, right, preferred_element_type=WIDE)


def allowed_pairs(kind, scalar, count):
    row = lax.broadcasted_iota(jnp.int32, (count, count), 0)
    col = lax.broadcasted_iota(jnp.int32, (count, count), 1)
    if kind == "space":
        return (scalar == 0) | (row // SMALL_TOKENS == col // SMALL_TOKENS)
    lanes = count // FRAMES
    own = FRAMES // 2
    row_frame, col_frame = row // lanes, col // lanes
    row_at = row_frame + jnp.where(scalar == 0, 0, jnp.where(row_frame < own, own, -own))
    col_at = col_frame + jnp.where(scalar == 0, 0, jnp.where(col_frame < own, own, -own))
    return (row % lanes == col % lanes) & (col_at <= row_at)


def softmax_rows(query, key, allowed):
    scores = jnp.where(allowed, dot_nt(query, key) * HEAD ** (-0.5), NEG)
    expd = jnp.exp(scores - jnp.max(scores, axis=-1, keepdims=True))
    return expd / jnp.sum(expd, axis=-1, keepdims=True)


def block_of(ref, start, kind):
    if kind == "space":
        return ref[:, pl.ds(start, LANES)]
    part = ref[:, :, pl.ds(start, LANES)]
    return part.reshape(-1, LANES)


def store_to(ref, start, kind, value):
    if kind == "space":
        ref[:, pl.ds(start, LANES)] = value
    else:
        ref[:, :, pl.ds(start, LANES)] = value.reshape(FRAMES, -1, LANES)


def forward_body(kind, scalar_ref, own_ref, other_ref, mixed_ref):
    allowed = allowed_pairs(kind, scalar_ref[0], GROUP)
    first = lax.broadcasted_iota(jnp.int32, (GROUP, LANES), 1) < HEAD
    half = scalar_ref[1]

    def turn(pair, _):
        start = pl.multiple_of(pair * LANES, LANES)
        for ref, which in ((own_ref, half), (other_ref, 1 - half)):
            query, key, value = (
                block_of(ref, pl.multiple_of(part * HALF + start, LANES), kind)
                for part in range(3)
            )
            zero = jnp.zeros_like(query)
            one = softmax_rows(jnp.where(first, query, zero), key, allowed).astype(LOW)
            two = softmax_rows(jnp.where(first, zero, query), key, allowed).astype(LOW)
            mixed = jnp.where(first, dot_nn(one, value), dot_nn(two, value)).astype(LOW)
            store_to(mixed_ref, pl.multiple_of(which * HALF + start, LANES), kind, mixed)
        return 0

    lax.fori_loop(0, HALF // LANES, turn, 0, unroll=2)


def backward_body(kind, scalar_ref, own_ref, other_ref, up_ref, own_out_ref, other_out_ref):
    allowed = allowed_pairs(kind, scalar_ref[0], GROUP)
    first = lax.broadcasted_iota(jnp.int32, (GROUP, LANES), 1) < HEAD
    half = scalar_ref[1]

    def turn(pair, _):
        start = pl.multiple_of(pair * LANES, LANES)
        for ref, out_ref, which in (
            (own_ref, own_out_ref, half),
            (other_ref, other_out_ref, 1 - half),
        ):
            starts = [pl.multiple_of(part * HALF + start, LANES) for part in range(3)]
            query, key, value = (block_of(ref, place, kind) for place in starts)
            up = block_of(up_ref, pl.multiple_of(which * HALF + start, LANES), kind)
            zero = jnp.zeros_like(query)
            grads = []
            for mine in (first, ~first):
                probs = softmax_rows(jnp.where(mine, query, zero), key, allowed)
                inner = dot_nt(jnp.where(mine, up, zero), value)
                total = jnp.sum(probs * inner, axis=-1, keepdims=True)
                scores = (probs * (inner - total) * HEAD ** (-0.5)).astype(LOW)
                grads.append(
                    (dot_nn(scores, key), dot_tn(scores, query), dot_tn(probs.astype(LOW), up))
                )
            for place, one, two in zip(starts, *grads):
                store_to(out_ref, place, kind, jnp.where(first, one, two).astype(LOW))
        return 0

    lax.fori_loop(0, HALF // LANES, turn, 0)


def attention(kind, scalars, packed, up=None):
    shape = packed[0].shape[:-1]
    if kind == "space":
        grid, block, where = (shape[0] // GROUP,), (GROUP,), lambda g, s: (g, 0)
    else:
        grid, block, where = (
            (FRAMES * shape[1] // GROUP,),
            (FRAMES, GROUP // FRAMES),
            lambda g, s: (0, g, 0),
        )
    third = pl.BlockSpec(block + (3 * HALF,), where)
    whole = pl.BlockSpec(block + (D,), where)
    if up is None:
        body, ins, flops = forward_body, (*packed,), 9e9
        outs, shapes = whole, jax.ShapeDtypeStruct(shape + (D,), LOW)
    else:
        body, ins, flops = backward_body, (*packed, up.reshape(shape + (D,))), 22e9
        outs = (third, third)
        shapes = (jax.ShapeDtypeStruct(shape + (3 * HALF,), LOW),) * 2
    return pl.pallas_call(
        functools.partial(body, kind),
        out_shape=shapes,
        grid_spec=pltpu.PrefetchScalarGridSpec(
            num_scalar_prefetch=1,
            grid=grid,
            in_specs=[third, third, whole][: len(ins)],
            out_specs=outs,
        ),
        cost_estimate=pl.CostEstimate(
            flops=int(flops), transcendentals=4 * HEADS * GROUP * GROUP, bytes_accessed=8 << 20
        ),
    )(jnp.stack(scalars).astype(jnp.int32), *ins)


def adamw(weight, grad, first, second, rate, decay):
    first_new = BETA_ONE * first + (1.0 - BETA_ONE) * grad
    second_new = BETA_TWO * second + (1.0 - BETA_TWO) * grad * grad
    unbiased_first = first_new / (1.0 - BETA_ONE**STEP)
    unbiased_second = second_new / (1.0 - BETA_TWO**STEP)
    updated = weight - rate * (
        unbiased_first / (jnp.sqrt(unbiased_second) + ADAM_EPS) + decay * weight
    )
    return (updated, first_new, second_new)


def gelu(values):
    return jax.nn.gelu(values, approximate=True)


def gelu_backward(values, upstream):
    return jax.vjp(gelu, values)[1](upstream)[0]


def swap_slots(values):
    mine, other = halves(values, 1)
    return jnp.concatenate([mine, shifted(other, "h", 1)], axis=0)


def swap_frames(values):
    half = lax.axis_index("h")
    mine, other = jnp.split(values, 2, axis=0)
    other = shifted(other, "h", 1)
    return jnp.where(
        half == 0,
        jnp.concatenate([mine, other], axis=1),
        jnp.concatenate([other, mine], axis=1),
    )


def on_device(
    tokens,
    masked,
    small_grid,
    domains,
    attend_in,
    attend_out,
    expand,
    contract,
    gains,
    tables,
    mean_in,
    mean_out,
    mean_expand,
    mean_contract,
    mean_gains,
    mean_tables,
    square_in,
    square_out,
    square_expand,
    square_contract,
    square_gains,
    square_tables,
):
    micro = lax.axis_index("m")
    half = lax.axis_index("h")
    frames = FRAMES // lax.axis_size("h")
    block = contract.shape[0]
    kinds = gains.shape[0]

    def of_micro(array):
        return at(array[:, 0], micro, 0)

    codes = of_micro(tokens)
    hidden_mask = of_micro(masked).astype(WIDE)
    small = of_micro(small_grid)
    doms = of_micro(domains)

    turned = jnp.pad(gains.T, ((0, 0), (0, LANES - kinds)))
    low_in, low_out = tables.astype(LOW)
    one_job = Job(gather_layer(attend_in[0], attend_out[0], turned))
    down_job = Job(gather_half(contract.astype(LOW)))
    up_job = Job(gather_columns(expand.astype(LOW), block))
    in_table_job = Job(gather_table(low_in))
    token = advance(jnp.zeros((), WIDE), one_job, down_job, up_job)
    two_job = Job(gather_layer(attend_in[1], attend_out[1]))
    token = advance(token, one_job, down_job, up_job, two_job)
    token = advance(token, one_job, in_table_job, up_job)
    token = advance(token, one_job, in_table_job, two_job, down_job, up_job)
    out_table_job = Job(gather_table(low_out))
    token = advance(token, one_job, two_job, down_job, up_job)
    token = advance(token, one_job)
    layer_one, table_in = one_job.result, in_table_job.result
    code_ids = jnp.arange(table_in.shape[0])

    def own_frames(array):
        return lax.dynamic_slice_in_dim(array, half * frames, frames, 0)

    space_codes = own_frames(codes).reshape(-1)
    picked = dot_nn((space_codes[:, None] == code_ids[None, :]).astype(LOW), table_in)
    gain_all = layer_one[0][:, 4 * HALF :].T[:kinds].astype(WIDE)

    def layer_weights(layer):
        return [part[:, : 3 * HALF] for part in layer], [
            part[:, 3 * HALF : 4 * HALF] for part in layer
        ]

    def project_out(mixed, w_out):
        return in_order(*(dot_nn(mixed, part) for part in w_out), 1)

    w_in, w_out = layer_weights(layer_one)

    slot_ids = jnp.arange(SLOTS)
    segment = jnp.where(small > 0, slot_ids // SMALL_TOKENS, 0)
    dom_slot = jnp.sum((segment[:, None] == jnp.arange(CLIPS)[None, :]) * doms[None, :], axis=-1)
    domain_hot = (dom_slot[:, None] == jnp.arange(DOMAINS)[None, :]).astype(WIDE)
    counts = jnp.sum(jnp.sum(hidden_mask, axis=0)[:, None] * domain_hot, axis=0)[None, :]
    counts = Job(sum_over(counts, ("r", "z"))).finish()[0]
    scale = 1.0 / (MICRO * DOMAINS * jnp.maximum(counts, 1.0))
    slot_scale = jnp.sum(domain_hot * scale[None, :], axis=1)

    def time_order(array):
        mine = halves(array, 1)[0]
        return jnp.concatenate(halves(mine, 0), axis=0).reshape(-1)

    space_mask = own_frames(hidden_mask).reshape(-1)
    time_codes = time_order(codes)
    time_weight = time_order(hidden_mask * slot_scale[None, :])

    start = jnp.where(space_mask[:, None] > 0, gain_all[4], picked)
    normed_space = norm_forward(start, gain_all[0]).astype(LOW)
    packed_space = [dot_nn(normed_space, part).astype(LOW) for part in w_in]
    mixed_space = attention("space", (small, half), packed_space)
    mixed_space = advance(mixed_space, two_job)
    after_space = start + project_out(mixed_space, w_out)
    after_space = swap_slots(after_space.reshape(frames, SLOTS, D)).reshape(-1, D)
    after_space = advance(after_space, two_job, out_table_job)
    normed_time = norm_forward(after_space, gain_all[1]).astype(LOW)
    normed_time = advance(normed_time, two_job, down_job, up_job, out_table_job)
    next_in, next_out = layer_weights(two_job.finish())
    packed_time = [
        dot_nn(normed_time, part).astype(LOW).reshape(FRAMES, -1, 3 * HALF) for part in next_in
    ]
    mixed_time = attention("time", (half, half), packed_time).reshape(-1, D)
    after_time = after_space + project_out(mixed_time, next_out)
    normed_ffn = norm_forward(after_time, gain_all[2]).astype(LOW)
    ups, downs = up_job.finish(), down_job.finish()
    table_out = out_table_job.finish()
    pres = [dot_nn(normed_ffn, up) for up in ups]
    activs = [gelu(pre).astype(LOW) for pre in pres]
    after_ffn = after_time + dot_nn(activs[0], downs[0]) + dot_nn(activs[1], downs[1])
    final = norm_forward(after_ffn, gain_all[3]).astype(LOW)
    logits = dot_nt(final, table_out)
    hits = time_codes[:, None] == code_ids[None, :]
    top = jnp.max(logits, axis=1, keepdims=True)
    log_total = top + jnp.log(jnp.sum(jnp.exp(logits - top), axis=1, keepdims=True))
    target = jnp.sum(jnp.where(hits, logits, 0.0), axis=1)
    loss_part = jnp.sum(time_weight * (log_total[:, 0] - target))
    grad_logits = (time_weight[:, None] * (jnp.exp(logits - log_total) - hits)).astype(LOW)

    def product(make, left, mine, other, *rest):
        return Job(make(dot_tn(left, other).astype(LOW), lambda: dot_tn(left, mine), *rest))

    head_job = product(reduce_table, grad_logits, *halves(final, 1))
    grad_final = dot_nn(grad_logits, table_out)
    grad_ffn, gain_three = norm_backward(after_ffn, gain_all[3], grad_final)
    up_low = grad_ffn.astype(LOW)
    contract_job = Job(
        reduce_owned(
            dot_tn(activs[1], up_low).astype(LOW),
            lambda: dot_tn(activs[0], up_low),
            ("m", "r", "z"),
        )
    )
    grad_activs = [dot_nt(up_low, down) for down in downs]
    grad_pres = [gelu_backward(pre, grad).astype(LOW) for pre, grad in zip(pres, grad_activs)]
    grad_pres = advance(grad_pres, head_job, contract_job)
    expand_job = product(
        reduce_layer, normed_ffn, grad_pres[0], grad_pres[1], ("m", "r", "z"), block
    )
    grad_normed = dot_nt(grad_pres[0], ups[0]) + dot_nt(grad_pres[1], ups[1])
    inward, gain_two = norm_backward(after_time, gain_all[2], grad_normed)
    grad_time = grad_ffn + inward
    up_low = grad_time.astype(LOW)
    up_low = advance(up_low, head_job, expand_job)
    mine, other = halves(up_low, 1)
    out_job = product(reduce_layer, mixed_time, mine, other, ("r", "m", "z"))
    grad_mixed = (dot_nt(mine, next_out[0]) + dot_nt(other, next_out[1])).astype(LOW)
    grad_packed = attention("time", (half, half), packed_time, grad_mixed)
    grad_packed = [part.reshape(-1, 3 * HALF) for part in grad_packed]
    grad_packed = advance(grad_packed, head_job, contract_job, out_job)
    in_job = product(reduce_layer, normed_time, *grad_packed, ("r", "m", "z"), HALF)
    grad_normed = dot_nt(grad_packed[0], next_in[0]) + dot_nt(grad_packed[1], next_in[1])
    inward, gain_one = norm_backward(after_space, gain_all[1], grad_normed)
    grad_space = swap_frames((grad_time + inward).reshape(FRAMES, -1, D)).reshape(-1, D)
    up_low = grad_space.astype(LOW)
    up_low = advance(up_low, head_job, out_job, in_job)
    mine, other = halves(up_low, 1)
    first_out_job = product(reduce_layer, mixed_space, mine, other, ("r", "m", "z"))
    grad_mixed = (dot_nt(mine, w_out[0]) + dot_nt(other, w_out[1])).astype(LOW)
    grad_mixed = advance(grad_mixed, contract_job)
    grad_packed = attention("space", (small, half), packed_space, grad_mixed)
    grad_packed = advance(
        grad_packed, head_job, contract_job, expand_job, out_job, in_job, first_out_job
    )
    first_in_job = product(
        reduce_layer, normed_space, *grad_packed, ("r", "m", "z"), HALF, 2
    )
    grad_normed = dot_nt(grad_packed[0], w_in[0]) + dot_nt(grad_packed[1], w_in[1])
    grad_normed = advance(grad_normed, first_in_job, head_job, out_job)
    inward, gain_zero = norm_backward(start, gain_all[0], grad_normed)
    grad_start = grad_space + inward
    mask_grad = jnp.sum(grad_start * space_mask[:, None], axis=0)
    chosen = (jnp.where(space_mask > 0, -1, space_codes)[:, None] == code_ids[None, :]).astype(LOW)
    start_low = grad_start.astype(LOW)
    embed_job = product(reduce_table, chosen, *halves(start_low, 1))

    gain_grads = jnp.stack([gain_zero, gain_one, gain_two, gain_three, mask_grad])
    gain_job = Job(sum_over(gain_grads, ("h", "m", "r", "z")))
    token = jnp.zeros((), WIDE)
    late = (expand_job, contract_job, in_job, first_out_job)
    token = advance(token, embed_job, gain_job, head_job, out_job, *late)
    token = advance(token, first_in_job)
    token = advance(token, embed_job, gain_job, first_out_job)
    token = advance(token, first_in_job)
    token = advance(token, embed_job, gain_job, expand_job, in_job, first_out_job)
    token = advance(token, first_in_job, embed_job, gain_job)

    jobs = (in_job, first_in_job, out_job, first_out_job, expand_job, contract_job)
    jobs = jobs + (embed_job, head_job)
    owner = jnp.int32(0)
    for axis in ALL:
        owner = owner * lax.axis_size(axis) + lax.axis_index(axis)
    width = gains.shape[1]
    gain_grads = lax.dynamic_slice_in_dim(gain_job.finish(), owner * width, width, 1)
    results = [job.finish() for job in jobs]
    owned = sum(square for _, square in results) + jnp.sum(gain_grads * gain_grads)
    sums = jnp.stack([owned, loss_part]).reshape(1, 2)
    sums = Job(sum_over(sums, ("h", "m", "r", "z"))).finish()
    square_sum, loss = sums[0, 0], sums[0, 1]
    norm = jnp.sqrt(square_sum)
    factor = jnp.minimum(1.0, CLIP / (norm + 1e-06))

    made = [grad for grad, _ in results]
    grads = (
        jnp.stack([made[1], made[0]]),
        jnp.stack([made[3], made[2]]),
        made[4],
        made[5],
        gain_grads,
        jnp.stack([made[6], made[7]]),
    )
    params = (attend_in, attend_out, expand, contract, gains, tables)
    firsts = (mean_in, mean_out, mean_expand, mean_contract, mean_gains, mean_tables)
    seconds = (square_in, square_out, square_expand, square_contract, square_gains, square_tables)
    rates = (RATE, RATE, RATE, RATE, RATE_SMALL, RATE)
    decays = (DECAY, DECAY, DECAY, DECAY, 0.0, DECAY)
    results = [
        adamw(p, factor * g, f, s, r, k)
        for p, g, f, s, r, k in zip(params, grads, firsts, seconds, rates, decays)
    ]
    return (loss, norm) + tuple(result[k] for k in range(3) for result in results)


def solution(mesh):
    dp, code = mesh.shape["dp"], mesh.shape["code"]
    deep = next(n for n in (4, 2, 1) if dp % n == 0)
    fine = Mesh(mesh.devices.reshape(deep, dp // deep, MICRO, code // MICRO), ALL)
    group = ("z", "r")
    weights = (
        P(None, ALL, None),
        P(None, ALL, None),
        P(ALL, None),
        P(ALL, None),
        P(None, ALL),
        P(None, ("m", "h"), None),
    )
    return jax.shard_map(
        on_device,
        mesh=fine,
        in_specs=(
            P(None, group, None, None),
            P(None, group, None, None),
            P(None, group),
            P(None, group, None),
        )
        + weights * 3,
        out_specs=(P(), P()) + weights * 3,
        check_vma=False,
    )
```

```python
import functools
from typing import NamedTuple

import jax
import jax.numpy as jnp
from jax import lax
from jax.experimental import pallas as pl
from jax.experimental.pallas import tpu as pltpu
from jax.sharding import Mesh, PartitionSpec as P

D = 1024
HEADS = 16
HEAD = 64
FRAMES = 4
SLOTS = 256
SMALL_TOKENS = 64
CLIPS = 4
DOMAINS = 4
MICRO = 2
STEP = 10


EPS = 1e-05
NEG = -1e30
BETA_ONE = 0.9
BETA_TWO = 0.95
ADAM_EPS = 1e-08
DECAY = 0.1
RATE = 0.02
RATE_SMALL = 0.2
CLIP = 0.005
LOW = jnp.bfloat16
WIDE = jnp.float32
ALL = ("z", "r", "m", "h")
GROUP = 256
LANES = 128


def shifted(part, axis, shift):
    n = lax.axis_size(axis)
    return lax.ppermute(part, axis, [((i + shift) % n, i) for i in range(n)])


def at(array, index, dim):
    return lax.dynamic_index_in_dim(array, index, dim, keepdims=False)


def sent_around(part, axis):
    return [shifted(part, axis, shift) for shift in range(1, lax.axis_size(axis))]


def placed(part, others, axis, dim):
    n = lax.axis_size(axis)
    mine = lax.axis_index(axis)
    whole = jnp.broadcast_to(
        jnp.expand_dims(part, dim), part.shape[:dim] + (n,) + part.shape[dim:]
    )
    for shift, other in zip(range(1, n), others):
        whole = lax.dynamic_update_index_in_dim(whole, other, (mine + shift) % n, dim)
    return whole


def gather_axis(part, axis, dim):
    return placed(part, sent_around(part, axis), axis, dim)


def halves(array, dim):
    size = array.shape[dim] // lax.axis_size("h")
    half = lax.axis_index("h")
    return [
        lax.dynamic_slice_in_dim(array, start * size, size, dim) for start in (half, 1 - half)
    ]


class Squared(NamedTuple):
    square: jax.Array
    flight: list


class Job:
    def __init__(self, steps):
        self.steps = steps
        self.result = self.square = None
        self.flight = next(steps)

    def resume(self, arrived):
        try:
            self.flight = self.steps.send(arrived)
        except StopIteration as stop:
            self.flight, self.result = None, stop.value
        if isinstance(self.flight, Squared):
            self.square, self.flight = self.flight

    def finish(self):
        while self.flight is not None:
            self.resume(self.flight)
        return self.result


def advance(value, *jobs):
    jobs = [job for job in jobs if job.flight is not None]
    value, flights = lax.optimization_barrier((value, [job.flight for job in jobs]))
    for job, flight in zip(jobs, flights):
        job.resume(flight)
    return value


def gather_half(part):
    for axis, dim in (("r", 0), ("z", 0), ("m", 2)):
        others = yield sent_around(part, axis)
        part = placed(part, others, axis, dim)
    own = part.reshape(-1, part.shape[-1])
    (other,) = yield [shifted(own, "h", 1)]
    return (own, other)


def gather_table(part):
    others = yield sent_around(part, "m")
    part = placed(part, others, "m", 0)
    others = yield sent_around(part, "h")
    return placed(part, others, "h", 1).reshape(-1, part.shape[-1])


def by_owner(array, block):
    seen = array.reshape(array.shape[0], -1, 2, block)
    half = lax.axis_index("h")
    return [at(seen, which, 2).reshape(array.shape[0], -1) for which in (half, 1 - half)]


def gather_columns(part, block):
    mine, other = by_owner(part, block)
    (other,) = yield [shifted(other, "h", 1)]
    pair = placed(mine, [other], "h", 0)
    result = yield from gather_half(pair.reshape(-1, mine.shape[1]))
    return result


def pieces_of(total, dim, axis):
    n = lax.axis_size(axis)
    mine = lax.axis_index(axis)
    return [
        shifted(at(total, (mine + shift) % n, dim), axis, n - shift) for shift in range(1, n)
    ]


def added(total, dim, axis, pieces):
    total = at(total, lax.axis_index(axis), dim).astype(WIDE)
    for piece in pieces:
        total = total + piece.astype(WIDE)
    return total


def reduce_rows(other, own, names, order, parts=1):
    (arrived,) = yield [shifted(other, "h", 1)]
    total = (own() + arrived.astype(WIDE)).astype(LOW)
    names = list(names)
    total = total.reshape(
        tuple(lax.axis_size(name) for name in names) + (-1, total.shape[-1])
    )
    totals = jnp.split(total, parts, axis=-1)
    orders = [list(order), [order[1], order[0]] + list(order[2:])][:parts]
    left = [list(names) for _ in totals]
    for step in range(2):
        dims = [names.index(axes[step]) for names, axes in zip(left, orders)]
        steps = list(zip(totals, dims, [axes[step] for axes in orders]))
        pieces = yield [pieces_of(*each) for each in steps]
        totals = [added(*each, arrived).astype(LOW) for each, arrived in zip(steps, pieces)]
        for names, dim in zip(left, dims):
            names.pop(dim)
    total = totals[0] if parts == 1 else jnp.concatenate(totals, axis=-1)
    dim = left[0].index(order[2])
    pieces = yield pieces_of(total, dim, order[2])
    return added(total, dim, order[2], pieces)


def swap_rows(total, square=None):
    seen = total.reshape(2, -1, total.shape[-1])
    half = lax.axis_index("h")
    flight = [shifted(at(seen, 1 - half, 0), "h", 1)]
    (other,) = yield flight if square is None else Squared(square, flight)
    return (at(seen, half, 0), other)


def in_order(mine, other, dim):
    first = lax.axis_index("h") == 0
    return jnp.concatenate(
        [jnp.where(first, mine, other), jnp.where(first, other, mine)], axis=dim
    )


def reduce_layer(other, own, order, block=None, parts=1):
    total = yield from reduce_rows(other, own, ("z", "r", "m"), order, parts)
    total = total.reshape(-1, total.shape[-1])
    mine, other = yield from swap_rows(total, jnp.sum(total * total))
    if block is None:
        return in_order(mine, other, 1)
    rows = mine.shape[0]
    mine, other = (half.reshape(rows, -1, 1, block) for half in (mine, other))
    return in_order(mine, other, 2).reshape(rows, -1)


def reduce_owned(other, own, order, parts):
    total = yield from reduce_rows(other, own, ("z", "r", "m"), order, parts)
    total = total.reshape(-1, total.shape[-1])
    yield Squared(jnp.sum(total * total), [])
    return total


def reduce_table(other, own):
    total = yield from reduce_rows(other, own, ("m", "h", "r", "z"), ("m", "r", "z"))
    square = jnp.sum(total * total)
    total = total.astype(LOW)
    others = yield Squared(square, sent_around(total, "z"))
    total = placed(total, others, "z", 1)
    others = yield sent_around(total, "r")
    total = placed(total, others, "r", 1)
    mine, other = yield from swap_rows(total.reshape(-1, total.shape[-1]))
    return in_order(mine, other, 1).astype(WIDE)


def sum_over(part, axes):
    for axis in axes:
        n = lax.axis_size(axis)
        if n == 4:
            others = yield sent_around(part, axis)
            part = jnp.sum(placed(part, others, axis, 0), axis=0)
            continue
        shift = n // 2
        while shift:
            (other,) = yield [shifted(part, axis, shift)]
            part = part + other
            shift //= 2
    return part


def norm_forward(values, gain):
    return values * lax.rsqrt(jnp.mean(values * values, axis=-1, keepdims=True) + EPS) * gain


def norm_backward(values, gain, upstream):
    factor = lax.rsqrt(jnp.mean(values * values, axis=-1, keepdims=True) + EPS)
    scaled = upstream * gain
    inward = factor * scaled - values * factor**3 * jnp.mean(
        scaled * values, axis=-1, keepdims=True
    )
    gain_grad = jnp.sum(upstream * values * factor, axis=0)
    return (inward, gain_grad)


def dot_nt(left, right):
    return lax.dot_general(left, right, (((1,), (1,)), ((), ())), preferred_element_type=WIDE)


def dot_tn(left, right):
    return lax.dot_general(left, right, (((0,), (0,)), ((), ())), preferred_element_type=WIDE)


def dot_nn(left, right):
    return jnp.dot(left, right, preferred_element_type=WIDE)


def allowed_pairs(kind, scalar, count):
    row = lax.broadcasted_iota(jnp.int32, (count, count), 0)
    col = lax.broadcasted_iota(jnp.int32, (count, count), 1)
    if kind == "space":
        return (scalar == 0) | (row // SMALL_TOKENS == col // SMALL_TOKENS)
    lanes = count // FRAMES
    own = FRAMES // 2
    row_frame, col_frame = row // lanes, col // lanes
    row_at = row_frame + jnp.where(scalar == 0, 0, jnp.where(row_frame < own, own, -own))
    col_at = col_frame + jnp.where(scalar == 0, 0, jnp.where(col_frame < own, own, -own))
    return (row % lanes == col % lanes) & (col_at <= row_at)


def softmax_rows(query, key, allowed):
    scores = jnp.where(allowed, dot_nt(query, key) * HEAD ** (-0.5), NEG)
    expd = jnp.exp(scores - jnp.max(scores, axis=-1, keepdims=True))
    return expd / jnp.sum(expd, axis=-1, keepdims=True)


def block_of(ref, start, kind):
    if kind == "space":
        return ref[:, pl.ds(start, LANES)]
    part = ref[:, :, pl.ds(start, LANES)]
    return part.reshape(-1, LANES)


def store_to(ref, start, kind, value):
    if kind == "space":
        ref[:, pl.ds(start, LANES)] = value
    else:
        ref[:, :, pl.ds(start, LANES)] = value.reshape(FRAMES, -1, LANES)


def forward_body(kind, scalar_ref, packed_ref, mixed_ref):
    allowed = allowed_pairs(kind, scalar_ref[0], GROUP)
    first = lax.broadcasted_iota(jnp.int32, (GROUP, LANES), 1) < HEAD

    def turn(pair, _):
        start = pl.multiple_of(pair * LANES, LANES)
        query = block_of(packed_ref, start, kind)
        key = block_of(packed_ref, pl.multiple_of(D + start, LANES), kind)
        value = block_of(packed_ref, pl.multiple_of(2 * D + start, LANES), kind)
        zero = jnp.zeros_like(query)
        one = dot_nn(softmax_rows(jnp.where(first, query, zero), key, allowed).astype(LOW), value)
        two = dot_nn(softmax_rows(jnp.where(first, zero, query), key, allowed).astype(LOW), value)
        store_to(mixed_ref, start, kind, jnp.where(first, one, two).astype(LOW))
        return 0

    lax.fori_loop(0, D // LANES, turn, 0, unroll=4)


def backward_body(kind, scalar_ref, packed_ref, up_ref, out_ref):
    allowed = allowed_pairs(kind, scalar_ref[0], GROUP)
    first = lax.broadcasted_iota(jnp.int32, (GROUP, LANES), 1) < HEAD

    def turn(pair, _):
        start = pl.multiple_of(pair * LANES, LANES)
        key_at = pl.multiple_of(D + start, LANES)
        value_at = pl.multiple_of(2 * D + start, LANES)
        query = block_of(packed_ref, start, kind)
        key = block_of(packed_ref, key_at, kind)
        value = block_of(packed_ref, value_at, kind)
        up = block_of(up_ref, start, kind)
        zero = jnp.zeros_like(query)
        grads = []
        for mine in (first, ~first):
            probs = softmax_rows(jnp.where(mine, query, zero), key, allowed)
            inner = dot_nt(jnp.where(mine, up, zero), value)
            total = jnp.sum(probs * inner, axis=-1, keepdims=True)
            scores = (probs * (inner - total) * HEAD ** (-0.5)).astype(LOW)
            grads.append((dot_nn(scores, key), dot_tn(scores, query), dot_tn(probs.astype(LOW), up)))
        for place, one, two in zip((start, key_at, value_at), *grads):
            store_to(out_ref, place, kind, jnp.where(first, one, two).astype(LOW))
        return 0

    lax.fori_loop(0, D // LANES, turn, 0, unroll=2)


def attention(kind, scalar, packed, up=None):
    shape = packed.shape[:-1]
    if kind == "space":
        grid, block, where = (shape[0] // GROUP,), (GROUP,), lambda g, s: (g, 0)
    else:
        grid, block, where = (FRAMES * shape[1] // GROUP,), (FRAMES, GROUP // FRAMES), lambda g, s: (0, g, 0)
    wide = pl.BlockSpec(block + (3 * D,), where)
    narrow = pl.BlockSpec(block + (D,), where)
    body, last, ins, flops = forward_body, D, (packed,), 9e9
    if up is not None:
        body, last, flops = backward_body, 3 * D, 22e9
        ins = (packed, up.reshape(shape + (D,)))
    return pl.pallas_call(
        functools.partial(body, kind),
        out_shape=jax.ShapeDtypeStruct(shape + (last,), LOW),
        grid_spec=pltpu.PrefetchScalarGridSpec(
            num_scalar_prefetch=1,
            grid=grid,
            in_specs=[wide, narrow][: len(ins)],
            out_specs=narrow if up is None else wide,
        ),
        cost_estimate=pl.CostEstimate(
            flops=int(flops), transcendentals=4 * HEADS * GROUP * GROUP, bytes_accessed=8 << 20
        ),
    )(scalar.reshape(1).astype(jnp.int32), *ins)


def adamw(weight, grad, first, second, rate, decay):
    first_new = BETA_ONE * first + (1.0 - BETA_ONE) * grad
    second_new = BETA_TWO * second + (1.0 - BETA_TWO) * grad * grad
    unbiased_first = first_new / (1.0 - BETA_ONE**STEP)
    unbiased_second = second_new / (1.0 - BETA_TWO**STEP)
    updated = weight - rate * (
        unbiased_first / (jnp.sqrt(unbiased_second) + ADAM_EPS) + decay * weight
    )
    return (updated, first_new, second_new)


def gelu(values):
    return jax.nn.gelu(values, approximate=True)


def gelu_backward(values, upstream):
    return jax.vjp(gelu, values)[1](upstream)[0]


def swap_slots(values):
    mine, other = halves(values, 1)
    return jnp.concatenate([mine, shifted(other, "h", 1)], axis=0)


def swap_frames(values):
    half = lax.axis_index("h")
    mine, other = jnp.split(values, 2, axis=0)
    other = shifted(other, "h", 1)
    return jnp.where(
        half == 0,
        jnp.concatenate([mine, other], axis=1),
        jnp.concatenate([other, mine], axis=1),
    )


def on_device(
    tokens,
    masked,
    small_grid,
    domains,
    attend_in,
    attend_out,
    expand,
    contract,
    gains,
    tables,
    mean_in,
    mean_out,
    mean_expand,
    mean_contract,
    mean_gains,
    mean_tables,
    square_in,
    square_out,
    square_expand,
    square_contract,
    square_gains,
    square_tables,
):
    micro = lax.axis_index("m")
    half = lax.axis_index("h")
    frames = FRAMES // lax.axis_size("h")
    block = contract.shape[0]
    kinds = gains.shape[0]

    def of_micro(array):
        return at(array[:, 0], micro, 0)

    codes = of_micro(tokens)
    hidden_mask = of_micro(masked).astype(WIDE)
    small = of_micro(small_grid)
    doms = of_micro(domains)

    turned = jnp.pad(gains.T, ((0, 0), (0, LANES - kinds)))
    layers = [attend_in[0], attend_out[0], turned, attend_in[1], attend_out[1]]
    ends = [0]
    for array in layers:
        ends.append(ends[-1] + array.shape[1])
    gathered = jnp.concatenate(layers, axis=1).astype(LOW)
    gathered = lax.all_gather(gathered, ALL, axis=0, tiled=True)
    low_in, low_out = tables.astype(LOW)
    up_job = Job(gather_columns(expand.astype(LOW), block))
    down_job = Job(gather_half(contract.astype(LOW)))
    in_table_job = Job(gather_table(low_in))
    token = advance(jnp.zeros((), WIDE), up_job, down_job)
    token = advance(token, in_table_job, up_job)
    table_in = in_table_job.finish()
    code_ids = jnp.arange(table_in.shape[0])

    def own_frames(array):
        return lax.dynamic_slice_in_dim(array, half * frames, frames, 0)

    space_codes = own_frames(codes).reshape(-1)
    picked = dot_nn((space_codes[:, None] == code_ids[None, :]).astype(LOW), table_in)
    token = advance(token, down_job)
    out_table_job = Job(gather_table(low_out))
    token = advance(token, up_job)
    picked, token = lax.optimization_barrier((picked, token))
    gathered = advance(gathered, out_table_job)
    first_in, first_out, turned, next_in, next_out = (
        gathered[:, start:end] for start, end in zip(ends, ends[1:])
    )
    w_in, w_out = (first_in, next_in), (first_out, next_out)
    gain_all = turned.T[:kinds].astype(WIDE)

    slot_ids = jnp.arange(SLOTS)
    segment = jnp.where(small > 0, slot_ids // SMALL_TOKENS, 0)
    dom_slot = jnp.sum((segment[:, None] == jnp.arange(CLIPS)[None, :]) * doms[None, :], axis=-1)
    domain_hot = (dom_slot[:, None] == jnp.arange(DOMAINS)[None, :]).astype(WIDE)
    counts = jnp.sum(jnp.sum(hidden_mask, axis=0)[:, None] * domain_hot, axis=0)[None, :]
    counts = Job(sum_over(counts, ("r", "z"))).finish()[0]
    scale = 1.0 / (MICRO * DOMAINS * jnp.maximum(counts, 1.0))
    slot_scale = jnp.sum(domain_hot * scale[None, :], axis=1)

    def time_order(array):
        mine = halves(array, 1)[0]
        return jnp.concatenate(halves(mine, 0), axis=0).reshape(-1)

    space_mask = own_frames(hidden_mask).reshape(-1)
    time_codes = time_order(codes)
    time_weight = time_order(hidden_mask * slot_scale[None, :])

    start = jnp.where(space_mask[:, None] > 0, gain_all[4], picked)
    normed_space = norm_forward(start, gain_all[0]).astype(LOW)
    packed_space = dot_nn(normed_space, w_in[0]).astype(LOW)
    mixed_space = attention("space", small, packed_space)
    after_space = start + dot_nn(mixed_space, w_out[0])
    after_space = swap_slots(after_space.reshape(frames, SLOTS, D)).reshape(-1, D)
    normed_time = norm_forward(after_space, gain_all[1]).astype(LOW)
    normed_time = advance(normed_time, up_job, down_job, out_table_job)
    table_out = out_table_job.finish()
    packed_time = dot_nn(normed_time, w_in[1]).astype(LOW).reshape(FRAMES, -1, 3 * D)
    mixed_time = attention("time", half, packed_time).reshape(-1, D)
    after_time = after_space + dot_nn(mixed_time, w_out[1])
    normed_ffn = norm_forward(after_time, gain_all[2]).astype(LOW)
    ups, downs = up_job.finish(), down_job.finish()
    pres = [dot_nn(normed_ffn, up) for up in ups]
    activs = [gelu(pre).astype(LOW) for pre in pres]
    after_ffn = after_time + dot_nn(activs[0], downs[0]) + dot_nn(activs[1], downs[1])
    final = norm_forward(after_ffn, gain_all[3]).astype(LOW)
    logits = dot_nt(final, table_out)
    hits = time_codes[:, None] == code_ids[None, :]
    top = jnp.max(logits, axis=1, keepdims=True)
    log_total = top + jnp.log(jnp.sum(jnp.exp(logits - top), axis=1, keepdims=True))
    target = jnp.sum(jnp.where(hits, logits, 0.0), axis=1)
    loss_part = jnp.sum(time_weight * (log_total[:, 0] - target))
    grad_logits = (time_weight[:, None] * (jnp.exp(logits - log_total) - hits)).astype(LOW)

    def product(make, left, mine, other, *rest):
        return Job(make(dot_tn(left, other).astype(LOW), lambda: dot_tn(left, mine), *rest))

    head_job = product(reduce_table, grad_logits, *halves(final, 1))
    grad_final = dot_nn(grad_logits, table_out)
    grad_ffn, gain_three = norm_backward(after_ffn, gain_all[3], grad_final)
    up_low = grad_ffn.astype(LOW)
    contract_job = Job(
        reduce_owned(
            dot_tn(activs[1], up_low).astype(LOW),
            lambda: dot_tn(activs[0], up_low),
            ("m", "r", "z"),
            2,
        )
    )
    grad_activs = [dot_nt(up_low, down) for down in downs]
    grad_pres = [gelu_backward(pre, grad).astype(LOW) for pre, grad in zip(pres, grad_activs)]
    grad_pres = advance(grad_pres, head_job, contract_job)
    expand_job = product(
        reduce_layer, normed_ffn, grad_pres[0], grad_pres[1], ("r", "m", "z"), block, 2
    )
    grad_normed = dot_nt(grad_pres[0], ups[0]) + dot_nt(grad_pres[1], ups[1])
    inward, gain_two = norm_backward(after_time, gain_all[2], grad_normed)
    grad_time = grad_ffn + inward
    up_low = grad_time.astype(LOW)
    up_low = advance(up_low, head_job, expand_job)
    out_job = product(reduce_layer, mixed_time, *halves(up_low, 1), ("m", "r", "z"))
    grad_mixed = dot_nt(up_low, w_out[1]).astype(LOW)
    grad_packed = attention("time", half, packed_time, grad_mixed).reshape(-1, 3 * D)
    grad_packed = advance(grad_packed, head_job, contract_job, out_job)
    in_job = product(
        reduce_layer, normed_time, *halves(grad_packed, 1), ("m", "r", "z"), None, 2
    )
    grad_normed = dot_nt(grad_packed, w_in[1])
    inward, gain_one = norm_backward(after_space, gain_all[1], grad_normed)
    grad_space = swap_frames((grad_time + inward).reshape(FRAMES, -1, D)).reshape(-1, D)
    up_low = grad_space.astype(LOW)
    up_low = advance(up_low, head_job, contract_job, out_job, in_job)
    first_out_job = product(reduce_layer, mixed_space, *halves(up_low, 1), ("r", "m", "z"))
    grad_mixed = dot_nt(up_low, w_out[0]).astype(LOW)
    grad_mixed = advance(grad_mixed, contract_job, expand_job, first_out_job)
    grad_packed = attention("space", small, packed_space, grad_mixed)
    grad_packed = advance(
        grad_packed, head_job, expand_job, out_job, in_job, first_out_job
    )
    first_in_job = product(
        reduce_layer, normed_space, *halves(grad_packed, 1), ("r", "m", "z"), None, 2
    )
    grad_normed = dot_nt(grad_packed, w_in[0])
    grad_normed = advance(grad_normed, first_in_job, head_job, out_job, in_job, first_out_job)
    inward, gain_zero = norm_backward(start, gain_all[0], grad_normed)
    grad_start = grad_space + inward
    mask_grad = jnp.sum(grad_start * space_mask[:, None], axis=0)
    chosen = (jnp.where(space_mask > 0, -1, space_codes)[:, None] == code_ids[None, :]).astype(LOW)
    start_low = grad_start.astype(LOW)
    embed_job = product(reduce_table, chosen, *halves(start_low, 1))

    gain_grads = jnp.stack([gain_zero, gain_one, gain_two, gain_three, mask_grad])
    gain_job = Job(sum_over(gain_grads, ("h", "m", "r", "z")))
    token = jnp.zeros((), WIDE)
    token = advance(token, embed_job, gain_job, head_job, out_job, expand_job)
    token = advance(token, first_in_job)
    token = advance(token, embed_job, gain_job, in_job, first_out_job)
    token = advance(token, first_in_job)
    token = advance(token, embed_job, gain_job, expand_job)
    token = advance(token, first_in_job, embed_job, gain_job, in_job, first_out_job)

    owner = jnp.int32(0)
    for axis in ALL:
        owner = owner * lax.axis_size(axis) + lax.axis_index(axis)
    width = gains.shape[1]
    gain_grads = lax.dynamic_slice_in_dim(gain_job.finish(), owner * width, width, 1)
    jobs = (in_job, first_in_job, out_job, first_out_job, expand_job, contract_job)
    jobs = jobs + (embed_job, head_job)
    owned = sum(job.square for job in jobs) + jnp.sum(gain_grads * gain_grads)
    sums = jnp.stack([owned, loss_part]).reshape(1, 2)
    norm_job = Job(sum_over(sums, ("h", "m", "r", "z")))
    while norm_job.flight is not None:
        token = advance(token, norm_job, *jobs)
    results = [(job.finish(), None) for job in jobs]
    square_sum, loss = norm_job.result[0, 0], norm_job.result[0, 1]
    norm = jnp.sqrt(square_sum)
    factor = jnp.minimum(1.0, CLIP / (norm + 1e-06))

    made = [grad for grad, _ in results]
    grads = (
        jnp.stack([made[1], made[0]]),
        jnp.stack([made[3], made[2]]),
        made[4],
        made[5],
        gain_grads,
        jnp.stack([made[6], made[7]]),
    )
    params = (attend_in, attend_out, expand, contract, gains, tables)
    firsts = (mean_in, mean_out, mean_expand, mean_contract, mean_gains, mean_tables)
    seconds = (square_in, square_out, square_expand, square_contract, square_gains, square_tables)
    rates = (RATE, RATE, RATE, RATE, RATE_SMALL, RATE)
    decays = (DECAY, DECAY, DECAY, DECAY, 0.0, DECAY)
    results = [
        adamw(p, factor * g, f, s, r, k)
        for p, g, f, s, r, k in zip(params, grads, firsts, seconds, rates, decays)
    ]
    return (loss, norm) + tuple(result[k] for k in range(3) for result in results)


def solution(mesh):
    dp, code = mesh.shape["dp"], mesh.shape["code"]
    deep = next(n for n in (4, 2, 1) if dp % n == 0)
    fine = Mesh(mesh.devices.reshape(deep, dp // deep, MICRO, code // MICRO), ALL)
    group = ("z", "r")
    weights = (
        P(None, ALL, None),
        P(None, ALL, None),
        P(ALL, None),
        P(ALL, None),
        P(None, ALL),
        P(None, ("m", "h"), None),
    )
    return jax.shard_map(
        on_device,
        mesh=fine,
        in_specs=(
            P(None, group, None, None),
            P(None, group, None, None),
            P(None, group),
            P(None, group, None),
        )
        + weights * 3,
        out_specs=(P(), P()) + weights * 3,
        check_vma=False,
    )
```

```python
import functools
from typing import NamedTuple

import jax
import jax.numpy as jnp
from jax import lax
from jax.experimental import pallas as pl
from jax.experimental.pallas import tpu as pltpu
from jax.sharding import Mesh, PartitionSpec as P

D = 1024
HEADS = 16
HEAD = 64
FRAMES = 4
SLOTS = 256
SMALL_TOKENS = 64
CLIPS = 4
DOMAINS = 4
MICRO = 2
STEP = 10


EPS = 1e-05
NEG = -1e30
BETA_ONE = 0.9
BETA_TWO = 0.95
ADAM_EPS = 1e-08
DECAY = 0.1
RATE = 0.02
RATE_SMALL = 0.2
CLIP = 0.005
LOW = jnp.bfloat16
WIDE = jnp.float32
ALL = ("z", "r", "m", "h")
GROUP = 256
LANES = 128


def shifted(part, axis, shift):
    n = lax.axis_size(axis)
    return lax.ppermute(part, axis, [((i + shift) % n, i) for i in range(n)])


def at(array, index, dim):
    return lax.dynamic_index_in_dim(array, index, dim, keepdims=False)


def sent_around(part, axis):
    return [shifted(part, axis, shift) for shift in range(1, lax.axis_size(axis))]


def placed(part, others, axis, dim):
    n = lax.axis_size(axis)
    mine = lax.axis_index(axis)
    whole = jnp.broadcast_to(
        jnp.expand_dims(part, dim), part.shape[:dim] + (n,) + part.shape[dim:]
    )
    for shift, other in zip(range(1, n), others):
        whole = lax.dynamic_update_index_in_dim(whole, other, (mine + shift) % n, dim)
    return whole


def gather_axis(part, axis, dim):
    return placed(part, sent_around(part, axis), axis, dim)


def halves(array, dim):
    size = array.shape[dim] // lax.axis_size("h")
    half = lax.axis_index("h")
    return [
        lax.dynamic_slice_in_dim(array, start * size, size, dim) for start in (half, 1 - half)
    ]


class Squared(NamedTuple):
    square: jax.Array
    flight: list


class Job:
    def __init__(self, steps):
        self.steps = steps
        self.result = self.square = None
        self.flight = next(steps)

    def resume(self, arrived):
        try:
            self.flight = self.steps.send(arrived)
        except StopIteration as stop:
            self.flight, self.result = None, stop.value
        if isinstance(self.flight, Squared):
            self.square, self.flight = self.flight

    def finish(self):
        while self.flight is not None:
            self.resume(self.flight)
        return self.result


def advance(value, *jobs):
    jobs = [job for job in jobs if job.flight is not None]
    value, flights = lax.optimization_barrier((value, [job.flight for job in jobs]))
    for job, flight in zip(jobs, flights):
        job.resume(flight)
    return value


def split_columns(array):
    cut = array.shape[-1] // (2 * LANES) * LANES
    return array[..., :cut], array[..., cut:]


def gather_deep(part):
    if lax.axis_size("z") != 4:
        others = yield sent_around(part, "z")
        return placed(part, others, "z", 0)
    above, below = yield [shifted(part, "z", 1), shifted(part, "z", 3)]
    first, second = split_columns(above)[0], split_columns(below)[1]
    first, second = yield [shifted(first, "z", 1), shifted(second, "z", 3)]
    mine = lax.axis_index("z")
    whole = jnp.broadcast_to(part[None], (4,) + part.shape)
    whole = lax.dynamic_update_index_in_dim(whole, above, (mine + 1) % 4, 0)
    whole = lax.dynamic_update_index_in_dim(whole, below, (mine + 3) % 4, 0)
    zero = jnp.int32(0)
    place = [(mine + 2) % 4] + [zero] * part.ndim
    whole = lax.dynamic_update_slice(whole, first[None], place)
    place[-1] = jnp.int32(first.shape[-1])
    return lax.dynamic_update_slice(whole, second[None], place)


def gather_flat(part, dim):
    first, second = split_columns(part)
    one, two = yield (sent_around(first, "m"), sent_around(second, "r"))
    first, second = placed(first, one, "m", dim), placed(second, two, "r", dim)
    one, two = yield (sent_around(first, "r"), sent_around(second, "m"))
    first, second = placed(first, one, "r", dim), placed(second, two, "m", dim + 1)
    return jnp.concatenate([first, second], axis=-1)


def exchanged(own):
    own = own.reshape(-1, own.shape[-1])
    (other,) = yield [shifted(own, "h", 1)]
    return (own, other)


def gather_half(part):
    whole = yield from gather_deep(part)
    whole = yield from gather_flat(whole, 1)
    return (yield from exchanged(whole))


def gather_table(part):
    others = yield sent_around(part, "m")
    part = placed(part, others, "m", 0)
    others = yield sent_around(part, "h")
    return placed(part, others, "h", 1).reshape(-1, part.shape[-1])


def by_owner(array, block):
    seen = array.reshape(array.shape[0], -1, 2, block)
    half = lax.axis_index("h")
    return [at(seen, which, 2).reshape(array.shape[0], -1) for which in (half, 1 - half)]


def gather_columns(part, block):
    mine, other = by_owner(part, block)
    (other,) = yield [shifted(other, "h", 1)]
    pair = placed(mine, [other], "h", 0)
    result = yield from gather_half(pair.reshape(-1, mine.shape[1]))
    return result


def pieces_of(total, dim, axis):
    n = lax.axis_size(axis)
    mine = lax.axis_index(axis)
    return [
        shifted(at(total, (mine + shift) % n, dim), axis, n - shift) for shift in range(1, n)
    ]


def added(total, dim, axis, pieces):
    total = at(total, lax.axis_index(axis), dim).astype(WIDE)
    for piece in pieces:
        total = total + piece.astype(WIDE)
    return total


def reduce_rows(other, own, names, order, parts=1):
    (arrived,) = yield [shifted(other, "h", 1)]
    total = (own() + arrived.astype(WIDE)).astype(LOW)
    names = list(names)
    total = total.reshape(
        tuple(lax.axis_size(name) for name in names) + (-1, total.shape[-1])
    )
    totals = jnp.split(total, parts, axis=-1)
    orders = [list(order), [order[1], order[0]] + list(order[2:])][:parts]
    left = [list(names) for _ in totals]
    for step in range(2):
        dims = [names.index(axes[step]) for names, axes in zip(left, orders)]
        steps = list(zip(totals, dims, [axes[step] for axes in orders]))
        pieces = yield [pieces_of(*each) for each in steps]
        totals = [added(*each, arrived).astype(LOW) for each, arrived in zip(steps, pieces)]
        for names, dim in zip(left, dims):
            names.pop(dim)
    total = totals[0] if parts == 1 else jnp.concatenate(totals, axis=-1)
    dim = left[0].index(order[2])
    pieces = yield pieces_of(total, dim, order[2])
    return added(total, dim, order[2], pieces)


def squares(total):
    total = total.reshape(-1, total.shape[-1] // LANES, LANES)
    return jnp.sum(total * total, axis=(0, 1))


def swap_rows(total, square=None):
    seen = total.reshape(2, -1, total.shape[-1])
    half = lax.axis_index("h")
    flight = [shifted(at(seen, 1 - half, 0), "h", 1)]
    (other,) = yield flight if square is None else Squared(square, flight)
    return (at(seen, half, 0), other)


def in_order(mine, other, dim):
    first = lax.axis_index("h") == 0
    return jnp.concatenate(
        [jnp.where(first, mine, other), jnp.where(first, other, mine)], axis=dim
    )


def reduce_layer(other, own, order, block=None, parts=1):
    total = yield from reduce_rows(other, own, ("z", "r", "m"), order, parts)
    total = total.reshape(-1, total.shape[-1])
    mine, other = yield from swap_rows(total, squares(total))
    if block is None:
        return in_order(mine, other, 1)
    rows = mine.shape[0]
    mine, other = (half.reshape(rows, -1, 1, block) for half in (mine, other))
    return in_order(mine, other, 2).reshape(rows, -1)


def reduce_owned(other, own, order, parts):
    total = yield from reduce_rows(other, own, ("z", "r", "m"), order, parts)
    total = total.reshape(-1, total.shape[-1])
    yield Squared(squares(total), [])
    return total


def reduce_table(other, own):
    total = yield from reduce_rows(other, own, ("m", "h", "r", "z"), ("m", "r", "z"))
    square = squares(total)
    total = total.astype(LOW)
    others = yield Squared(square, sent_around(total, "z"))
    total = placed(total, others, "z", 1)
    others = yield sent_around(total, "r")
    total = placed(total, others, "r", 1)
    mine, other = yield from swap_rows(total.reshape(-1, total.shape[-1]))
    return in_order(mine, other, 1).astype(WIDE)


def sum_over(part, axes):
    for axis in axes:
        n = lax.axis_size(axis)
        if n == 4:
            others = yield sent_around(part, axis)
            part = jnp.sum(placed(part, others, axis, 0), axis=0)
            continue
        shift = n // 2
        while shift:
            (other,) = yield [shifted(part, axis, shift)]
            part = part + other
            shift //= 2
    return part


def norm_forward(values, gain):
    return values * lax.rsqrt(jnp.mean(values * values, axis=-1, keepdims=True) + EPS) * gain


def norm_backward(values, gain, upstream):
    factor = lax.rsqrt(jnp.mean(values * values, axis=-1, keepdims=True) + EPS)
    scaled = upstream * gain
    inward = factor * scaled - values * factor**3 * jnp.mean(
        scaled * values, axis=-1, keepdims=True
    )
    gain_grad = jnp.sum(upstream * values * factor, axis=0)
    return (inward, gain_grad)


def dot_nt(left, right):
    return lax.dot_general(left, right, (((1,), (1,)), ((), ())), preferred_element_type=WIDE)


def dot_tn(left, right):
    return lax.dot_general(left, right, (((0,), (0,)), ((), ())), preferred_element_type=WIDE)


def dot_nn(left, right):
    return jnp.dot(left, right, preferred_element_type=WIDE)


def allowed_pairs(kind, scalar, count):
    row = lax.broadcasted_iota(jnp.int32, (count, count), 0)
    col = lax.broadcasted_iota(jnp.int32, (count, count), 1)
    if kind == "space":
        return (scalar == 0) | (row // SMALL_TOKENS == col // SMALL_TOKENS)
    lanes = count // FRAMES
    own = FRAMES // 2
    row_frame, col_frame = row // lanes, col // lanes
    row_at = row_frame + jnp.where(scalar == 0, 0, jnp.where(row_frame < own, own, -own))
    col_at = col_frame + jnp.where(scalar == 0, 0, jnp.where(col_frame < own, own, -own))
    return (row % lanes == col % lanes) & (col_at <= row_at)


def softmax_rows(query, key, allowed):
    scores = jnp.where(allowed, dot_nt(query, key) * HEAD ** (-0.5), NEG)
    expd = jnp.exp(scores - jnp.max(scores, axis=-1, keepdims=True))
    return expd / jnp.sum(expd, axis=-1, keepdims=True)


def block_of(ref, start, kind):
    if kind == "space":
        return ref[:, pl.ds(start, LANES)]
    part = ref[:, :, pl.ds(start, LANES)]
    return part.reshape(-1, LANES)


def store_to(ref, start, kind, value):
    if kind == "space":
        ref[:, pl.ds(start, LANES)] = value
    else:
        ref[:, :, pl.ds(start, LANES)] = value.reshape(FRAMES, -1, LANES)


def forward_body(kind, scalar_ref, packed_ref, mixed_ref):
    allowed = allowed_pairs(kind, scalar_ref[0], GROUP)
    first = lax.broadcasted_iota(jnp.int32, (GROUP, LANES), 1) < HEAD

    def turn(pair, _):
        start = pl.multiple_of(pair * LANES, LANES)
        query = block_of(packed_ref, start, kind)
        key = block_of(packed_ref, pl.multiple_of(D + start, LANES), kind)
        value = block_of(packed_ref, pl.multiple_of(2 * D + start, LANES), kind)
        zero = jnp.zeros_like(query)
        one = dot_nn(softmax_rows(jnp.where(first, query, zero), key, allowed).astype(LOW), value)
        two = dot_nn(softmax_rows(jnp.where(first, zero, query), key, allowed).astype(LOW), value)
        store_to(mixed_ref, start, kind, jnp.where(first, one, two).astype(LOW))
        return 0

    lax.fori_loop(0, D // LANES, turn, 0, unroll=4)


def backward_body(kind, scalar_ref, packed_ref, up_ref, out_ref):
    allowed = allowed_pairs(kind, scalar_ref[0], GROUP)
    first = lax.broadcasted_iota(jnp.int32, (GROUP, LANES), 1) < HEAD

    def turn(pair, _):
        start = pl.multiple_of(pair * LANES, LANES)
        key_at = pl.multiple_of(D + start, LANES)
        value_at = pl.multiple_of(2 * D + start, LANES)
        query = block_of(packed_ref, start, kind)
        key = block_of(packed_ref, key_at, kind)
        value = block_of(packed_ref, value_at, kind)
        up = block_of(up_ref, start, kind)
        zero = jnp.zeros_like(query)
        grads = []
        for mine in (first, ~first):
            probs = softmax_rows(jnp.where(mine, query, zero), key, allowed)
            inner = dot_nt(jnp.where(mine, up, zero), value)
            total = jnp.sum(probs * inner, axis=-1, keepdims=True)
            scores = (probs * (inner - total) * HEAD ** (-0.5)).astype(LOW)
            grads.append((dot_nn(scores, key), dot_tn(scores, query), dot_tn(probs.astype(LOW), up)))
        for place, one, two in zip((start, key_at, value_at), *grads):
            store_to(out_ref, place, kind, jnp.where(first, one, two).astype(LOW))
        return 0

    lax.fori_loop(0, D // LANES, turn, 0, unroll=2)


def attention(kind, scalar, packed, up=None):
    shape = packed.shape[:-1]
    if kind == "space":
        grid, block, where = (shape[0] // GROUP,), (GROUP,), lambda g, s: (g, 0)
    else:
        grid, block, where = (FRAMES * shape[1] // GROUP,), (FRAMES, GROUP // FRAMES), lambda g, s: (0, g, 0)
    wide = pl.BlockSpec(block + (3 * D,), where)
    narrow = pl.BlockSpec(block + (D,), where)
    body, last, ins, flops = forward_body, D, (packed,), 9e9
    if up is not None:
        body, last, flops = backward_body, 3 * D, 22e9
        ins = (packed, up.reshape(shape + (D,)))
    return pl.pallas_call(
        functools.partial(body, kind),
        out_shape=jax.ShapeDtypeStruct(shape + (last,), LOW),
        grid_spec=pltpu.PrefetchScalarGridSpec(
            num_scalar_prefetch=1,
            grid=grid,
            in_specs=[wide, narrow][: len(ins)],
            out_specs=narrow if up is None else wide,
        ),
        cost_estimate=pl.CostEstimate(
            flops=int(flops), transcendentals=4 * HEADS * GROUP * GROUP, bytes_accessed=8 << 20
        ),
    )(scalar.reshape(1).astype(jnp.int32), *ins)


def adamw(weight, grad, first, second, rate, decay):
    first_new = BETA_ONE * first + (1.0 - BETA_ONE) * grad
    second_new = BETA_TWO * second + (1.0 - BETA_TWO) * grad * grad
    unbiased_first = first_new / (1.0 - BETA_ONE**STEP)
    unbiased_second = second_new / (1.0 - BETA_TWO**STEP)
    updated = weight - rate * (
        unbiased_first / (jnp.sqrt(unbiased_second) + ADAM_EPS) + decay * weight
    )
    return (updated, first_new, second_new)


def gelu(values):
    return jax.nn.gelu(values, approximate=True)


def gelu_backward(values, upstream):
    return jax.vjp(gelu, values)[1](upstream)[0]


def swap_slots(values):
    mine, other = halves(values, 1)
    return jnp.concatenate([mine, shifted(other, "h", 1)], axis=0)


def swap_frames(values):
    half = lax.axis_index("h")
    mine, other = jnp.split(values, 2, axis=0)
    other = shifted(other, "h", 1)
    return jnp.where(
        half == 0,
        jnp.concatenate([mine, other], axis=1),
        jnp.concatenate([other, mine], axis=1),
    )


def on_device(
    tokens,
    masked,
    small_grid,
    domains,
    attend_in,
    attend_out,
    expand,
    contract,
    gains,
    tables,
    mean_in,
    mean_out,
    mean_expand,
    mean_contract,
    mean_gains,
    mean_tables,
    square_in,
    square_out,
    square_expand,
    square_contract,
    square_gains,
    square_tables,
):
    micro = lax.axis_index("m")
    half = lax.axis_index("h")
    frames = FRAMES // lax.axis_size("h")
    block = contract.shape[0]
    kinds = gains.shape[0]

    def of_micro(array):
        return at(array[:, 0], micro, 0)

    codes = of_micro(tokens)
    hidden_mask = of_micro(masked).astype(WIDE)
    small = of_micro(small_grid)
    doms = of_micro(domains)

    turned = jnp.pad(gains.T, ((0, 0), (0, LANES - kinds)))
    layers = [attend_in[0], attend_out[0], turned, attend_in[1], attend_out[1]]
    ends = [0]
    for array in layers:
        ends.append(ends[-1] + array.shape[1])
    gathered = jnp.concatenate(layers, axis=1).astype(LOW)
    gathered = lax.all_gather(gathered, ALL, axis=0, tiled=True)
    low_in, low_out = tables.astype(LOW)
    up_job = Job(gather_columns(expand.astype(LOW), block))
    down_job = Job(gather_half(contract.astype(LOW)))
    in_table_job = Job(gather_table(low_in))
    token = advance(jnp.zeros((), WIDE), up_job, down_job)
    token = advance(token, in_table_job, up_job, down_job)
    token = advance(token, in_table_job, up_job)
    table_in = in_table_job.finish()
    code_ids = jnp.arange(table_in.shape[0])

    def own_frames(array):
        return lax.dynamic_slice_in_dim(array, half * frames, frames, 0)

    space_codes = own_frames(codes).reshape(-1)
    picked = dot_nn((space_codes[:, None] == code_ids[None, :]).astype(LOW), table_in)
    token = advance(token, down_job, up_job)
    out_table_job = Job(gather_table(low_out))
    token = advance(token, down_job, up_job)
    picked, token = lax.optimization_barrier((picked, token))
    gathered = advance(gathered, out_table_job)
    first_in, first_out, turned, next_in, next_out = (
        gathered[:, start:end] for start, end in zip(ends, ends[1:])
    )
    w_in, w_out = (first_in, next_in), (first_out, next_out)
    gain_all = turned.T[:kinds].astype(WIDE)

    slot_ids = jnp.arange(SLOTS)
    segment = jnp.where(small > 0, slot_ids // SMALL_TOKENS, 0)
    dom_slot = jnp.sum((segment[:, None] == jnp.arange(CLIPS)[None, :]) * doms[None, :], axis=-1)
    domain_hot = (dom_slot[:, None] == jnp.arange(DOMAINS)[None, :]).astype(WIDE)
    counts = jnp.sum(jnp.sum(hidden_mask, axis=0)[:, None] * domain_hot, axis=0)[None, :]
    counts = Job(sum_over(counts, ("r", "z"))).finish()[0]
    scale = 1.0 / (MICRO * DOMAINS * jnp.maximum(counts, 1.0))
    slot_scale = jnp.sum(domain_hot * scale[None, :], axis=1)

    def time_order(array):
        mine = halves(array, 1)[0]
        return jnp.concatenate(halves(mine, 0), axis=0).reshape(-1)

    space_mask = own_frames(hidden_mask).reshape(-1)
    time_codes = time_order(codes)
    time_weight = time_order(hidden_mask * slot_scale[None, :])

    start = jnp.where(space_mask[:, None] > 0, gain_all[4], picked)
    normed_space = norm_forward(start, gain_all[0]).astype(LOW)
    packed_space = dot_nn(normed_space, w_in[0]).astype(LOW)
    mixed_space = attention("space", small, packed_space)
    after_space = start + dot_nn(mixed_space, w_out[0])
    after_space = swap_slots(after_space.reshape(frames, SLOTS, D)).reshape(-1, D)
    normed_time = norm_forward(after_space, gain_all[1]).astype(LOW)
    normed_time = advance(normed_time, out_table_job)
    table_out = out_table_job.finish()
    packed_time = dot_nn(normed_time, w_in[1]).astype(LOW).reshape(FRAMES, -1, 3 * D)
    mixed_time = attention("time", half, packed_time).reshape(-1, D)
    after_time = after_space + dot_nn(mixed_time, w_out[1])
    normed_ffn = norm_forward(after_time, gain_all[2]).astype(LOW)
    ups, downs = up_job.finish(), down_job.finish()
    pres = [dot_nn(normed_ffn, up) for up in ups]
    activs = [gelu(pre).astype(LOW) for pre in pres]
    after_ffn = after_time + dot_nn(activs[0], downs[0]) + dot_nn(activs[1], downs[1])
    final = norm_forward(after_ffn, gain_all[3]).astype(LOW)
    logits = dot_nt(final, table_out)
    hits = time_codes[:, None] == code_ids[None, :]
    top = jnp.max(logits, axis=1, keepdims=True)
    log_total = top + jnp.log(jnp.sum(jnp.exp(logits - top), axis=1, keepdims=True))
    target = jnp.sum(jnp.where(hits, logits, 0.0), axis=1)
    loss_part = jnp.sum(time_weight * (log_total[:, 0] - target))
    grad_logits = (time_weight[:, None] * (jnp.exp(logits - log_total) - hits)).astype(LOW)

    def product(make, left, mine, other, *rest):
        return Job(make(dot_tn(left, other).astype(LOW), lambda: dot_tn(left, mine), *rest))

    head_job = product(reduce_table, grad_logits, *halves(final, 1))
    grad_final = dot_nn(grad_logits, table_out)
    grad_ffn, gain_three = norm_backward(after_ffn, gain_all[3], grad_final)
    up_low = grad_ffn.astype(LOW)
    contract_job = Job(
        reduce_owned(
            dot_tn(activs[1], up_low).astype(LOW),
            lambda: dot_tn(activs[0], up_low),
            ("m", "r", "z"),
            2,
        )
    )
    grad_activs = [dot_nt(up_low, down) for down in downs]
    grad_pres = [gelu_backward(pre, grad).astype(LOW) for pre, grad in zip(pres, grad_activs)]
    grad_pres = advance(grad_pres, head_job, contract_job)
    expand_job = product(
        reduce_layer, normed_ffn, grad_pres[0], grad_pres[1], ("r", "m", "z"), block, 2
    )
    grad_normed = dot_nt(grad_pres[0], ups[0]) + dot_nt(grad_pres[1], ups[1])
    inward, gain_two = norm_backward(after_time, gain_all[2], grad_normed)
    grad_time = grad_ffn + inward
    up_low = grad_time.astype(LOW)
    up_low = advance(up_low, head_job, expand_job)
    out_job = product(reduce_layer, mixed_time, *halves(up_low, 1), ("m", "r", "z"))
    grad_mixed = dot_nt(up_low, w_out[1]).astype(LOW)
    grad_packed = attention("time", half, packed_time, grad_mixed).reshape(-1, 3 * D)
    grad_packed = advance(grad_packed, head_job, contract_job, out_job)
    in_job = product(
        reduce_layer, normed_time, *halves(grad_packed, 1), ("m", "r", "z"), None, 2
    )
    grad_normed = dot_nt(grad_packed, w_in[1])
    inward, gain_one = norm_backward(after_space, gain_all[1], grad_normed)
    grad_space = swap_frames((grad_time + inward).reshape(FRAMES, -1, D)).reshape(-1, D)
    up_low = grad_space.astype(LOW)
    up_low = advance(up_low, head_job, contract_job, in_job)
    first_out_job = product(reduce_layer, mixed_space, *halves(up_low, 1), ("r", "m", "z"))
    grad_mixed = dot_nt(up_low, w_out[0]).astype(LOW)
    grad_mixed = advance(grad_mixed, contract_job, expand_job, out_job, first_out_job)
    grad_packed = attention("space", small, packed_space, grad_mixed)
    grad_packed = advance(
        grad_packed, head_job, expand_job, out_job, in_job
    )
    first_in_job = product(
        reduce_layer, normed_space, *halves(grad_packed, 1), ("r", "m", "z"), None, 2
    )
    grad_normed = dot_nt(grad_packed, w_in[0])
    grad_normed = advance(grad_normed, first_in_job, head_job, out_job, in_job, first_out_job)
    inward, gain_zero = norm_backward(start, gain_all[0], grad_normed)
    grad_start = grad_space + inward
    mask_grad = jnp.sum(grad_start * space_mask[:, None], axis=0)
    chosen = (jnp.where(space_mask > 0, -1, space_codes)[:, None] == code_ids[None, :]).astype(LOW)
    start_low = grad_start.astype(LOW)
    embed_job = product(reduce_table, chosen, *halves(start_low, 1))

    gain_grads = jnp.stack([gain_zero, gain_one, gain_two, gain_three, mask_grad])
    gain_job = Job(sum_over(gain_grads, ("h", "m", "r", "z")))
    token = jnp.zeros((), WIDE)
    token = advance(token, embed_job, gain_job, head_job, out_job, expand_job, first_out_job)
    token = advance(token, first_in_job)
    token = advance(token, embed_job, gain_job, in_job, first_out_job)
    token = advance(token, first_in_job)
    token = advance(token, embed_job, gain_job, expand_job, in_job, first_out_job)
    token = advance(token, first_in_job, embed_job, gain_job, first_out_job)

    owner = jnp.int32(0)
    for axis in ALL:
        owner = owner * lax.axis_size(axis) + lax.axis_index(axis)
    width = gains.shape[1]
    gain_grads = lax.dynamic_slice_in_dim(gain_job.finish(), owner * width, width, 1)
    jobs = (in_job, first_in_job, out_job, first_out_job, expand_job, contract_job)
    jobs = jobs + (embed_job, head_job)
    lane = jnp.arange(LANES)
    small_square = jnp.pad(jnp.sum(gain_grads * gain_grads, axis=0), (0, LANES - width))
    owned = sum(job.square for job in jobs) + small_square
    sums = jnp.stack([owned, jnp.where(lane == 0, loss_part, 0.0)])
    norm_job = Job(sum_over(sums, ("h", "m", "r", "z")))
    while norm_job.flight is not None:
        token = advance(token, norm_job, *jobs)
    results = [(job.finish(), None) for job in jobs]
    square_sum, loss = jnp.sum(norm_job.result, axis=1)
    norm = jnp.sqrt(square_sum)
    factor = jnp.minimum(1.0, CLIP / (norm + 1e-06))

    made = [grad for grad, _ in results]
    grads = (
        jnp.stack([made[1], made[0]]),
        jnp.stack([made[3], made[2]]),
        made[4],
        made[5],
        gain_grads,
        jnp.stack([made[6], made[7]]),
    )
    params = (attend_in, attend_out, expand, contract, gains, tables)
    firsts = (mean_in, mean_out, mean_expand, mean_contract, mean_gains, mean_tables)
    seconds = (square_in, square_out, square_expand, square_contract, square_gains, square_tables)
    rates = (RATE, RATE, RATE, RATE, RATE_SMALL, RATE)
    decays = (DECAY, DECAY, DECAY, DECAY, 0.0, DECAY)
    results = [
        adamw(p, factor * g, f, s, r, k)
        for p, g, f, s, r, k in zip(params, grads, firsts, seconds, rates, decays)
    ]
    return (loss, norm) + tuple(result[k] for k in range(3) for result in results)


def solution(mesh):
    dp, code = mesh.shape["dp"], mesh.shape["code"]
    deep = next(n for n in (4, 2, 1) if dp % n == 0)
    fine = Mesh(mesh.devices.reshape(deep, dp // deep, MICRO, code // MICRO), ALL)
    group = ("z", "r")
    weights = (
        P(None, ALL, None),
        P(None, ALL, None),
        P(ALL, None),
        P(ALL, None),
        P(None, ALL),
        P(None, ("m", "h"), None),
    )
    return jax.shard_map(
        on_device,
        mesh=fine,
        in_specs=(
            P(None, group, None, None),
            P(None, group, None, None),
            P(None, group),
            P(None, group, None),
        )
        + weights * 3,
        out_specs=(P(), P()) + weights * 3,
        check_vma=False,
    )
```

```python
import functools
from typing import NamedTuple

import jax
import jax.numpy as jnp
from jax import lax
from jax.experimental import pallas as pl
from jax.experimental.pallas import tpu as pltpu
from jax.sharding import Mesh, PartitionSpec as P

D = 1024
HEADS = 16
HEAD = 64
FRAMES = 4
SLOTS = 256
SMALL_TOKENS = 64
CLIPS = 4
DOMAINS = 4
MICRO = 2
STEP = 10


EPS = 1e-05
NEG = -1e30
BETA_ONE = 0.9
BETA_TWO = 0.95
ADAM_EPS = 1e-08
DECAY = 0.1
RATE = 0.02
RATE_SMALL = 0.2
CLIP = 0.005
LOW = jnp.bfloat16
WIDE = jnp.float32
ALL = ("z", "r", "m", "h")
GROUP = 256
LANES = 128


def shifted(part, axis, shift):
    n = lax.axis_size(axis)
    return lax.ppermute(part, axis, [((i + shift) % n, i) for i in range(n)])


def at(array, index, dim):
    return lax.dynamic_index_in_dim(array, index, dim, keepdims=False)


def sent_around(part, axis):
    return [shifted(part, axis, shift) for shift in range(1, lax.axis_size(axis))]


def placed(part, others, axis, dim):
    n = lax.axis_size(axis)
    mine = lax.axis_index(axis)
    whole = jnp.broadcast_to(
        jnp.expand_dims(part, dim), part.shape[:dim] + (n,) + part.shape[dim:]
    )
    for shift, other in zip(range(1, n), others):
        whole = lax.dynamic_update_index_in_dim(whole, other, (mine + shift) % n, dim)
    return whole


def gather_axis(part, axis, dim):
    return placed(part, sent_around(part, axis), axis, dim)


def halves(array, dim):
    size = array.shape[dim] // lax.axis_size("h")
    half = lax.axis_index("h")
    return [
        lax.dynamic_slice_in_dim(array, start * size, size, dim) for start in (half, 1 - half)
    ]


class Squared(NamedTuple):
    square: jax.Array
    flight: list


class Job:
    def __init__(self, steps):
        self.steps = steps
        self.result = self.square = None
        self.flight = next(steps)

    def resume(self, arrived):
        try:
            self.flight = self.steps.send(arrived)
        except StopIteration as stop:
            self.flight, self.result = None, stop.value
        if isinstance(self.flight, Squared):
            self.square, self.flight = self.flight

    def finish(self):
        while self.flight is not None:
            self.resume(self.flight)
        return self.result


def advance(value, *jobs):
    jobs = [job for job in jobs if job.flight is not None]
    value, flights = lax.optimization_barrier((value, [job.flight for job in jobs]))
    for job, flight in zip(jobs, flights):
        job.resume(flight)
    return value


def split_columns(array):
    cut = array.shape[-1] // (2 * LANES) * LANES
    return array[..., :cut], array[..., cut:]


def gather_deep(part):
    if lax.axis_size("z") != 4:
        others = yield sent_around(part, "z")
        return placed(part, others, "z", 0)
    above, below = yield [shifted(part, "z", 1), shifted(part, "z", 3)]
    first, second = split_columns(above)[0], split_columns(below)[1]
    first, second = yield [shifted(first, "z", 1), shifted(second, "z", 3)]
    mine = lax.axis_index("z")
    whole = jnp.broadcast_to(part[None], (4,) + part.shape)
    whole = lax.dynamic_update_index_in_dim(whole, above, (mine + 1) % 4, 0)
    whole = lax.dynamic_update_index_in_dim(whole, below, (mine + 3) % 4, 0)
    zero = jnp.int32(0)
    place = [(mine + 2) % 4] + [zero] * part.ndim
    whole = lax.dynamic_update_slice(whole, first[None], place)
    place[-1] = jnp.int32(first.shape[-1])
    return lax.dynamic_update_slice(whole, second[None], place)


def gather_flat(part, dim):
    first, second = split_columns(part)
    one, two = yield (sent_around(first, "m"), sent_around(second, "r"))
    first, second = placed(first, one, "m", dim), placed(second, two, "r", dim)
    one, two = yield (sent_around(first, "r"), sent_around(second, "m"))
    first, second = placed(first, one, "r", dim), placed(second, two, "m", dim + 1)
    return jnp.concatenate([first, second], axis=-1)


def exchanged(own):
    own = own.reshape(-1, own.shape[-1])
    (other,) = yield [shifted(own, "h", 1)]
    return (own, other)


def gather_half(part):
    whole = yield from gather_deep(part)
    whole = yield from gather_flat(whole, 1)
    return (yield from exchanged(whole))


def gather_table(part):
    others = yield sent_around(part, "m")
    part = placed(part, others, "m", 0)
    others = yield sent_around(part, "h")
    return placed(part, others, "h", 1).reshape(-1, part.shape[-1])


def by_owner(array, block):
    seen = array.reshape(array.shape[0], -1, 2, block)
    half = lax.axis_index("h")
    return [at(seen, which, 2).reshape(array.shape[0], -1) for which in (half, 1 - half)]


def gather_columns(part, block):
    mine, other = by_owner(part, block)
    (other,) = yield [shifted(other, "h", 1)]
    pair = placed(mine, [other], "h", 0)
    result = yield from gather_half(pair.reshape(-1, mine.shape[1]))
    return result


def pieces_of(total, dim, axis):
    n = lax.axis_size(axis)
    mine = lax.axis_index(axis)
    return [
        shifted(at(total, (mine + shift) % n, dim), axis, n - shift) for shift in range(1, n)
    ]


def added(total, dim, axis, pieces):
    total = at(total, lax.axis_index(axis), dim).astype(WIDE)
    for piece in pieces:
        total = total + piece.astype(WIDE)
    return total


def reduce_rows(other, own, names, order, parts=1):
    (arrived,) = yield [shifted(other, "h", 1)]
    total = (own() + arrived.astype(WIDE)).astype(LOW)
    names = list(names)
    total = total.reshape(
        tuple(lax.axis_size(name) for name in names) + (-1, total.shape[-1])
    )
    totals = jnp.split(total, parts, axis=-1)
    orders = [list(order), [order[1], order[0]] + list(order[2:])][:parts]
    left = [list(names) for _ in totals]
    for step in range(2):
        dims = [names.index(axes[step]) for names, axes in zip(left, orders)]
        steps = list(zip(totals, dims, [axes[step] for axes in orders]))
        pieces = yield [pieces_of(*each) for each in steps]
        totals = [added(*each, arrived).astype(LOW) for each, arrived in zip(steps, pieces)]
        for names, dim in zip(left, dims):
            names.pop(dim)
    total = totals[0] if parts == 1 else jnp.concatenate(totals, axis=-1)
    dim = left[0].index(order[2])
    pieces = yield pieces_of(total, dim, order[2])
    return added(total, dim, order[2], pieces)


def squares(total):
    total = total.reshape(-1, total.shape[-1] // LANES, LANES)
    return jnp.sum(total * total, axis=(0, 1))


def swap_rows(total, square=None):
    seen = total.reshape(2, -1, total.shape[-1])
    half = lax.axis_index("h")
    flight = [shifted(at(seen, 1 - half, 0), "h", 1)]
    (other,) = yield flight if square is None else Squared(square, flight)
    return (at(seen, half, 0), other)


def in_order(mine, other, dim):
    first = lax.axis_index("h") == 0
    return jnp.concatenate(
        [jnp.where(first, mine, other), jnp.where(first, other, mine)], axis=dim
    )


def reduce_layer(other, own, order, block=None, parts=1):
    total = yield from reduce_rows(other, own, ("z", "r", "m"), order, parts)
    total = total.reshape(-1, total.shape[-1])
    mine, other = yield from swap_rows(total, squares(total))
    if block is None:
        return in_order(mine, other, 1)
    rows = mine.shape[0]
    mine, other = (half.reshape(rows, -1, 1, block) for half in (mine, other))
    return in_order(mine, other, 2).reshape(rows, -1)


def reduce_owned(other, own, order, parts):
    total = yield from reduce_rows(other, own, ("z", "r", "m"), order, parts)
    total = total.reshape(-1, total.shape[-1])
    yield Squared(squares(total), [])
    return total


def reduce_table(other, own):
    total = yield from reduce_rows(other, own, ("m", "h", "r", "z"), ("m", "r", "z"))
    square = squares(total)
    total = total.astype(LOW)
    others = yield Squared(square, sent_around(total, "z"))
    total = placed(total, others, "z", 1)
    others = yield sent_around(total, "r")
    total = placed(total, others, "r", 1)
    mine, other = yield from swap_rows(total.reshape(-1, total.shape[-1]))
    return in_order(mine, other, 1).astype(WIDE)


def sum_table(other, own):
    (arrived,) = yield [shifted(other, "h", 1)]
    total = (own() + arrived.astype(WIDE)).astype(LOW)
    total = total.reshape(lax.axis_size("m"), -1, total.shape[-1])
    pieces = yield pieces_of(total, 0, "m")
    total = added(total, 0, "m", pieces).astype(LOW)
    for axis in ("r", "z"):
        shift = lax.axis_size(axis) // 2
        while shift:
            (other,) = yield [shifted(total, axis, shift)]
            total = (total.astype(WIDE) + other.astype(WIDE)).astype(LOW)
            shift //= 2
    square = squares(total.astype(WIDE)) / (lax.axis_size("r") * lax.axis_size("z"))
    mine, other = yield from swap_rows(total, square)
    return in_order(mine, other, 1).astype(WIDE)


def sum_over(part, axes):
    for axis in axes:
        n = lax.axis_size(axis)
        if n == 4:
            others = yield sent_around(part, axis)
            part = jnp.sum(placed(part, others, axis, 0), axis=0)
            continue
        shift = n // 2
        while shift:
            (other,) = yield [shifted(part, axis, shift)]
            part = part + other
            shift //= 2
    return part


def norm_forward(values, gain):
    return values * lax.rsqrt(jnp.mean(values * values, axis=-1, keepdims=True) + EPS) * gain


def norm_backward(values, gain, upstream):
    factor = lax.rsqrt(jnp.mean(values * values, axis=-1, keepdims=True) + EPS)
    scaled = upstream * gain
    inward = factor * scaled - values * factor**3 * jnp.mean(
        scaled * values, axis=-1, keepdims=True
    )
    gain_grad = jnp.sum(upstream * values * factor, axis=0)
    return (inward, gain_grad)


def dot_nt(left, right):
    return lax.dot_general(left, right, (((1,), (1,)), ((), ())), preferred_element_type=WIDE)


def dot_tn(left, right):
    return lax.dot_general(left, right, (((0,), (0,)), ((), ())), preferred_element_type=WIDE)


def dot_nn(left, right):
    return jnp.dot(left, right, preferred_element_type=WIDE)


def allowed_pairs(kind, scalar, count, query_dim=0):
    row = lax.broadcasted_iota(jnp.int32, (count, count), query_dim)
    col = lax.broadcasted_iota(jnp.int32, (count, count), 1 - query_dim)
    if kind == "space":
        return (scalar == 0) | (row // SMALL_TOKENS == col // SMALL_TOKENS)
    lanes = count // FRAMES
    own = FRAMES // 2
    row_frame, col_frame = row // lanes, col // lanes
    row_at = row_frame + jnp.where(scalar == 0, 0, jnp.where(row_frame < own, own, -own))
    col_at = col_frame + jnp.where(scalar == 0, 0, jnp.where(col_frame < own, own, -own))
    return (row % lanes == col % lanes) & (col_at <= row_at)


def softmax_rows(query, key, allowed):
    scores = jnp.where(allowed, dot_nt(query, key) * HEAD ** (-0.5), NEG)
    expd = jnp.exp(scores - jnp.max(scores, axis=-1, keepdims=True))
    return expd / jnp.sum(expd, axis=-1, keepdims=True)


def block_of(ref, start, kind):
    if kind == "space":
        return ref[:, pl.ds(start, LANES)]
    part = ref[:, :, pl.ds(start, LANES)]
    return part.reshape(-1, LANES)


def store_to(ref, start, kind, value):
    if kind == "space":
        ref[:, pl.ds(start, LANES)] = value
    else:
        ref[:, :, pl.ds(start, LANES)] = value.reshape(FRAMES, -1, LANES)


def forward_body(kind, scalar_ref, packed_ref, mixed_ref):
    allowed = allowed_pairs(kind, scalar_ref[0], GROUP)
    first = lax.broadcasted_iota(jnp.int32, (GROUP, LANES), 1) < HEAD

    def turn(pair, _):
        start = pl.multiple_of(pair * LANES, LANES)
        query = block_of(packed_ref, start, kind)
        key = block_of(packed_ref, pl.multiple_of(D + start, LANES), kind)
        value = block_of(packed_ref, pl.multiple_of(2 * D + start, LANES), kind)
        zero = jnp.zeros_like(query)
        one = dot_nn(softmax_rows(jnp.where(first, query, zero), key, allowed).astype(LOW), value)
        two = dot_nn(softmax_rows(jnp.where(first, zero, query), key, allowed).astype(LOW), value)
        store_to(mixed_ref, start, kind, jnp.where(first, one, two).astype(LOW))
        return 0

    lax.fori_loop(0, D // LANES, turn, 0, unroll=4)


def backward_body(kind, scalar_ref, packed_ref, up_ref, out_ref):
    allowed = allowed_pairs(kind, scalar_ref[0], GROUP, 1)
    first = lax.broadcasted_iota(jnp.int32, (GROUP, LANES), 1) < HEAD

    def turn(pair, _):
        start = pl.multiple_of(pair * LANES, LANES)
        key_at = pl.multiple_of(D + start, LANES)
        value_at = pl.multiple_of(2 * D + start, LANES)
        query = block_of(packed_ref, start, kind)
        key = block_of(packed_ref, key_at, kind)
        value = block_of(packed_ref, value_at, kind)
        up = block_of(up_ref, start, kind)
        zero = jnp.zeros_like(query)
        grads = []
        for mine in (first, ~first):
            scores = dot_nt(key, jnp.where(mine, query, zero)) * HEAD ** (-0.5)
            scores = jnp.where(allowed, scores, NEG)
            expd = jnp.exp(scores - jnp.max(scores, axis=0, keepdims=True))
            probs = expd / jnp.sum(expd, axis=0, keepdims=True)
            inner = dot_nt(value, jnp.where(mine, up, zero))
            total = jnp.sum(probs * inner, axis=0, keepdims=True)
            scores = (probs * (inner - total) * HEAD ** (-0.5)).astype(LOW)
            grads.append((dot_tn(scores, key), dot_nn(scores, query), dot_nn(probs.astype(LOW), up)))
        for place, one, two in zip((start, key_at, value_at), *grads):
            store_to(out_ref, place, kind, jnp.where(first, one, two).astype(LOW))
        return 0

    lax.fori_loop(0, D // LANES, turn, 0, unroll=2)


def attention(kind, scalar, packed, up=None):
    shape = packed.shape[:-1]
    if kind == "space":
        grid, block, where = (shape[0] // GROUP,), (GROUP,), lambda g, s: (g, 0)
    else:
        grid, block, where = (FRAMES * shape[1] // GROUP,), (FRAMES, GROUP // FRAMES), lambda g, s: (0, g, 0)
    wide = pl.BlockSpec(block + (3 * D,), where)
    narrow = pl.BlockSpec(block + (D,), where)
    body, last, ins, flops = forward_body, D, (packed,), 9e9
    if up is not None:
        body, last, flops = backward_body, 3 * D, 22e9
        ins = (packed, up.reshape(shape + (D,)))
    return pl.pallas_call(
        functools.partial(body, kind),
        out_shape=jax.ShapeDtypeStruct(shape + (last,), LOW),
        grid_spec=pltpu.PrefetchScalarGridSpec(
            num_scalar_prefetch=1,
            grid=grid,
            in_specs=[wide, narrow][: len(ins)],
            out_specs=narrow if up is None else wide,
        ),
        cost_estimate=pl.CostEstimate(
            flops=int(flops), transcendentals=4 * HEADS * GROUP * GROUP, bytes_accessed=8 << 20
        ),
    )(scalar.reshape(1).astype(jnp.int32), *ins)


def adamw(weight, grad, first, second, rate, decay):
    first_new = BETA_ONE * first + (1.0 - BETA_ONE) * grad
    second_new = BETA_TWO * second + (1.0 - BETA_TWO) * grad * grad
    unbiased_first = first_new / (1.0 - BETA_ONE**STEP)
    unbiased_second = second_new / (1.0 - BETA_TWO**STEP)
    updated = weight - rate * (
        unbiased_first / (jnp.sqrt(unbiased_second) + ADAM_EPS) + decay * weight
    )
    return (updated, first_new, second_new)


def gelu(values):
    return jax.nn.gelu(values, approximate=True)


def gelu_backward(values, upstream):
    return jax.vjp(gelu, values)[1](upstream)[0]


def swap_slots(values):
    mine, other = halves(values, 1)
    return jnp.concatenate([mine, shifted(other, "h", 1)], axis=0)


def swap_frames(values):
    half = lax.axis_index("h")
    mine, other = jnp.split(values, 2, axis=0)
    other = shifted(other, "h", 1)
    return jnp.where(
        half == 0,
        jnp.concatenate([mine, other], axis=1),
        jnp.concatenate([other, mine], axis=1),
    )


def on_device(
    tokens,
    masked,
    small_grid,
    domains,
    attend_in,
    attend_out,
    expand,
    contract,
    gains,
    tables,
    mean_in,
    mean_out,
    mean_expand,
    mean_contract,
    mean_gains,
    mean_tables,
    square_in,
    square_out,
    square_expand,
    square_contract,
    square_gains,
    square_tables,
):
    micro = lax.axis_index("m")
    half = lax.axis_index("h")
    frames = FRAMES // lax.axis_size("h")
    block = contract.shape[0]
    kinds = gains.shape[0]

    def of_micro(array):
        return at(array[:, 0], micro, 0)

    codes = of_micro(tokens)
    hidden_mask = of_micro(masked).astype(WIDE)
    small = of_micro(small_grid)
    doms = of_micro(domains)

    turned = jnp.pad(gains.T, ((0, 0), (0, LANES - kinds)))
    layers = [attend_in[0], attend_out[0], turned, attend_in[1], attend_out[1]]
    ends = [0]
    for array in layers:
        ends.append(ends[-1] + array.shape[1])
    gathered = jnp.concatenate(layers, axis=1).astype(LOW)
    gathered = lax.all_gather(gathered, ALL, axis=0, tiled=True)
    low_in, low_out = tables.astype(LOW)
    up_job = Job(gather_columns(expand.astype(LOW), block))
    down_job = Job(gather_half(contract.astype(LOW)))
    in_table_job = Job(gather_table(low_in))
    token = advance(jnp.zeros((), WIDE), up_job, down_job)
    token = advance(token, in_table_job, up_job, down_job)
    token = advance(token, in_table_job, up_job)
    table_in = in_table_job.finish()
    code_ids = jnp.arange(table_in.shape[0])

    def own_frames(array):
        return lax.dynamic_slice_in_dim(array, half * frames, frames, 0)

    space_codes = own_frames(codes).reshape(-1)
    picked = dot_nn((space_codes[:, None] == code_ids[None, :]).astype(LOW), table_in)
    token = advance(token, down_job, up_job)
    out_table_job = Job(gather_table(low_out))
    picked, token = lax.optimization_barrier((picked, token))
    gathered = advance(gathered, out_table_job)
    first_in, first_out, turned, next_in, next_out = (
        gathered[:, start:end] for start, end in zip(ends, ends[1:])
    )
    w_in, w_out = (first_in, next_in), (first_out, next_out)
    gain_all = turned.T[:kinds].astype(WIDE)

    slot_ids = jnp.arange(SLOTS)
    segment = jnp.where(small > 0, slot_ids // SMALL_TOKENS, 0)
    dom_slot = jnp.sum((segment[:, None] == jnp.arange(CLIPS)[None, :]) * doms[None, :], axis=-1)
    domain_hot = (dom_slot[:, None] == jnp.arange(DOMAINS)[None, :]).astype(WIDE)
    counts = jnp.sum(jnp.sum(hidden_mask, axis=0)[:, None] * domain_hot, axis=0)[None, :]
    counts = Job(sum_over(counts, ("r", "z"))).finish()[0]
    scale = 1.0 / (MICRO * DOMAINS * jnp.maximum(counts, 1.0))
    slot_scale = jnp.sum(domain_hot * scale[None, :], axis=1)

    def time_order(array):
        mine = halves(array, 1)[0]
        return jnp.concatenate(halves(mine, 0), axis=0).reshape(-1)

    space_mask = own_frames(hidden_mask).reshape(-1)
    time_codes = time_order(codes)
    time_weight = time_order(hidden_mask * slot_scale[None, :])

    start = jnp.where(space_mask[:, None] > 0, gain_all[4], picked)
    normed_space = norm_forward(start, gain_all[0]).astype(LOW)
    packed_space = dot_nn(normed_space, w_in[0]).astype(LOW)
    mixed_space = attention("space", small, packed_space)
    mixed_space = advance(mixed_space, down_job, up_job)
    after_space = start + dot_nn(mixed_space, w_out[0])
    after_space = swap_slots(after_space.reshape(frames, SLOTS, D)).reshape(-1, D)
    normed_time = norm_forward(after_space, gain_all[1]).astype(LOW)
    normed_time = advance(normed_time, out_table_job)
    table_out = out_table_job.finish()
    packed_time = dot_nn(normed_time, w_in[1]).astype(LOW).reshape(FRAMES, -1, 3 * D)
    mixed_time = attention("time", half, packed_time).reshape(-1, D)
    after_time = after_space + dot_nn(mixed_time, w_out[1])
    normed_ffn = norm_forward(after_time, gain_all[2]).astype(LOW)
    ups, downs = up_job.finish(), down_job.finish()
    pres = [dot_nn(normed_ffn, up) for up in ups]
    activs = [gelu(pre).astype(LOW) for pre in pres]
    after_ffn = after_time + dot_nn(activs[0], downs[0]) + dot_nn(activs[1], downs[1])
    final = norm_forward(after_ffn, gain_all[3]).astype(LOW)
    logits = dot_nt(final, table_out)
    hits = time_codes[:, None] == code_ids[None, :]
    top = jnp.max(logits, axis=1, keepdims=True)
    log_total = top + jnp.log(jnp.sum(jnp.exp(logits - top), axis=1, keepdims=True))
    target = jnp.sum(jnp.where(hits, logits, 0.0), axis=1)
    loss_part = jnp.sum(time_weight * (log_total[:, 0] - target))
    grad_logits = (time_weight[:, None] * (jnp.exp(logits - log_total) - hits)).astype(LOW)

    def product(make, left, mine, other, *rest):
        return Job(make(dot_tn(left, other).astype(LOW), lambda: dot_tn(left, mine), *rest))

    head_job = product(sum_table, grad_logits, *halves(final, 1))
    grad_final = dot_nn(grad_logits, table_out)
    grad_ffn, gain_three = norm_backward(after_ffn, gain_all[3], grad_final)
    up_low = grad_ffn.astype(LOW)
    contract_job = Job(
        reduce_owned(
            dot_tn(activs[1], up_low).astype(LOW),
            lambda: dot_tn(activs[0], up_low),
            ("m", "r", "z"),
            2,
        )
    )
    grad_activs = [dot_nt(up_low, down) for down in downs]
    grad_pres = [gelu_backward(pre, grad).astype(LOW) for pre, grad in zip(pres, grad_activs)]
    grad_pres = advance(grad_pres, head_job, contract_job)
    expand_job = product(
        reduce_layer, normed_ffn, grad_pres[0], grad_pres[1], ("r", "m", "z"), block, 2
    )
    grad_normed = dot_nt(grad_pres[0], ups[0]) + dot_nt(grad_pres[1], ups[1])
    inward, gain_two = norm_backward(after_time, gain_all[2], grad_normed)
    grad_time = grad_ffn + inward
    up_low = grad_time.astype(LOW)
    up_low = advance(up_low, head_job, expand_job)
    out_job = product(reduce_layer, mixed_time, *halves(up_low, 1), ("m", "r", "z"))
    grad_mixed = dot_nt(up_low, w_out[1]).astype(LOW)
    grad_packed = attention("time", half, packed_time, grad_mixed).reshape(-1, 3 * D)
    grad_packed = advance(grad_packed, head_job, contract_job, out_job)
    in_job = product(
        reduce_layer, normed_time, *halves(grad_packed, 1), ("m", "r", "z"), None, 2
    )
    grad_normed = dot_nt(grad_packed, w_in[1])
    inward, gain_one = norm_backward(after_space, gain_all[1], grad_normed)
    grad_space = swap_frames((grad_time + inward).reshape(FRAMES, -1, D)).reshape(-1, D)
    up_low = grad_space.astype(LOW)
    up_low = advance(up_low, head_job, contract_job, in_job)
    first_out_job = product(reduce_layer, mixed_space, *halves(up_low, 1), ("r", "m", "z"))
    grad_mixed = dot_nt(up_low, w_out[0]).astype(LOW)
    grad_mixed = advance(grad_mixed, out_job, first_out_job)
    grad_packed = attention("space", small, packed_space, grad_mixed)
    grad_packed = advance(
        grad_packed, head_job, contract_job, expand_job, in_job
    )
    first_in_job = product(
        reduce_layer, normed_space, *halves(grad_packed, 1), ("r", "m", "z"), None, 2
    )
    grad_normed = dot_nt(grad_packed, w_in[0])
    grad_normed = advance(
        grad_normed, first_in_job, head_job, expand_job, out_job, in_job, first_out_job
    )
    inward, gain_zero = norm_backward(start, gain_all[0], grad_normed)
    grad_start = grad_space + inward
    mask_grad = jnp.sum(grad_start * space_mask[:, None], axis=0)
    chosen = (jnp.where(space_mask > 0, -1, space_codes)[:, None] == code_ids[None, :]).astype(LOW)
    start_low = grad_start.astype(LOW)
    embed_job = product(reduce_table, chosen, *halves(start_low, 1))

    gain_grads = jnp.stack([gain_zero, gain_one, gain_two, gain_three, mask_grad])
    gain_job = Job(sum_over(gain_grads, ("h", "m", "r", "z")))
    token = jnp.zeros((), WIDE)
    token = advance(token, embed_job, gain_job, head_job, out_job, expand_job, first_out_job)
    token = advance(token, first_in_job)
    token = advance(token, embed_job, gain_job, in_job, first_out_job)
    token = advance(token, first_in_job)
    token = advance(token, embed_job, gain_job, expand_job, in_job, first_out_job)
    token = advance(token, first_in_job, embed_job, gain_job, first_out_job)

    owner = jnp.int32(0)
    for axis in ALL:
        owner = owner * lax.axis_size(axis) + lax.axis_index(axis)
    width = gains.shape[1]
    gain_grads = lax.dynamic_slice_in_dim(gain_job.finish(), owner * width, width, 1)
    jobs = (in_job, first_in_job, out_job, first_out_job, expand_job, contract_job)
    jobs = jobs + (embed_job, head_job)
    lane = jnp.arange(LANES)
    small_square = jnp.pad(jnp.sum(gain_grads * gain_grads, axis=0), (0, LANES - width))
    owned = sum(job.square for job in jobs) + small_square
    sums = jnp.stack([owned, jnp.where(lane == 0, loss_part, 0.0)])
    norm_job = Job(sum_over(sums, ("h", "m", "r", "z")))
    while norm_job.flight is not None:
        token = advance(token, norm_job, *jobs)
    results = [(job.finish(), None) for job in jobs]
    square_sum, loss = jnp.sum(norm_job.result, axis=1)
    norm = jnp.sqrt(square_sum)
    factor = jnp.minimum(1.0, CLIP / (norm + 1e-06))

    made = [grad for grad, _ in results]
    grads = (
        jnp.stack([made[1], made[0]]),
        jnp.stack([made[3], made[2]]),
        made[4],
        made[5],
        gain_grads,
        jnp.stack([made[6], made[7]]),
    )
    params = (attend_in, attend_out, expand, contract, gains, tables)
    firsts = (mean_in, mean_out, mean_expand, mean_contract, mean_gains, mean_tables)
    seconds = (square_in, square_out, square_expand, square_contract, square_gains, square_tables)
    rates = (RATE, RATE, RATE, RATE, RATE_SMALL, RATE)
    decays = (DECAY, DECAY, DECAY, DECAY, 0.0, DECAY)
    results = [
        adamw(p, factor * g, f, s, r, k)
        for p, g, f, s, r, k in zip(params, grads, firsts, seconds, rates, decays)
    ]
    return (loss, norm) + tuple(result[k] for k in range(3) for result in results)


def solution(mesh):
    dp, code = mesh.shape["dp"], mesh.shape["code"]
    deep = next(n for n in (4, 2, 1) if dp % n == 0)
    fine = Mesh(mesh.devices.reshape(deep, dp // deep, MICRO, code // MICRO), ALL)
    group = ("z", "r")
    weights = (
        P(None, ALL, None),
        P(None, ALL, None),
        P(ALL, None),
        P(ALL, None),
        P(None, ALL),
        P(None, ("m", "h"), None),
    )
    return jax.shard_map(
        on_device,
        mesh=fine,
        in_specs=(
            P(None, group, None, None),
            P(None, group, None, None),
            P(None, group),
            P(None, group, None),
        )
        + weights * 3,
        out_specs=(P(), P()) + weights * 3,
        check_vma=False,
    )
```

```python
import functools
from typing import NamedTuple

import jax
import jax.numpy as jnp
from jax import lax
from jax.experimental import pallas as pl
from jax.experimental.pallas import tpu as pltpu
from jax.sharding import Mesh, PartitionSpec as P

D = 1024
HEADS = 16
HEAD = 64
FRAMES = 4
SLOTS = 256
SMALL_TOKENS = 64
CLIPS = 4
DOMAINS = 4
MICRO = 2
STEP = 10


EPS = 1e-05
NEG = -1e30
BETA_ONE = 0.9
BETA_TWO = 0.95
ADAM_EPS = 1e-08
DECAY = 0.1
RATE = 0.02
RATE_SMALL = 0.2
CLIP = 0.005
LOW = jnp.bfloat16
WIDE = jnp.float32
ALL = ("z", "r", "m", "h")
GROUP = 256
LANES = 128


def shifted(part, axis, shift):
    n = lax.axis_size(axis)
    return lax.ppermute(part, axis, [((i + shift) % n, i) for i in range(n)])


def at(array, index, dim):
    return lax.dynamic_index_in_dim(array, index, dim, keepdims=False)


def sent_around(part, axis):
    return [shifted(part, axis, shift) for shift in range(1, lax.axis_size(axis))]


def placed(part, others, axis, dim):
    n = lax.axis_size(axis)
    mine = lax.axis_index(axis)
    whole = jnp.broadcast_to(
        jnp.expand_dims(part, dim), part.shape[:dim] + (n,) + part.shape[dim:]
    )
    for shift, other in zip(range(1, n), others):
        whole = lax.dynamic_update_index_in_dim(whole, other, (mine + shift) % n, dim)
    return whole


def gather_axis(part, axis, dim):
    return placed(part, sent_around(part, axis), axis, dim)


def halves(array, dim):
    size = array.shape[dim] // lax.axis_size("h")
    half = lax.axis_index("h")
    return [
        lax.dynamic_slice_in_dim(array, start * size, size, dim) for start in (half, 1 - half)
    ]


class Squared(NamedTuple):
    square: jax.Array
    flight: list


class Job:
    def __init__(self, steps):
        self.steps = steps
        self.result = self.square = None
        self.flight = next(steps)

    def resume(self, arrived):
        try:
            self.flight = self.steps.send(arrived)
        except StopIteration as stop:
            self.flight, self.result = None, stop.value
        if isinstance(self.flight, Squared):
            self.square, self.flight = self.flight

    def finish(self):
        while self.flight is not None:
            self.resume(self.flight)
        return self.result


def advance(value, *jobs):
    jobs = [job for job in jobs if job.flight is not None]
    value, flights = lax.optimization_barrier((value, [job.flight for job in jobs]))
    for job, flight in zip(jobs, flights):
        job.resume(flight)
    return value


def split_columns(array):
    cut = array.shape[-1] // (2 * LANES) * LANES
    return array[..., :cut], array[..., cut:]


def gather_deep(part):
    if lax.axis_size("z") != 4:
        others = yield sent_around(part, "z")
        return placed(part, others, "z", 0)
    above, below = yield [shifted(part, "z", 1), shifted(part, "z", 3)]
    first, second = split_columns(above)[0], split_columns(below)[1]
    first, second = yield [shifted(first, "z", 1), shifted(second, "z", 3)]
    mine = lax.axis_index("z")
    whole = jnp.broadcast_to(part[None], (4,) + part.shape)
    whole = lax.dynamic_update_index_in_dim(whole, above, (mine + 1) % 4, 0)
    whole = lax.dynamic_update_index_in_dim(whole, below, (mine + 3) % 4, 0)
    zero = jnp.int32(0)
    place = [(mine + 2) % 4] + [zero] * part.ndim
    whole = lax.dynamic_update_slice(whole, first[None], place)
    place[-1] = jnp.int32(first.shape[-1])
    return lax.dynamic_update_slice(whole, second[None], place)


def gather_flat(part, dim):
    first, second = split_columns(part)
    one, two = yield (sent_around(first, "m"), sent_around(second, "r"))
    first, second = placed(first, one, "m", dim), placed(second, two, "r", dim)
    one, two = yield (sent_around(first, "r"), sent_around(second, "m"))
    first, second = placed(first, one, "r", dim), placed(second, two, "m", dim + 1)
    return jnp.concatenate([first, second], axis=-1)


def exchanged(own):
    own = own.reshape(-1, own.shape[-1])
    (other,) = yield [shifted(own, "h", 1)]
    return (own, other)


def gather_half(part):
    whole = yield from gather_deep(part)
    whole = yield from gather_flat(whole, 1)
    return (yield from exchanged(whole))


def gather_table(part):
    others = yield sent_around(part, "m")
    part = placed(part, others, "m", 0)
    others = yield sent_around(part, "h")
    return placed(part, others, "h", 1).reshape(-1, part.shape[-1])


def by_owner(array, block):
    seen = array.reshape(array.shape[0], -1, 2, block)
    half = lax.axis_index("h")
    return [at(seen, which, 2).reshape(array.shape[0], -1) for which in (half, 1 - half)]


def gather_columns(part, block):
    mine, other = by_owner(part, block)
    (other,) = yield [shifted(other, "h", 1)]
    pair = placed(mine, [other], "h", 0)
    result = yield from gather_half(pair.reshape(-1, mine.shape[1]))
    return result


def pieces_of(total, dim, axis):
    n = lax.axis_size(axis)
    mine = lax.axis_index(axis)
    return [
        shifted(at(total, (mine + shift) % n, dim), axis, n - shift) for shift in range(1, n)
    ]


def added(total, dim, axis, pieces):
    total = at(total, lax.axis_index(axis), dim).astype(WIDE)
    for piece in pieces:
        total = total + piece.astype(WIDE)
    return total


def reduce_flat(other, own, names, order, parts=1):
    (arrived,) = yield [shifted(other, "h", 1)]
    total = (own() + arrived.astype(WIDE)).astype(LOW)
    names = list(names)
    total = total.reshape(
        tuple(lax.axis_size(name) for name in names) + (-1, total.shape[-1])
    )
    totals = jnp.split(total, parts, axis=-1)
    orders = [list(order), [order[1], order[0]] + list(order[2:])][:parts]
    left = [list(names) for _ in totals]
    for step in range(2):
        dims = [names.index(axes[step]) for names, axes in zip(left, orders)]
        steps = list(zip(totals, dims, [axes[step] for axes in orders]))
        pieces = yield [pieces_of(*each) for each in steps]
        totals = [added(*each, arrived).astype(LOW) for each, arrived in zip(steps, pieces)]
        for names, dim in zip(left, dims):
            names.pop(dim)
    return totals[0] if parts == 1 else jnp.concatenate(totals, axis=-1)


def reduce_rows(other, own, names, order, parts=1):
    total = yield from reduce_flat(other, own, names, order, parts)
    dim = [name for name in names if name not in order[:2]].index(order[2])
    pieces = yield pieces_of(total, dim, order[2])
    return added(total, dim, order[2], pieces)


def squares(total):
    total = total.reshape(-1, total.shape[-1] // LANES, LANES)
    return jnp.sum(total * total, axis=(0, 1))


def swap_rows(total, square=None):
    seen = total.reshape(2, -1, total.shape[-1])
    half = lax.axis_index("h")
    flight = [shifted(at(seen, 1 - half, 0), "h", 1)]
    (other,) = yield flight if square is None else Squared(square, flight)
    return (at(seen, half, 0), other)


def in_order(mine, other, dim):
    first = lax.axis_index("h") == 0
    return jnp.concatenate(
        [jnp.where(first, mine, other), jnp.where(first, other, mine)], axis=dim
    )


def reduce_layer(other, own, order, parts=1):
    return (yield from reduce_flat(other, own, ("z", "r", "m"), order, parts))


def reduce_deep(totals, blocks):
    ends = [0]
    for total in totals:
        ends.append(ends[-1] + total.shape[-1])
    total = totals[0] if len(totals) == 1 else jnp.concatenate(totals, axis=-1)
    pieces = yield pieces_of(total, 0, "z")
    total = added(total, 0, "z", pieces)
    pair = yield from swap_rows(total, squares(total))
    grads = []
    for start, end, block in zip(ends, ends[1:], blocks):
        mine, other = (half[:, start:end] for half in pair)
        if block is None:
            grads.append(in_order(mine, other, 1))
            continue
        rows = mine.shape[0]
        mine, other = (half.reshape(rows, -1, 1, block) for half in (mine, other))
        grads.append(in_order(mine, other, 2).reshape(rows, -1))
    return grads


def reduce_owned(other, own, order, parts):
    total = yield from reduce_rows(other, own, ("z", "r", "m"), order, parts)
    total = total.reshape(-1, total.shape[-1])
    yield Squared(squares(total), [])
    return total


def reduce_table(other, own):
    total = yield from reduce_rows(other, own, ("m", "h", "r", "z"), ("m", "r", "z"))
    square = squares(total)
    total = total.astype(LOW)
    others = yield Squared(square, sent_around(total, "z"))
    total = placed(total, others, "z", 1)
    others = yield sent_around(total, "r")
    total = placed(total, others, "r", 1)
    mine, other = yield from swap_rows(total.reshape(-1, total.shape[-1]))
    return in_order(mine, other, 1).astype(WIDE)


def sum_over(part, axes):
    for axis in axes:
        n = lax.axis_size(axis)
        if n == 4:
            others = yield sent_around(part, axis)
            part = jnp.sum(placed(part, others, axis, 0), axis=0)
            continue
        shift = n // 2
        while shift:
            (other,) = yield [shifted(part, axis, shift)]
            part = part + other
            shift //= 2
    return part


def norm_forward(values, gain):
    return values * lax.rsqrt(jnp.mean(values * values, axis=-1, keepdims=True) + EPS) * gain


def norm_backward(values, gain, upstream):
    factor = lax.rsqrt(jnp.mean(values * values, axis=-1, keepdims=True) + EPS)
    scaled = upstream * gain
    inward = factor * scaled - values * factor**3 * jnp.mean(
        scaled * values, axis=-1, keepdims=True
    )
    gain_grad = jnp.sum(upstream * values * factor, axis=0)
    return (inward, gain_grad)


def dot_nt(left, right):
    return lax.dot_general(left, right, (((1,), (1,)), ((), ())), preferred_element_type=WIDE)


def dot_tn(left, right):
    return lax.dot_general(left, right, (((0,), (0,)), ((), ())), preferred_element_type=WIDE)


def dot_nn(left, right):
    return jnp.dot(left, right, preferred_element_type=WIDE)


def allowed_pairs(kind, scalar, count, query_dim=0):
    row = lax.broadcasted_iota(jnp.int32, (count, count), query_dim)
    col = lax.broadcasted_iota(jnp.int32, (count, count), 1 - query_dim)
    if kind == "space":
        return (scalar == 0) | (row // SMALL_TOKENS == col // SMALL_TOKENS)
    lanes = count // FRAMES
    own = FRAMES // 2
    row_frame, col_frame = row // lanes, col // lanes
    row_at = row_frame + jnp.where(scalar == 0, 0, jnp.where(row_frame < own, own, -own))
    col_at = col_frame + jnp.where(scalar == 0, 0, jnp.where(col_frame < own, own, -own))
    return (row % lanes == col % lanes) & (col_at <= row_at)


def softmax_rows(query, key, allowed):
    scores = jnp.where(allowed, dot_nt(query, key) * HEAD ** (-0.5), NEG)
    expd = jnp.exp(scores - jnp.max(scores, axis=-1, keepdims=True))
    return expd / jnp.sum(expd, axis=-1, keepdims=True)


def block_of(ref, start, kind):
    if kind == "space":
        return ref[:, pl.ds(start, LANES)]
    part = ref[:, :, pl.ds(start, LANES)]
    return part.reshape(-1, LANES)


def store_to(ref, start, kind, value):
    if kind == "space":
        ref[:, pl.ds(start, LANES)] = value
    else:
        ref[:, :, pl.ds(start, LANES)] = value.reshape(FRAMES, -1, LANES)


def forward_body(kind, scalar_ref, packed_ref, mixed_ref):
    allowed = allowed_pairs(kind, scalar_ref[0], GROUP)
    first = lax.broadcasted_iota(jnp.int32, (GROUP, LANES), 1) < HEAD

    def turn(pair, _):
        start = pl.multiple_of(pair * LANES, LANES)
        query = block_of(packed_ref, start, kind)
        key = block_of(packed_ref, pl.multiple_of(D + start, LANES), kind)
        value = block_of(packed_ref, pl.multiple_of(2 * D + start, LANES), kind)
        zero = jnp.zeros_like(query)
        one = dot_nn(softmax_rows(jnp.where(first, query, zero), key, allowed).astype(LOW), value)
        two = dot_nn(softmax_rows(jnp.where(first, zero, query), key, allowed).astype(LOW), value)
        store_to(mixed_ref, start, kind, jnp.where(first, one, two).astype(LOW))
        return 0

    lax.fori_loop(0, D // LANES, turn, 0, unroll=4)


def backward_body(kind, scalar_ref, packed_ref, up_ref, out_ref):
    allowed = allowed_pairs(kind, scalar_ref[0], GROUP, 1)
    first = lax.broadcasted_iota(jnp.int32, (GROUP, LANES), 1) < HEAD

    def turn(pair, _):
        start = pl.multiple_of(pair * LANES, LANES)
        key_at = pl.multiple_of(D + start, LANES)
        value_at = pl.multiple_of(2 * D + start, LANES)
        query = block_of(packed_ref, start, kind)
        key = block_of(packed_ref, key_at, kind)
        value = block_of(packed_ref, value_at, kind)
        up = block_of(up_ref, start, kind)
        zero = jnp.zeros_like(query)
        grads = []
        for mine in (first, ~first):
            scores = dot_nt(key, jnp.where(mine, query, zero)) * HEAD ** (-0.5)
            scores = jnp.where(allowed, scores, NEG)
            expd = jnp.exp(scores - jnp.max(scores, axis=0, keepdims=True))
            probs = expd / jnp.sum(expd, axis=0, keepdims=True)
            inner = dot_nt(value, jnp.where(mine, up, zero))
            total = jnp.sum(probs * inner, axis=0, keepdims=True)
            scores = (probs * (inner - total) * HEAD ** (-0.5)).astype(LOW)
            grads.append((dot_tn(scores, key), dot_nn(scores, query), dot_nn(probs.astype(LOW), up)))
        for place, one, two in zip((start, key_at, value_at), *grads):
            store_to(out_ref, place, kind, jnp.where(first, one, two).astype(LOW))
        return 0

    lax.fori_loop(0, D // LANES, turn, 0, unroll=2)


def attention(kind, scalar, packed, up=None):
    shape = packed.shape[:-1]
    if kind == "space":
        grid, block, where = (shape[0] // GROUP,), (GROUP,), lambda g, s: (g, 0)
    else:
        grid, block, where = (FRAMES * shape[1] // GROUP,), (FRAMES, GROUP // FRAMES), lambda g, s: (0, g, 0)
    wide = pl.BlockSpec(block + (3 * D,), where)
    narrow = pl.BlockSpec(block + (D,), where)
    body, last, ins, flops = forward_body, D, (packed,), 9e9
    if up is not None:
        body, last, flops = backward_body, 3 * D, 22e9
        ins = (packed, up.reshape(shape + (D,)))
    return pl.pallas_call(
        functools.partial(body, kind),
        out_shape=jax.ShapeDtypeStruct(shape + (last,), LOW),
        grid_spec=pltpu.PrefetchScalarGridSpec(
            num_scalar_prefetch=1,
            grid=grid,
            in_specs=[wide, narrow][: len(ins)],
            out_specs=narrow if up is None else wide,
        ),
        cost_estimate=pl.CostEstimate(
            flops=int(flops), transcendentals=4 * HEADS * GROUP * GROUP, bytes_accessed=8 << 20
        ),
    )(scalar.reshape(1).astype(jnp.int32), *ins)


def adamw(weight, grad, first, second, rate, decay):
    first_new = BETA_ONE * first + (1.0 - BETA_ONE) * grad
    second_new = BETA_TWO * second + (1.0 - BETA_TWO) * grad * grad
    unbiased_first = first_new / (1.0 - BETA_ONE**STEP)
    unbiased_second = second_new / (1.0 - BETA_TWO**STEP)
    updated = weight - rate * (
        unbiased_first / (jnp.sqrt(unbiased_second) + ADAM_EPS) + decay * weight
    )
    return (updated, first_new, second_new)


def gelu(values):
    return jax.nn.gelu(values, approximate=True)


def gelu_backward(values, upstream):
    return jax.vjp(gelu, values)[1](upstream)[0]


def swap_slots(values):
    mine, other = halves(values, 1)
    return jnp.concatenate([mine, shifted(other, "h", 1)], axis=0)


def swap_frames(values):
    half = lax.axis_index("h")
    mine, other = jnp.split(values, 2, axis=0)
    other = shifted(other, "h", 1)
    return jnp.where(
        half == 0,
        jnp.concatenate([mine, other], axis=1),
        jnp.concatenate([other, mine], axis=1),
    )


def on_device(
    tokens,
    masked,
    small_grid,
    domains,
    attend_in,
    attend_out,
    expand,
    contract,
    gains,
    tables,
    mean_in,
    mean_out,
    mean_expand,
    mean_contract,
    mean_gains,
    mean_tables,
    square_in,
    square_out,
    square_expand,
    square_contract,
    square_gains,
    square_tables,
):
    micro = lax.axis_index("m")
    half = lax.axis_index("h")
    frames = FRAMES // lax.axis_size("h")
    block = contract.shape[0]
    kinds = gains.shape[0]

    def of_micro(array):
        return at(array[:, 0], micro, 0)

    codes = of_micro(tokens)
    hidden_mask = of_micro(masked).astype(WIDE)
    small = of_micro(small_grid)
    doms = of_micro(domains)

    turned = jnp.pad(gains.T, ((0, 0), (0, LANES - kinds)))
    layers = [attend_in[0], attend_out[0], turned, attend_in[1], attend_out[1]]
    ends = [0]
    for array in layers:
        ends.append(ends[-1] + array.shape[1])
    gathered = jnp.concatenate(layers, axis=1).astype(LOW)
    gathered = lax.all_gather(gathered, ALL, axis=0, tiled=True)
    low_in, low_out = tables.astype(LOW)
    up_job = Job(gather_columns(expand.astype(LOW), block))
    down_job = Job(gather_half(contract.astype(LOW)))
    in_table_job = Job(gather_table(low_in))
    token = advance(jnp.zeros((), WIDE), up_job, down_job)
    token = advance(token, in_table_job, up_job, down_job)
    token = advance(token, in_table_job, up_job)
    table_in = in_table_job.finish()
    code_ids = jnp.arange(table_in.shape[0])

    def own_frames(array):
        return lax.dynamic_slice_in_dim(array, half * frames, frames, 0)

    space_codes = own_frames(codes).reshape(-1)
    picked = dot_nn((space_codes[:, None] == code_ids[None, :]).astype(LOW), table_in)
    token = advance(token, down_job, up_job)
    out_table_job = Job(gather_table(low_out))
    picked, token = lax.optimization_barrier((picked, token))
    gathered = advance(gathered, out_table_job)
    first_in, first_out, turned, next_in, next_out = (
        gathered[:, start:end] for start, end in zip(ends, ends[1:])
    )
    w_in, w_out = (first_in, next_in), (first_out, next_out)
    gain_all = turned.T[:kinds].astype(WIDE)

    slot_ids = jnp.arange(SLOTS)
    segment = jnp.where(small > 0, slot_ids // SMALL_TOKENS, 0)
    dom_slot = jnp.sum((segment[:, None] == jnp.arange(CLIPS)[None, :]) * doms[None, :], axis=-1)
    domain_hot = (dom_slot[:, None] == jnp.arange(DOMAINS)[None, :]).astype(WIDE)
    counts = jnp.sum(jnp.sum(hidden_mask, axis=0)[:, None] * domain_hot, axis=0)[None, :]
    counts = Job(sum_over(counts, ("r", "z"))).finish()[0]
    scale = 1.0 / (MICRO * DOMAINS * jnp.maximum(counts, 1.0))
    slot_scale = jnp.sum(domain_hot * scale[None, :], axis=1)

    def time_order(array):
        mine = halves(array, 1)[0]
        return jnp.concatenate(halves(mine, 0), axis=0).reshape(-1)

    space_mask = own_frames(hidden_mask).reshape(-1)
    time_codes = time_order(codes)
    time_weight = time_order(hidden_mask * slot_scale[None, :])

    start = jnp.where(space_mask[:, None] > 0, gain_all[4], picked)
    normed_space = norm_forward(start, gain_all[0]).astype(LOW)
    packed_space = dot_nn(normed_space, w_in[0]).astype(LOW)
    mixed_space = attention("space", small, packed_space)
    mixed_space = advance(mixed_space, down_job, up_job)
    after_space = start + dot_nn(mixed_space, w_out[0])
    after_space = swap_slots(after_space.reshape(frames, SLOTS, D)).reshape(-1, D)
    normed_time = norm_forward(after_space, gain_all[1]).astype(LOW)
    normed_time = advance(normed_time, out_table_job)
    table_out = out_table_job.finish()
    packed_time = dot_nn(normed_time, w_in[1]).astype(LOW).reshape(FRAMES, -1, 3 * D)
    mixed_time = attention("time", half, packed_time).reshape(-1, D)
    after_time = after_space + dot_nn(mixed_time, w_out[1])
    normed_ffn = norm_forward(after_time, gain_all[2]).astype(LOW)
    ups, downs = up_job.finish(), down_job.finish()
    pres = [dot_nn(normed_ffn, up) for up in ups]
    activs = [gelu(pre).astype(LOW) for pre in pres]
    after_ffn = after_time + dot_nn(activs[0], downs[0]) + dot_nn(activs[1], downs[1])
    final = norm_forward(after_ffn, gain_all[3]).astype(LOW)
    logits = dot_nt(final, table_out)
    hits = time_codes[:, None] == code_ids[None, :]
    top = jnp.max(logits, axis=1, keepdims=True)
    log_total = top + jnp.log(jnp.sum(jnp.exp(logits - top), axis=1, keepdims=True))
    target = jnp.sum(jnp.where(hits, logits, 0.0), axis=1)
    loss_part = jnp.sum(time_weight * (log_total[:, 0] - target))
    grad_logits = (time_weight[:, None] * (jnp.exp(logits - log_total) - hits)).astype(LOW)

    def product(make, left, mine, other, *rest):
        return Job(make(dot_tn(left, other).astype(LOW), lambda: dot_tn(left, mine), *rest))

    head_job = product(reduce_table, grad_logits, *halves(final, 1))
    grad_final = dot_nn(grad_logits, table_out)
    grad_ffn, gain_three = norm_backward(after_ffn, gain_all[3], grad_final)
    up_low = grad_ffn.astype(LOW)
    contract_job = Job(
        reduce_owned(
            dot_tn(activs[1], up_low).astype(LOW),
            lambda: dot_tn(activs[0], up_low),
            ("m", "r", "z"),
            2,
        )
    )
    grad_activs = [dot_nt(up_low, down) for down in downs]
    grad_pres = [gelu_backward(pre, grad).astype(LOW) for pre, grad in zip(pres, grad_activs)]
    grad_pres = advance(grad_pres, head_job, contract_job)
    expand_job = product(
        reduce_layer, normed_ffn, grad_pres[0], grad_pres[1], ("r", "m", "z"), 2
    )
    grad_normed = dot_nt(grad_pres[0], ups[0]) + dot_nt(grad_pres[1], ups[1])
    inward, gain_two = norm_backward(after_time, gain_all[2], grad_normed)
    grad_time = grad_ffn + inward
    up_low = grad_time.astype(LOW)
    up_low = advance(up_low, head_job, expand_job)
    out_job = product(reduce_layer, mixed_time, *halves(up_low, 1), ("m", "r", "z"))
    grad_mixed = dot_nt(up_low, w_out[1]).astype(LOW)
    grad_packed = attention("time", half, packed_time, grad_mixed).reshape(-1, 3 * D)
    grad_packed = advance(grad_packed, head_job, contract_job, out_job)
    in_job = product(
        reduce_layer, normed_time, *halves(grad_packed, 1), ("m", "r", "z"), 2
    )
    grad_normed = dot_nt(grad_packed, w_in[1])
    inward, gain_one = norm_backward(after_space, gain_all[1], grad_normed)
    grad_space = swap_frames((grad_time + inward).reshape(FRAMES, -1, D)).reshape(-1, D)
    up_low = grad_space.astype(LOW)
    up_low = advance(up_low, head_job, contract_job, in_job)
    first_out_job = product(reduce_layer, mixed_space, *halves(up_low, 1), ("r", "m", "z"))
    grad_mixed = dot_nt(up_low, w_out[0]).astype(LOW)
    grad_mixed = advance(grad_mixed, first_out_job)
    grad_packed = attention("space", small, packed_space, grad_mixed)
    grad_packed = advance(
        grad_packed, head_job, contract_job, expand_job, out_job, in_job
    )
    first_in_job = product(
        reduce_layer, normed_space, *halves(grad_packed, 1), ("r", "m", "z"), 2
    )
    grad_normed = dot_nt(grad_packed, w_in[0])
    grad_normed = advance(grad_normed, first_in_job, head_job, expand_job, out_job)
    early_job = Job(reduce_deep([expand_job.result, out_job.result], [block, None]))
    inward, gain_zero = norm_backward(start, gain_all[0], grad_normed)
    grad_start = grad_space + inward
    mask_grad = jnp.sum(grad_start * space_mask[:, None], axis=0)
    chosen = (jnp.where(space_mask > 0, -1, space_codes)[:, None] == code_ids[None, :]).astype(LOW)
    start_low = grad_start.astype(LOW)
    embed_job = product(reduce_table, chosen, *halves(start_low, 1))

    gain_grads = jnp.stack([gain_zero, gain_one, gain_two, gain_three, mask_grad])
    gain_job = Job(sum_over(gain_grads, ("h", "m", "r", "z")))
    token = jnp.zeros((), WIDE)
    token = advance(token, embed_job, gain_job, head_job, in_job, first_out_job)
    token = advance(token, first_in_job)
    token = advance(token, embed_job, gain_job, head_job, early_job, first_out_job)
    late_job = Job(reduce_deep([in_job.result, first_out_job.result], [None, None]))
    token = advance(token, first_in_job)
    last_job = Job(reduce_deep([first_in_job.result], [None]))
    token = advance(token, embed_job, gain_job, early_job, late_job)
    token = advance(token, last_job, embed_job, gain_job)

    owner = jnp.int32(0)
    for axis in ALL:
        owner = owner * lax.axis_size(axis) + lax.axis_index(axis)
    width = gains.shape[1]
    gain_grads = lax.dynamic_slice_in_dim(gain_job.finish(), owner * width, width, 1)
    jobs = (early_job, late_job, last_job, contract_job, embed_job, head_job)
    lane = jnp.arange(LANES)
    small_square = jnp.pad(jnp.sum(gain_grads * gain_grads, axis=0), (0, LANES - width))
    owned = sum(job.square for job in jobs) + small_square
    sums = jnp.stack([owned, jnp.where(lane == 0, loss_part, 0.0)])
    norm_job = Job(sum_over(sums, ("h", "m", "r", "z")))
    while norm_job.flight is not None:
        token = advance(token, norm_job, *jobs)
    (up_grad, next_out), (next_in, first_out), (first_in,) = (job.finish() for job in jobs[:3])
    square_sum, loss = jnp.sum(norm_job.result, axis=1)
    norm = jnp.sqrt(square_sum)
    factor = jnp.minimum(1.0, CLIP / (norm + 1e-06))

    grads = (
        jnp.stack([first_in, next_in]),
        jnp.stack([first_out, next_out]),
        up_grad,
        contract_job.finish(),
        gain_grads,
        jnp.stack([embed_job.finish(), head_job.finish()]),
    )
    params = (attend_in, attend_out, expand, contract, gains, tables)
    firsts = (mean_in, mean_out, mean_expand, mean_contract, mean_gains, mean_tables)
    seconds = (square_in, square_out, square_expand, square_contract, square_gains, square_tables)
    rates = (RATE, RATE, RATE, RATE, RATE_SMALL, RATE)
    decays = (DECAY, DECAY, DECAY, DECAY, 0.0, DECAY)
    results = [
        adamw(p, factor * g, f, s, r, k)
        for p, g, f, s, r, k in zip(params, grads, firsts, seconds, rates, decays)
    ]
    return (loss, norm) + tuple(result[k] for k in range(3) for result in results)


def solution(mesh):
    dp, code = mesh.shape["dp"], mesh.shape["code"]
    deep = next(n for n in (4, 2, 1) if dp % n == 0)
    fine = Mesh(mesh.devices.reshape(deep, dp // deep, MICRO, code // MICRO), ALL)
    group = ("z", "r")
    weights = (
        P(None, ALL, None),
        P(None, ALL, None),
        P(ALL, None),
        P(ALL, None),
        P(None, ALL),
        P(None, ("m", "h"), None),
    )
    return jax.shard_map(
        on_device,
        mesh=fine,
        in_specs=(
            P(None, group, None, None),
            P(None, group, None, None),
            P(None, group),
            P(None, group, None),
        )
        + weights * 3,
        out_specs=(P(), P()) + weights * 3,
        check_vma=False,
    )
```

```python
import functools
from typing import NamedTuple

import jax
import jax.numpy as jnp
from jax import lax
from jax.experimental import pallas as pl
from jax.experimental.pallas import tpu as pltpu
from jax.sharding import Mesh, PartitionSpec as P

D = 1024
HEADS = 16
HEAD = 64
FRAMES = 4
SLOTS = 256
SMALL_TOKENS = 64
CLIPS = 4
DOMAINS = 4
MICRO = 2
STEP = 10


EPS = 1e-05
NEG = -1e30
BETA_ONE = 0.9
BETA_TWO = 0.95
ADAM_EPS = 1e-08
DECAY = 0.1
RATE = 0.02
RATE_SMALL = 0.2
CLIP = 0.005
LOW = jnp.bfloat16
WIDE = jnp.float32
ALL = ("z", "r", "m", "h")
GROUP = 256
LANES = 128


def shifted(part, axis, shift):
    n = lax.axis_size(axis)
    return lax.ppermute(part, axis, [((i + shift) % n, i) for i in range(n)])


def at(array, index, dim):
    return lax.dynamic_index_in_dim(array, index, dim, keepdims=False)


def sent_around(part, axis):
    return [shifted(part, axis, shift) for shift in range(1, lax.axis_size(axis))]


def placed(part, others, axis, dim):
    n = lax.axis_size(axis)
    mine = lax.axis_index(axis)
    whole = jnp.broadcast_to(
        jnp.expand_dims(part, dim), part.shape[:dim] + (n,) + part.shape[dim:]
    )
    for shift, other in zip(range(1, n), others):
        whole = lax.dynamic_update_index_in_dim(whole, other, (mine + shift) % n, dim)
    return whole


def gather_axis(part, axis, dim):
    return placed(part, sent_around(part, axis), axis, dim)


def halves(array, dim):
    size = array.shape[dim] // lax.axis_size("h")
    half = lax.axis_index("h")
    return [
        lax.dynamic_slice_in_dim(array, start * size, size, dim) for start in (half, 1 - half)
    ]


class Squared(NamedTuple):
    square: jax.Array
    flight: list


class Job:
    def __init__(self, steps):
        self.steps = steps
        self.result = self.square = None
        self.flight = next(steps)

    def resume(self, arrived):
        try:
            self.flight = self.steps.send(arrived)
        except StopIteration as stop:
            self.flight, self.result = None, stop.value
        if isinstance(self.flight, Squared):
            self.square, self.flight = self.flight

    def finish(self):
        while self.flight is not None:
            self.resume(self.flight)
        return self.result


def advance(value, *jobs):
    jobs = [job for job in jobs if job.flight is not None]
    value, flights = lax.optimization_barrier((value, [job.flight for job in jobs]))
    for job, flight in zip(jobs, flights):
        job.resume(flight)
    return value


def split_columns(array):
    cut = array.shape[-1] // (2 * LANES) * LANES
    return array[..., :cut], array[..., cut:]


def gather_deep(part):
    if lax.axis_size("z") != 4:
        others = yield sent_around(part, "z")
        return placed(part, others, "z", 0)
    above, below = yield [shifted(part, "z", 1), shifted(part, "z", 3)]
    first, second = split_columns(above)[0], split_columns(below)[1]
    first, second = yield [shifted(first, "z", 1), shifted(second, "z", 3)]
    mine = lax.axis_index("z")
    whole = jnp.broadcast_to(part[None], (4,) + part.shape)
    whole = lax.dynamic_update_index_in_dim(whole, above, (mine + 1) % 4, 0)
    whole = lax.dynamic_update_index_in_dim(whole, below, (mine + 3) % 4, 0)
    zero = jnp.int32(0)
    place = [(mine + 2) % 4] + [zero] * part.ndim
    whole = lax.dynamic_update_slice(whole, first[None], place)
    place[-1] = jnp.int32(first.shape[-1])
    return lax.dynamic_update_slice(whole, second[None], place)


def gather_flat(part, dim):
    first, second = split_columns(part)
    one, two = yield (sent_around(first, "m"), sent_around(second, "r"))
    first, second = placed(first, one, "m", dim), placed(second, two, "r", dim)
    one, two = yield (sent_around(first, "r"), sent_around(second, "m"))
    first, second = placed(first, one, "r", dim), placed(second, two, "m", dim + 1)
    return jnp.concatenate([first, second], axis=-1)


def exchanged(own):
    own = own.reshape(-1, own.shape[-1])
    (other,) = yield [shifted(own, "h", 1)]
    return (own, other)


def gather_half(part):
    whole = yield from gather_deep(part)
    whole = yield from gather_flat(whole, 1)
    return (yield from exchanged(whole))


def gather_table(part):
    others = yield sent_around(part, "m")
    part = placed(part, others, "m", 0)
    others = yield sent_around(part, "h")
    return placed(part, others, "h", 1).reshape(-1, part.shape[-1])


def by_owner(array, block):
    seen = array.reshape(array.shape[0], -1, 2, block)
    half = lax.axis_index("h")
    return [at(seen, which, 2).reshape(array.shape[0], -1) for which in (half, 1 - half)]


def gather_columns(part, block):
    mine, other = by_owner(part, block)
    (other,) = yield [shifted(other, "h", 1)]
    pair = placed(mine, [other], "h", 0)
    result = yield from gather_half(pair.reshape(-1, mine.shape[1]))
    return result


def pieces_of(total, dim, axis):
    n = lax.axis_size(axis)
    mine = lax.axis_index(axis)
    return [
        shifted(at(total, (mine + shift) % n, dim), axis, n - shift) for shift in range(1, n)
    ]


def added(total, dim, axis, pieces):
    total = at(total, lax.axis_index(axis), dim).astype(WIDE)
    for piece in pieces:
        total = total + piece.astype(WIDE)
    return total


def reduce_flat(other, own, names, order, parts=1):
    (arrived,) = yield [shifted(other, "h", 1)]
    total = (own() + arrived.astype(WIDE)).astype(LOW)
    names = list(names)
    total = total.reshape(
        tuple(lax.axis_size(name) for name in names) + (-1, total.shape[-1])
    )
    totals = jnp.split(total, parts, axis=-1)
    orders = [list(order), [order[1], order[0]] + list(order[2:])][:parts]
    left = [list(names) for _ in totals]
    for step in range(2):
        dims = [names.index(axes[step]) for names, axes in zip(left, orders)]
        steps = list(zip(totals, dims, [axes[step] for axes in orders]))
        pieces = yield [pieces_of(*each) for each in steps]
        totals = [added(*each, arrived).astype(LOW) for each, arrived in zip(steps, pieces)]
        for names, dim in zip(left, dims):
            names.pop(dim)
    return totals[0] if parts == 1 else jnp.concatenate(totals, axis=-1)


def reduce_rows(other, own, names, order, parts=1):
    total = yield from reduce_flat(other, own, names, order, parts)
    dim = [name for name in names if name not in order[:2]].index(order[2])
    pieces = yield pieces_of(total, dim, order[2])
    return added(total, dim, order[2], pieces)


def squares(total):
    total = total.reshape(-1, total.shape[-1] // LANES, LANES)
    return jnp.sum(total * total, axis=(0, 1))


def swap_rows(total, square=None):
    seen = total.reshape(2, -1, total.shape[-1])
    half = lax.axis_index("h")
    flight = [shifted(at(seen, 1 - half, 0), "h", 1)]
    (other,) = yield flight if square is None else Squared(square, flight)
    return (at(seen, half, 0), other)


def in_order(mine, other, dim):
    first = lax.axis_index("h") == 0
    return jnp.concatenate(
        [jnp.where(first, mine, other), jnp.where(first, other, mine)], axis=dim
    )


def reduce_layer(other, own, order, parts=1):
    return (yield from reduce_flat(other, own, ("z", "r", "m"), order, parts))


def reduce_deep(totals, blocks):
    ends = [0]
    for total in totals:
        ends.append(ends[-1] + total.shape[-1])
    total = totals[0] if len(totals) == 1 else jnp.concatenate(totals, axis=-1)
    pieces = yield pieces_of(total, 0, "z")
    total = added(total, 0, "z", pieces)
    pair = yield from swap_rows(total, squares(total))
    grads = []
    for start, end, block in zip(ends, ends[1:], blocks):
        mine, other = (half[:, start:end] for half in pair)
        if block is None:
            grads.append(in_order(mine, other, 1))
            continue
        rows = mine.shape[0]
        mine, other = (half.reshape(rows, -1, 1, block) for half in (mine, other))
        grads.append(in_order(mine, other, 2).reshape(rows, -1))
    return grads


def reduce_owned(other, own, order, parts):
    total = yield from reduce_rows(other, own, ("z", "r", "m"), order, parts)
    total = total.reshape(-1, total.shape[-1])
    yield Squared(squares(total), [])
    return total


def reduce_table(other, own):
    total = yield from reduce_rows(other, own, ("m", "h", "r", "z"), ("m", "r", "z"))
    square = squares(total)
    total = total.astype(LOW)
    others = yield Squared(square, sent_around(total, "z"))
    total = placed(total, others, "z", 1)
    others = yield sent_around(total, "r")
    total = placed(total, others, "r", 1)
    mine, other = yield from swap_rows(total.reshape(-1, total.shape[-1]))
    return in_order(mine, other, 1).astype(WIDE)


def sum_over(part, axes):
    for axis in axes:
        n = lax.axis_size(axis)
        if n == 4:
            others = yield sent_around(part, axis)
            part = jnp.sum(placed(part, others, axis, 0), axis=0)
            continue
        shift = n // 2
        while shift:
            (other,) = yield [shifted(part, axis, shift)]
            part = part + other
            shift //= 2
    return part


def norm_forward(values, gain):
    return values * lax.rsqrt(jnp.mean(values * values, axis=-1, keepdims=True) + EPS) * gain


def norm_backward(values, gain, upstream):
    factor = lax.rsqrt(jnp.mean(values * values, axis=-1, keepdims=True) + EPS)
    scaled = upstream * gain
    inward = factor * scaled - values * factor**3 * jnp.mean(
        scaled * values, axis=-1, keepdims=True
    )
    gain_grad = jnp.sum(upstream * values * factor, axis=0)
    return (inward, gain_grad)


def dot_nt(left, right):
    return lax.dot_general(left, right, (((1,), (1,)), ((), ())), preferred_element_type=WIDE)


def dot_tn(left, right):
    return lax.dot_general(left, right, (((0,), (0,)), ((), ())), preferred_element_type=WIDE)


def dot_nn(left, right):
    return jnp.dot(left, right, preferred_element_type=WIDE)


def allowed_pairs(kind, scalar, count, query_dim=0):
    row = lax.broadcasted_iota(jnp.int32, (count, count), query_dim)
    col = lax.broadcasted_iota(jnp.int32, (count, count), 1 - query_dim)
    if kind == "space":
        return (scalar == 0) | (row // SMALL_TOKENS == col // SMALL_TOKENS)
    lanes = count // FRAMES
    own = FRAMES // 2
    row_frame, col_frame = row // lanes, col // lanes
    row_at = row_frame + jnp.where(scalar == 0, 0, jnp.where(row_frame < own, own, -own))
    col_at = col_frame + jnp.where(scalar == 0, 0, jnp.where(col_frame < own, own, -own))
    return (row % lanes == col % lanes) & (col_at <= row_at)


def softmax_rows(query, key, allowed):
    scores = jnp.where(allowed, dot_nt(query, key) * HEAD ** (-0.5), NEG)
    expd = jnp.exp(scores - jnp.max(scores, axis=-1, keepdims=True))
    return expd / jnp.sum(expd, axis=-1, keepdims=True)


def block_of(ref, start, kind):
    if kind == "space":
        return ref[:, pl.ds(start, LANES)]
    part = ref[:, :, pl.ds(start, LANES)]
    return part.reshape(-1, LANES)


def store_to(ref, start, kind, value):
    if kind == "space":
        ref[:, pl.ds(start, LANES)] = value
    else:
        ref[:, :, pl.ds(start, LANES)] = value.reshape(FRAMES, -1, LANES)


def forward_body(kind, scalar_ref, packed_ref, mixed_ref):
    allowed = allowed_pairs(kind, scalar_ref[0], GROUP)
    first = lax.broadcasted_iota(jnp.int32, (GROUP, LANES), 1) < HEAD

    def turn(pair, _):
        start = pl.multiple_of(pair * LANES, LANES)
        query = block_of(packed_ref, start, kind)
        key = block_of(packed_ref, pl.multiple_of(D + start, LANES), kind)
        value = block_of(packed_ref, pl.multiple_of(2 * D + start, LANES), kind)
        zero = jnp.zeros_like(query)
        one = dot_nn(softmax_rows(jnp.where(first, query, zero), key, allowed).astype(LOW), value)
        two = dot_nn(softmax_rows(jnp.where(first, zero, query), key, allowed).astype(LOW), value)
        store_to(mixed_ref, start, kind, jnp.where(first, one, two).astype(LOW))
        return 0

    lax.fori_loop(0, D // LANES, turn, 0, unroll=4)


def backward_body(kind, scalar_ref, packed_ref, up_ref, out_ref):
    allowed = allowed_pairs(kind, scalar_ref[0], GROUP, 1)
    first = lax.broadcasted_iota(jnp.int32, (GROUP, LANES), 1) < HEAD

    def turn(pair, _):
        start = pl.multiple_of(pair * LANES, LANES)
        key_at = pl.multiple_of(D + start, LANES)
        value_at = pl.multiple_of(2 * D + start, LANES)
        query = block_of(packed_ref, start, kind)
        key = block_of(packed_ref, key_at, kind)
        value = block_of(packed_ref, value_at, kind)
        up = block_of(up_ref, start, kind)
        zero = jnp.zeros_like(query)
        grads = []
        for mine in (first, ~first):
            scores = dot_nt(key, jnp.where(mine, query, zero)) * HEAD ** (-0.5)
            scores = jnp.where(allowed, scores, NEG)
            expd = jnp.exp(scores - jnp.max(scores, axis=0, keepdims=True))
            probs = expd / jnp.sum(expd, axis=0, keepdims=True)
            inner = dot_nt(value, jnp.where(mine, up, zero))
            total = jnp.sum(probs * inner, axis=0, keepdims=True)
            scores = (probs * (inner - total) * HEAD ** (-0.5)).astype(LOW)
            grads.append((dot_tn(scores, key), dot_nn(scores, query), dot_nn(probs.astype(LOW), up)))
        for place, one, two in zip((start, key_at, value_at), *grads):
            store_to(out_ref, place, kind, jnp.where(first, one, two).astype(LOW))
        return 0

    lax.fori_loop(0, D // LANES, turn, 0, unroll=2)


def attention(kind, scalar, packed, up=None):
    shape = packed.shape[:-1]
    if kind == "space":
        grid, block, where = (shape[0] // GROUP,), (GROUP,), lambda g, s: (g, 0)
    else:
        grid, block, where = (FRAMES * shape[1] // GROUP,), (FRAMES, GROUP // FRAMES), lambda g, s: (0, g, 0)
    wide = pl.BlockSpec(block + (3 * D,), where)
    narrow = pl.BlockSpec(block + (D,), where)
    body, last, ins, flops = forward_body, D, (packed,), 9e9
    if up is not None:
        body, last, flops = backward_body, 3 * D, 22e9
        ins = (packed, up.reshape(shape + (D,)))
    return pl.pallas_call(
        functools.partial(body, kind),
        out_shape=jax.ShapeDtypeStruct(shape + (last,), LOW),
        grid_spec=pltpu.PrefetchScalarGridSpec(
            num_scalar_prefetch=1,
            grid=grid,
            in_specs=[wide, narrow][: len(ins)],
            out_specs=narrow if up is None else wide,
        ),
        cost_estimate=pl.CostEstimate(
            flops=int(flops), transcendentals=4 * HEADS * GROUP * GROUP, bytes_accessed=8 << 20
        ),
    )(scalar.reshape(1).astype(jnp.int32), *ins)


def adamw(weight, grad, first, second, rate, decay):
    first_new = BETA_ONE * first + (1.0 - BETA_ONE) * grad
    second_new = BETA_TWO * second + (1.0 - BETA_TWO) * grad * grad
    unbiased_first = first_new / (1.0 - BETA_ONE**STEP)
    unbiased_second = second_new / (1.0 - BETA_TWO**STEP)
    updated = weight - rate * (
        unbiased_first / (jnp.sqrt(unbiased_second) + ADAM_EPS) + decay * weight
    )
    return (updated, first_new, second_new)


def gelu(values):
    return jax.nn.gelu(values, approximate=True)


def gelu_backward(values, upstream):
    return jax.vjp(gelu, values)[1](upstream)[0]


def swap_slots(values):
    mine, other = halves(values, 1)
    return jnp.concatenate([mine, shifted(other, "h", 1)], axis=0)


def swap_frames(values):
    half = lax.axis_index("h")
    mine, other = jnp.split(values, 2, axis=0)
    other = shifted(other, "h", 1)
    return jnp.where(
        half == 0,
        jnp.concatenate([mine, other], axis=1),
        jnp.concatenate([other, mine], axis=1),
    )


def on_device(
    tokens,
    masked,
    small_grid,
    domains,
    attend_in,
    attend_out,
    expand,
    contract,
    gains,
    tables,
    mean_in,
    mean_out,
    mean_expand,
    mean_contract,
    mean_gains,
    mean_tables,
    square_in,
    square_out,
    square_expand,
    square_contract,
    square_gains,
    square_tables,
):
    micro = lax.axis_index("m")
    half = lax.axis_index("h")
    frames = FRAMES // lax.axis_size("h")
    block = contract.shape[0]
    kinds = gains.shape[0]

    def of_micro(array):
        return at(array[:, 0], micro, 0)

    codes = of_micro(tokens)
    hidden_mask = of_micro(masked).astype(WIDE)
    small = of_micro(small_grid)
    doms = of_micro(domains)

    turned = jnp.pad(gains.T, ((0, 0), (0, LANES - kinds)))
    layers = [attend_in[0], attend_out[0], turned, attend_in[1], attend_out[1]]
    ends = [0]
    for array in layers:
        ends.append(ends[-1] + array.shape[1])
    gathered = jnp.concatenate(layers, axis=1).astype(LOW)
    gathered = lax.all_gather(gathered, ALL, axis=0, tiled=True)
    low_in, low_out = tables.astype(LOW)
    up_job = Job(gather_columns(expand.astype(LOW), block))
    down_job = Job(gather_half(contract.astype(LOW)))
    in_table_job = Job(gather_table(low_in))
    token = advance(jnp.zeros((), WIDE), up_job, down_job)
    token = advance(token, in_table_job, up_job, down_job)
    token = advance(token, in_table_job, up_job)
    table_in = in_table_job.finish()
    code_ids = jnp.arange(table_in.shape[0])

    def own_frames(array):
        return lax.dynamic_slice_in_dim(array, half * frames, frames, 0)

    space_codes = own_frames(codes).reshape(-1)
    picked = dot_nn((space_codes[:, None] == code_ids[None, :]).astype(LOW), table_in)
    token = advance(token, down_job, up_job)
    out_table_job = Job(gather_table(low_out))
    picked, token = lax.optimization_barrier((picked, token))
    gathered = advance(gathered, out_table_job)
    first_in, first_out, turned, next_in, next_out = (
        gathered[:, start:end] for start, end in zip(ends, ends[1:])
    )
    w_in, w_out = (first_in, next_in), (first_out, next_out)
    gain_all = turned.T[:kinds].astype(WIDE)

    slot_ids = jnp.arange(SLOTS)
    segment = jnp.where(small > 0, slot_ids // SMALL_TOKENS, 0)
    dom_slot = jnp.sum((segment[:, None] == jnp.arange(CLIPS)[None, :]) * doms[None, :], axis=-1)
    domain_hot = (dom_slot[:, None] == jnp.arange(DOMAINS)[None, :]).astype(WIDE)
    counts = jnp.sum(jnp.sum(hidden_mask, axis=0)[:, None] * domain_hot, axis=0)[None, :]
    counts = Job(sum_over(counts, ("r", "z"))).finish()[0]
    scale = 1.0 / (MICRO * DOMAINS * jnp.maximum(counts, 1.0))
    slot_scale = jnp.sum(domain_hot * scale[None, :], axis=1)

    def time_order(array):
        mine = halves(array, 1)[0]
        return jnp.concatenate(halves(mine, 0), axis=0).reshape(-1)

    space_mask = own_frames(hidden_mask).reshape(-1)
    time_codes = time_order(codes)
    time_weight = time_order(hidden_mask * slot_scale[None, :])

    start = jnp.where(space_mask[:, None] > 0, gain_all[4], picked)
    normed_space = norm_forward(start, gain_all[0]).astype(LOW)
    packed_space = dot_nn(normed_space, w_in[0]).astype(LOW)
    mixed_space = attention("space", small, packed_space)
    mixed_space = advance(mixed_space, down_job, up_job)
    after_space = start + dot_nn(mixed_space, w_out[0])
    after_space = swap_slots(after_space.reshape(frames, SLOTS, D)).reshape(-1, D)
    normed_time = norm_forward(after_space, gain_all[1]).astype(LOW)
    normed_time = advance(normed_time, out_table_job)
    table_out = out_table_job.finish()
    packed_time = dot_nn(normed_time, w_in[1]).astype(LOW).reshape(FRAMES, -1, 3 * D)
    mixed_time = attention("time", half, packed_time).reshape(-1, D)
    after_time = after_space + dot_nn(mixed_time, w_out[1])
    normed_ffn = norm_forward(after_time, gain_all[2]).astype(LOW)
    ups, downs = up_job.finish(), down_job.finish()
    pres = [dot_nn(normed_ffn, up) for up in ups]
    activs = [gelu(pre).astype(LOW) for pre in pres]
    after_ffn = after_time + dot_nn(activs[0], downs[0]) + dot_nn(activs[1], downs[1])
    final = norm_forward(after_ffn, gain_all[3]).astype(LOW)
    logits = dot_nt(final, table_out)
    hits = time_codes[:, None] == code_ids[None, :]
    top = jnp.max(logits, axis=1, keepdims=True)
    log_total = top + jnp.log(jnp.sum(jnp.exp(logits - top), axis=1, keepdims=True))
    target = jnp.sum(jnp.where(hits, logits, 0.0), axis=1)
    loss_part = jnp.sum(time_weight * (log_total[:, 0] - target))
    grad_logits = (time_weight[:, None] * (jnp.exp(logits - log_total) - hits)).astype(LOW)

    def product(make, left, mine, other, *rest):
        return Job(make(dot_tn(left, other).astype(LOW), lambda: dot_tn(left, mine), *rest))

    head_job = product(reduce_table, grad_logits, *halves(final, 1))
    grad_final = dot_nn(grad_logits, table_out)
    grad_ffn, gain_three = norm_backward(after_ffn, gain_all[3], grad_final)
    up_low = grad_ffn.astype(LOW)
    contract_job = Job(
        reduce_owned(
            dot_tn(activs[1], up_low).astype(LOW),
            lambda: dot_tn(activs[0], up_low),
            ("m", "r", "z"),
            2,
        )
    )
    grad_activs = [dot_nt(up_low, down) for down in downs]
    grad_pres = [gelu_backward(pre, grad).astype(LOW) for pre, grad in zip(pres, grad_activs)]
    grad_pres = advance(grad_pres, head_job, contract_job)
    expand_job = product(
        reduce_layer, normed_ffn, grad_pres[0], grad_pres[1], ("r", "m", "z"), 2
    )
    grad_normed = dot_nt(grad_pres[0], ups[0]) + dot_nt(grad_pres[1], ups[1])
    inward, gain_two = norm_backward(after_time, gain_all[2], grad_normed)
    grad_time = grad_ffn + inward
    up_low = grad_time.astype(LOW)
    up_low = advance(up_low, head_job, expand_job)
    out_job = product(reduce_layer, mixed_time, *halves(up_low, 1), ("m", "r", "z"))
    grad_mixed = dot_nt(up_low, w_out[1]).astype(LOW)
    grad_packed = attention("time", half, packed_time, grad_mixed).reshape(-1, 3 * D)
    grad_packed = advance(grad_packed, head_job, contract_job, out_job)
    in_job = product(
        reduce_layer, normed_time, *halves(grad_packed, 1), ("m", "r", "z"), 2
    )
    grad_normed = dot_nt(grad_packed, w_in[1])
    inward, gain_one = norm_backward(after_space, gain_all[1], grad_normed)
    grad_space = swap_frames((grad_time + inward).reshape(FRAMES, -1, D)).reshape(-1, D)
    up_low = grad_space.astype(LOW)
    up_low = advance(up_low, head_job, contract_job, in_job)
    first_out_job = product(reduce_layer, mixed_space, *halves(up_low, 1), ("r", "m", "z"))
    grad_mixed = dot_nt(up_low, w_out[0]).astype(LOW)
    grad_mixed = advance(grad_mixed, first_out_job)
    grad_packed = attention("space", small, packed_space, grad_mixed)
    grad_packed = advance(
        grad_packed, head_job, contract_job, expand_job, in_job
    )
    first_in_job = product(
        reduce_layer, normed_space, *halves(grad_packed, 1), ("r", "m", "z"), 2
    )
    grad_normed = dot_nt(grad_packed, w_in[0])
    grad_normed = advance(grad_normed, first_in_job, head_job, expand_job, out_job)
    early_job = Job(reduce_deep([expand_job.result], [block]))
    inward, gain_zero = norm_backward(start, gain_all[0], grad_normed)
    grad_start = grad_space + inward
    mask_grad = jnp.sum(grad_start * space_mask[:, None], axis=0)
    chosen = (jnp.where(space_mask > 0, -1, space_codes)[:, None] == code_ids[None, :]).astype(LOW)
    start_low = grad_start.astype(LOW)
    embed_job = product(reduce_table, chosen, *halves(start_low, 1))

    gain_grads = jnp.stack([gain_zero, gain_one, gain_two, gain_three, mask_grad])
    gain_job = Job(sum_over(gain_grads, ("h", "m", "r", "z")))
    token = jnp.zeros((), WIDE)
    token = advance(token, embed_job, gain_job, head_job, in_job, out_job, first_out_job)
    token = advance(token, first_in_job)
    token = advance(token, embed_job, gain_job, head_job, early_job, first_out_job)
    token = advance(token, first_in_job)
    last_job = Job(reduce_deep([first_in_job.result], [None]))
    held = [in_job.result, first_out_job.result, out_job.result]
    token, held = lax.optimization_barrier((token, held))
    late_job = Job(reduce_deep(held, [None, None, None]))
    token = advance(token, embed_job, gain_job, early_job)
    token = advance(token, last_job, embed_job, gain_job, late_job)

    owner = jnp.int32(0)
    for axis in ALL:
        owner = owner * lax.axis_size(axis) + lax.axis_index(axis)
    width = gains.shape[1]
    gain_grads = lax.dynamic_slice_in_dim(gain_job.finish(), owner * width, width, 1)
    jobs = (early_job, late_job, last_job, contract_job, embed_job, head_job)
    lane = jnp.arange(LANES)
    small_square = jnp.pad(jnp.sum(gain_grads * gain_grads, axis=0), (0, LANES - width))
    owned = sum(job.square for job in jobs) + small_square
    sums = jnp.stack([owned, jnp.where(lane == 0, loss_part, 0.0)])
    norm_job = Job(sum_over(sums, ("h", "m", "r", "z")))
    while norm_job.flight is not None:
        token = advance(token, norm_job, *jobs)
    (up_grad,), (next_in, first_out, next_out), (first_in,) = (job.finish() for job in jobs[:3])
    square_sum, loss = jnp.sum(norm_job.result, axis=1)
    norm = jnp.sqrt(square_sum)
    factor = jnp.minimum(1.0, CLIP / (norm + 1e-06))

    grads = (
        jnp.stack([first_in, next_in]),
        jnp.stack([first_out, next_out]),
        up_grad,
        contract_job.finish(),
        gain_grads,
        jnp.stack([embed_job.finish(), head_job.finish()]),
    )
    params = (attend_in, attend_out, expand, contract, gains, tables)
    firsts = (mean_in, mean_out, mean_expand, mean_contract, mean_gains, mean_tables)
    seconds = (square_in, square_out, square_expand, square_contract, square_gains, square_tables)
    rates = (RATE, RATE, RATE, RATE, RATE_SMALL, RATE)
    decays = (DECAY, DECAY, DECAY, DECAY, 0.0, DECAY)
    results = [
        adamw(p, factor * g, f, s, r, k)
        for p, g, f, s, r, k in zip(params, grads, firsts, seconds, rates, decays)
    ]
    return (loss, norm) + tuple(result[k] for k in range(3) for result in results)


def solution(mesh):
    dp, code = mesh.shape["dp"], mesh.shape["code"]
    deep = next(n for n in (4, 2, 1) if dp % n == 0)
    fine = Mesh(mesh.devices.reshape(deep, dp // deep, MICRO, code // MICRO), ALL)
    group = ("z", "r")
    weights = (
        P(None, ALL, None),
        P(None, ALL, None),
        P(ALL, None),
        P(ALL, None),
        P(None, ALL),
        P(None, ("m", "h"), None),
    )
    return jax.shard_map(
        on_device,
        mesh=fine,
        in_specs=(
            P(None, group, None, None),
            P(None, group, None, None),
            P(None, group),
            P(None, group, None),
        )
        + weights * 3,
        out_specs=(P(), P()) + weights * 3,
        check_vma=False,
    )
```

```python
import functools
from typing import NamedTuple

import jax
import jax.numpy as jnp
from jax import lax
from jax.experimental import pallas as pl
from jax.experimental.pallas import tpu as pltpu
from jax.sharding import Mesh, PartitionSpec as P

D = 1024
HEADS = 16
HEAD = 64
FRAMES = 4
SLOTS = 256
SMALL_TOKENS = 64
CLIPS = 4
DOMAINS = 4
MICRO = 2
STEP = 10


EPS = 1e-05
NEG = -1e30
BETA_ONE = 0.9
BETA_TWO = 0.95
ADAM_EPS = 1e-08
DECAY = 0.1
RATE = 0.02
RATE_SMALL = 0.2
CLIP = 0.005
LOW = jnp.bfloat16
WIDE = jnp.float32
ALL = ("z", "r", "m", "h")
GROUP = 256
LANES = 128


def shifted(part, axis, shift):
    n = lax.axis_size(axis)
    return lax.ppermute(part, axis, [((i + shift) % n, i) for i in range(n)])


def at(array, index, dim):
    return lax.dynamic_index_in_dim(array, index, dim, keepdims=False)


def sent_around(part, axis):
    return [shifted(part, axis, shift) for shift in range(1, lax.axis_size(axis))]


def placed(part, others, axis, dim):
    n = lax.axis_size(axis)
    mine = lax.axis_index(axis)
    whole = jnp.broadcast_to(
        jnp.expand_dims(part, dim), part.shape[:dim] + (n,) + part.shape[dim:]
    )
    for shift, other in zip(range(1, n), others):
        whole = lax.dynamic_update_index_in_dim(whole, other, (mine + shift) % n, dim)
    return whole


def gather_axis(part, axis, dim):
    return placed(part, sent_around(part, axis), axis, dim)


def halves(array, dim):
    size = array.shape[dim] // lax.axis_size("h")
    half = lax.axis_index("h")
    return [
        lax.dynamic_slice_in_dim(array, start * size, size, dim) for start in (half, 1 - half)
    ]


class Squared(NamedTuple):
    square: jax.Array
    flight: list


class Job:
    def __init__(self, steps):
        self.steps = steps
        self.result = self.square = None
        self.flight = next(steps)

    def resume(self, arrived):
        try:
            self.flight = self.steps.send(arrived)
        except StopIteration as stop:
            self.flight, self.result = None, stop.value
        if isinstance(self.flight, Squared):
            self.square, self.flight = self.flight

    def finish(self):
        while self.flight is not None:
            self.resume(self.flight)
        return self.result


def advance(value, *jobs):
    jobs = [job for job in jobs if job.flight is not None]
    value, flights = lax.optimization_barrier((value, [job.flight for job in jobs]))
    for job, flight in zip(jobs, flights):
        job.resume(flight)
    return value


def split_columns(array):
    cut = array.shape[-1] // (2 * LANES) * LANES
    return array[..., :cut], array[..., cut:]


def gather_deep(part):
    if lax.axis_size("z") != 4:
        others = yield sent_around(part, "z")
        return placed(part, others, "z", 0)
    above, below = yield [shifted(part, "z", 1), shifted(part, "z", 3)]
    first, second = split_columns(above)[0], split_columns(below)[1]
    first, second = yield [shifted(first, "z", 1), shifted(second, "z", 3)]
    mine = lax.axis_index("z")
    whole = jnp.broadcast_to(part[None], (4,) + part.shape)
    whole = lax.dynamic_update_index_in_dim(whole, above, (mine + 1) % 4, 0)
    whole = lax.dynamic_update_index_in_dim(whole, below, (mine + 3) % 4, 0)
    zero = jnp.int32(0)
    place = [(mine + 2) % 4] + [zero] * part.ndim
    whole = lax.dynamic_update_slice(whole, first[None], place)
    place[-1] = jnp.int32(first.shape[-1])
    return lax.dynamic_update_slice(whole, second[None], place)


def gather_flat(part, dim):
    first, second = split_columns(part)
    one, two = yield (sent_around(first, "m"), sent_around(second, "r"))
    first, second = placed(first, one, "m", dim), placed(second, two, "r", dim)
    one, two = yield (sent_around(first, "r"), sent_around(second, "m"))
    first, second = placed(first, one, "r", dim), placed(second, two, "m", dim + 1)
    return jnp.concatenate([first, second], axis=-1)


def exchanged(own):
    own = own.reshape(-1, own.shape[-1])
    (other,) = yield [shifted(own, "h", 1)]
    return (own, other)


def gather_half(part):
    whole = yield from gather_deep(part)
    whole = yield from gather_flat(whole, 1)
    return (yield from exchanged(whole))


def gather_table(part):
    others = yield sent_around(part, "m")
    part = placed(part, others, "m", 0)
    others = yield sent_around(part, "h")
    return placed(part, others, "h", 1).reshape(-1, part.shape[-1])


def by_owner(array, block):
    seen = array.reshape(array.shape[0], -1, 2, block)
    half = lax.axis_index("h")
    return [at(seen, which, 2).reshape(array.shape[0], -1) for which in (half, 1 - half)]


def gather_columns(part, block):
    mine, other = by_owner(part, block)
    (other,) = yield [shifted(other, "h", 1)]
    pair = placed(mine, [other], "h", 0)
    result = yield from gather_half(pair.reshape(-1, mine.shape[1]))
    return result


def pieces_of(total, dim, axis):
    n = lax.axis_size(axis)
    mine = lax.axis_index(axis)
    return [
        shifted(at(total, (mine + shift) % n, dim), axis, n - shift) for shift in range(1, n)
    ]


def added(total, dim, axis, pieces):
    total = at(total, lax.axis_index(axis), dim).astype(WIDE)
    for piece in pieces:
        total = total + piece.astype(WIDE)
    return total


def reduce_flat(other, own, names, order, parts=1):
    (arrived,) = yield [shifted(other, "h", 1)]
    total = (own() + arrived.astype(WIDE)).astype(LOW)
    names = list(names)
    total = total.reshape(
        tuple(lax.axis_size(name) for name in names) + (-1, total.shape[-1])
    )
    totals = jnp.split(total, parts, axis=-1)
    orders = [list(order), [order[1], order[0]] + list(order[2:])][:parts]
    left = [list(names) for _ in totals]
    for step in range(2):
        dims = [names.index(axes[step]) for names, axes in zip(left, orders)]
        steps = list(zip(totals, dims, [axes[step] for axes in orders]))
        pieces = yield [pieces_of(*each) for each in steps]
        totals = [added(*each, arrived).astype(LOW) for each, arrived in zip(steps, pieces)]
        for names, dim in zip(left, dims):
            names.pop(dim)
    return totals[0] if parts == 1 else jnp.concatenate(totals, axis=-1)


def reduce_rows(other, own, names, order, parts=1):
    total = yield from reduce_flat(other, own, names, order, parts)
    dim = [name for name in names if name not in order[:2]].index(order[2])
    pieces = yield pieces_of(total, dim, order[2])
    return added(total, dim, order[2], pieces)


def squares(total):
    total = total.reshape(-1, total.shape[-1] // LANES, LANES)
    return jnp.sum(total * total, axis=(0, 1))


def swap_rows(total, square=None):
    seen = total.reshape(2, -1, total.shape[-1])
    half = lax.axis_index("h")
    flight = [shifted(at(seen, 1 - half, 0), "h", 1)]
    (other,) = yield flight if square is None else Squared(square, flight)
    return (at(seen, half, 0), other)


def in_order(mine, other, dim):
    first = lax.axis_index("h") == 0
    return jnp.concatenate(
        [jnp.where(first, mine, other), jnp.where(first, other, mine)], axis=dim
    )


def reduce_layer(other, own, order, parts=1):
    return (yield from reduce_flat(other, own, ("z", "r", "m"), order, parts))


def reduce_deep(totals, blocks):
    ends = [0]
    for total in totals:
        ends.append(ends[-1] + total.shape[-1])
    total = totals[0] if len(totals) == 1 else jnp.concatenate(totals, axis=-1)
    pieces = yield pieces_of(total, 0, "z")
    total = added(total, 0, "z", pieces)
    pair = yield from swap_rows(total, squares(total))
    grads = []
    for start, end, block in zip(ends, ends[1:], blocks):
        mine, other = (half[:, start:end] for half in pair)
        if block is None:
            grads.append(in_order(mine, other, 1))
            continue
        rows = mine.shape[0]
        mine, other = (half.reshape(rows, -1, 1, block) for half in (mine, other))
        grads.append(in_order(mine, other, 2).reshape(rows, -1))
    return grads


def reduce_owned(other, own, order, parts):
    total = yield from reduce_rows(other, own, ("z", "r", "m"), order, parts)
    total = total.reshape(-1, total.shape[-1])
    yield Squared(squares(total), [])
    return total


def reduce_table(other, own):
    total = yield from reduce_rows(other, own, ("m", "h", "r", "z"), ("m", "r", "z"))
    square = squares(total)
    total = total.astype(LOW)
    others = yield Squared(square, sent_around(total, "z"))
    total = placed(total, others, "z", 1)
    others = yield sent_around(total, "r")
    total = placed(total, others, "r", 1)
    mine, other = yield from swap_rows(total.reshape(-1, total.shape[-1]))
    return in_order(mine, other, 1).astype(WIDE)


def sum_over(part, axes):
    for axis in axes:
        n = lax.axis_size(axis)
        if n == 4:
            others = yield sent_around(part, axis)
            part = jnp.sum(placed(part, others, axis, 0), axis=0)
            continue
        shift = n // 2
        while shift:
            (other,) = yield [shifted(part, axis, shift)]
            part = part + other
            shift //= 2
    return part


def norm_forward(values, gain):
    return values * lax.rsqrt(jnp.mean(values * values, axis=-1, keepdims=True) + EPS) * gain


def norm_backward(values, gain, upstream):
    factor = lax.rsqrt(jnp.mean(values * values, axis=-1, keepdims=True) + EPS)
    scaled = upstream * gain
    inward = factor * scaled - values * factor**3 * jnp.mean(
        scaled * values, axis=-1, keepdims=True
    )
    gain_grad = jnp.sum(upstream * values * factor, axis=0)
    return (inward, gain_grad)


def dot_nt(left, right):
    return lax.dot_general(left, right, (((1,), (1,)), ((), ())), preferred_element_type=WIDE)


def dot_tn(left, right):
    return lax.dot_general(left, right, (((0,), (0,)), ((), ())), preferred_element_type=WIDE)


def dot_nn(left, right):
    return jnp.dot(left, right, preferred_element_type=WIDE)


def allowed_pairs(kind, scalar, count, query_dim=0):
    row = lax.broadcasted_iota(jnp.int32, (count, count), query_dim)
    col = lax.broadcasted_iota(jnp.int32, (count, count), 1 - query_dim)
    if kind == "space":
        return (scalar == 0) | (row // SMALL_TOKENS == col // SMALL_TOKENS)
    lanes = count // FRAMES
    own = FRAMES // 2
    row_frame, col_frame = row // lanes, col // lanes
    row_at = row_frame + jnp.where(scalar == 0, 0, jnp.where(row_frame < own, own, -own))
    col_at = col_frame + jnp.where(scalar == 0, 0, jnp.where(col_frame < own, own, -own))
    return (row % lanes == col % lanes) & (col_at <= row_at)


def softmax_rows(query, key, allowed):
    scores = jnp.where(allowed, dot_nt(query, key) * HEAD ** (-0.5), NEG)
    expd = jnp.exp(scores - jnp.max(scores, axis=-1, keepdims=True))
    return expd / jnp.sum(expd, axis=-1, keepdims=True)


def block_of(ref, start, kind):
    if kind == "space":
        return ref[:, pl.ds(start, LANES)]
    part = ref[:, :, pl.ds(start, LANES)]
    return part.reshape(-1, LANES)


def store_to(ref, start, kind, value):
    if kind == "space":
        ref[:, pl.ds(start, LANES)] = value
    else:
        ref[:, :, pl.ds(start, LANES)] = value.reshape(FRAMES, -1, LANES)


def forward_body(kind, scalar_ref, packed_ref, mixed_ref):
    allowed = allowed_pairs(kind, scalar_ref[0], GROUP)
    first = lax.broadcasted_iota(jnp.int32, (GROUP, LANES), 1) < HEAD

    def turn(pair, _):
        start = pl.multiple_of(pair * LANES, LANES)
        query = block_of(packed_ref, start, kind)
        key = block_of(packed_ref, pl.multiple_of(D + start, LANES), kind)
        value = block_of(packed_ref, pl.multiple_of(2 * D + start, LANES), kind)
        zero = jnp.zeros_like(query)
        one = dot_nn(softmax_rows(jnp.where(first, query, zero), key, allowed).astype(LOW), value)
        two = dot_nn(softmax_rows(jnp.where(first, zero, query), key, allowed).astype(LOW), value)
        store_to(mixed_ref, start, kind, jnp.where(first, one, two).astype(LOW))
        return 0

    lax.fori_loop(0, D // LANES, turn, 0, unroll=4)


def backward_body(kind, scalar_ref, packed_ref, up_ref, out_ref):
    allowed = allowed_pairs(kind, scalar_ref[0], GROUP, 1)
    first = lax.broadcasted_iota(jnp.int32, (GROUP, LANES), 1) < HEAD

    def turn(pair, _):
        start = pl.multiple_of(pair * LANES, LANES)
        key_at = pl.multiple_of(D + start, LANES)
        value_at = pl.multiple_of(2 * D + start, LANES)
        query = block_of(packed_ref, start, kind)
        key = block_of(packed_ref, key_at, kind)
        value = block_of(packed_ref, value_at, kind)
        up = block_of(up_ref, start, kind)
        zero = jnp.zeros_like(query)
        grads = []
        for mine in (first, ~first):
            scores = dot_nt(key, jnp.where(mine, query, zero)) * HEAD ** (-0.5)
            scores = jnp.where(allowed, scores, NEG)
            expd = jnp.exp(scores - jnp.max(scores, axis=0, keepdims=True))
            probs = expd / jnp.sum(expd, axis=0, keepdims=True)
            inner = dot_nt(value, jnp.where(mine, up, zero))
            total = jnp.sum(probs * inner, axis=0, keepdims=True)
            scores = (probs * (inner - total) * HEAD ** (-0.5)).astype(LOW)
            grads.append((dot_tn(scores, key), dot_nn(scores, query), dot_nn(probs.astype(LOW), up)))
        for place, one, two in zip((start, key_at, value_at), *grads):
            store_to(out_ref, place, kind, jnp.where(first, one, two).astype(LOW))
        return 0

    lax.fori_loop(0, D // LANES, turn, 0, unroll=2)


def attention(kind, scalar, packed, up=None):
    shape = packed.shape[:-1]
    if kind == "space":
        grid, block, where = (shape[0] // GROUP,), (GROUP,), lambda g, s: (g, 0)
    else:
        grid, block, where = (FRAMES * shape[1] // GROUP,), (FRAMES, GROUP // FRAMES), lambda g, s: (0, g, 0)
    wide = pl.BlockSpec(block + (3 * D,), where)
    narrow = pl.BlockSpec(block + (D,), where)
    body, last, ins, flops = forward_body, D, (packed,), 9e9
    if up is not None:
        body, last, flops = backward_body, 3 * D, 22e9
        ins = (packed, up.reshape(shape + (D,)))
    return pl.pallas_call(
        functools.partial(body, kind),
        out_shape=jax.ShapeDtypeStruct(shape + (last,), LOW),
        grid_spec=pltpu.PrefetchScalarGridSpec(
            num_scalar_prefetch=1,
            grid=grid,
            in_specs=[wide, narrow][: len(ins)],
            out_specs=narrow if up is None else wide,
        ),
        cost_estimate=pl.CostEstimate(
            flops=int(flops), transcendentals=4 * HEADS * GROUP * GROUP, bytes_accessed=8 << 20
        ),
    )(scalar.reshape(1).astype(jnp.int32), *ins)


def adamw(weight, grad, first, second, rate, decay):
    first_new = BETA_ONE * first + (1.0 - BETA_ONE) * grad
    second_new = BETA_TWO * second + (1.0 - BETA_TWO) * grad * grad
    unbiased_first = first_new / (1.0 - BETA_ONE**STEP)
    unbiased_second = second_new / (1.0 - BETA_TWO**STEP)
    updated = weight - rate * (
        unbiased_first / (jnp.sqrt(unbiased_second) + ADAM_EPS) + decay * weight
    )
    return (updated, first_new, second_new)


def gelu(values):
    return jax.nn.gelu(values, approximate=True)


def gelu_backward(values, upstream):
    return jax.vjp(gelu, values)[1](upstream)[0]


def swap_slots(values):
    mine, other = halves(values, 1)
    return jnp.concatenate([mine, shifted(other, "h", 1)], axis=0)


def swap_frames(values):
    half = lax.axis_index("h")
    mine, other = jnp.split(values, 2, axis=0)
    other = shifted(other, "h", 1)
    return jnp.where(
        half == 0,
        jnp.concatenate([mine, other], axis=1),
        jnp.concatenate([other, mine], axis=1),
    )


def on_device(
    tokens,
    masked,
    small_grid,
    domains,
    attend_in,
    attend_out,
    expand,
    contract,
    gains,
    tables,
    mean_in,
    mean_out,
    mean_expand,
    mean_contract,
    mean_gains,
    mean_tables,
    square_in,
    square_out,
    square_expand,
    square_contract,
    square_gains,
    square_tables,
):
    micro = lax.axis_index("m")
    half = lax.axis_index("h")
    frames = FRAMES // lax.axis_size("h")
    block = contract.shape[0]
    kinds = gains.shape[0]

    def of_micro(array):
        return at(array[:, 0], micro, 0)

    codes = of_micro(tokens)
    hidden_mask = of_micro(masked).astype(WIDE)
    small = of_micro(small_grid)
    doms = of_micro(domains)

    turned = jnp.pad(gains.T, ((0, 0), (0, LANES - kinds)))
    layers = [attend_in[0], attend_out[0], turned, attend_in[1], attend_out[1]]
    ends = [0]
    for array in layers:
        ends.append(ends[-1] + array.shape[1])
    gathered = jnp.concatenate(layers, axis=1).astype(LOW)
    gathered = lax.all_gather(gathered, ALL, axis=0, tiled=True)
    low_in, low_out = tables.astype(LOW)
    up_job = Job(gather_columns(expand.astype(LOW), block))
    down_job = Job(gather_half(contract.astype(LOW)))
    in_table_job = Job(gather_table(low_in))
    token = advance(jnp.zeros((), WIDE), up_job, down_job)
    token = advance(token, in_table_job, up_job, down_job)
    token = advance(token, in_table_job, up_job)
    table_in = in_table_job.finish()
    code_ids = jnp.arange(table_in.shape[0])

    def own_frames(array):
        return lax.dynamic_slice_in_dim(array, half * frames, frames, 0)

    space_codes = own_frames(codes).reshape(-1)
    picked = dot_nn((space_codes[:, None] == code_ids[None, :]).astype(LOW), table_in)
    token = advance(token, down_job, up_job)
    out_table_job = Job(gather_table(low_out))
    picked, token = lax.optimization_barrier((picked, token))
    gathered = advance(gathered, out_table_job)
    first_in, first_out, turned, next_in, next_out = (
        gathered[:, start:end] for start, end in zip(ends, ends[1:])
    )
    w_in, w_out = (first_in, next_in), (first_out, next_out)
    gain_all = turned.T[:kinds].astype(WIDE)

    slot_ids = jnp.arange(SLOTS)
    segment = jnp.where(small > 0, slot_ids // SMALL_TOKENS, 0)
    dom_slot = jnp.sum((segment[:, None] == jnp.arange(CLIPS)[None, :]) * doms[None, :], axis=-1)
    domain_hot = (dom_slot[:, None] == jnp.arange(DOMAINS)[None, :]).astype(WIDE)
    counts = jnp.sum(jnp.sum(hidden_mask, axis=0)[:, None] * domain_hot, axis=0)[None, :]
    counts = Job(sum_over(counts, ("r", "z"))).finish()[0]
    scale = 1.0 / (MICRO * DOMAINS * jnp.maximum(counts, 1.0))
    slot_scale = jnp.sum(domain_hot * scale[None, :], axis=1)

    def time_order(array):
        mine = halves(array, 1)[0]
        return jnp.concatenate(halves(mine, 0), axis=0).reshape(-1)

    space_mask = own_frames(hidden_mask).reshape(-1)
    time_codes = time_order(codes)
    time_weight = time_order(hidden_mask * slot_scale[None, :])

    start = jnp.where(space_mask[:, None] > 0, gain_all[4], picked)
    normed_space = norm_forward(start, gain_all[0]).astype(LOW)
    packed_space = dot_nn(normed_space, w_in[0]).astype(LOW)
    mixed_space = attention("space", small, packed_space)
    mixed_space = advance(mixed_space, down_job, up_job)
    after_space = start + dot_nn(mixed_space, w_out[0])
    after_space = swap_slots(after_space.reshape(frames, SLOTS, D)).reshape(-1, D)
    normed_time = norm_forward(after_space, gain_all[1]).astype(LOW)
    normed_time = advance(normed_time, out_table_job)
    table_out = out_table_job.finish()
    packed_time = dot_nn(normed_time, w_in[1]).astype(LOW).reshape(FRAMES, -1, 3 * D)
    mixed_time = attention("time", half, packed_time).reshape(-1, D)
    after_time = after_space + dot_nn(mixed_time, w_out[1])
    normed_ffn = norm_forward(after_time, gain_all[2]).astype(LOW)
    ups, downs = up_job.finish(), down_job.finish()
    pres = [dot_nn(normed_ffn, up) for up in ups]
    activs = [gelu(pre).astype(LOW) for pre in pres]
    after_ffn = after_time + dot_nn(activs[0], downs[0]) + dot_nn(activs[1], downs[1])
    final = norm_forward(after_ffn, gain_all[3]).astype(LOW)
    logits = dot_nt(final, table_out)
    hits = time_codes[:, None] == code_ids[None, :]
    top = jnp.max(logits, axis=1, keepdims=True)
    log_total = top + jnp.log(jnp.sum(jnp.exp(logits - top), axis=1, keepdims=True))
    target = jnp.sum(jnp.where(hits, logits, 0.0), axis=1)
    loss_part = jnp.sum(time_weight * (log_total[:, 0] - target))
    grad_logits = (time_weight[:, None] * (jnp.exp(logits - log_total) - hits)).astype(LOW)

    def product(make, left, mine, other, *rest):
        return Job(make(dot_tn(left, other).astype(LOW), lambda: dot_tn(left, mine), *rest))

    head_job = product(reduce_table, grad_logits, *halves(final, 1))
    grad_final = dot_nn(grad_logits, table_out)
    grad_ffn, gain_three = norm_backward(after_ffn, gain_all[3], grad_final)
    up_low = grad_ffn.astype(LOW)
    contract_job = Job(
        reduce_owned(
            dot_tn(activs[1], up_low).astype(LOW),
            lambda: dot_tn(activs[0], up_low),
            ("m", "r", "z"),
            2,
        )
    )
    grad_activs = [dot_nt(up_low, down) for down in downs]
    grad_pres = [gelu_backward(pre, grad).astype(LOW) for pre, grad in zip(pres, grad_activs)]
    grad_pres = advance(grad_pres, head_job, contract_job)
    expand_job = product(
        reduce_layer, normed_ffn, grad_pres[0], grad_pres[1], ("r", "m", "z"), 2
    )
    grad_normed = dot_nt(grad_pres[0], ups[0]) + dot_nt(grad_pres[1], ups[1])
    inward, gain_two = norm_backward(after_time, gain_all[2], grad_normed)
    grad_time = grad_ffn + inward
    up_low = grad_time.astype(LOW)
    up_low = advance(up_low, head_job, expand_job)
    out_job = product(reduce_layer, mixed_time, *halves(up_low, 1), ("m", "r", "z"))
    grad_mixed = dot_nt(up_low, w_out[1]).astype(LOW)
    grad_packed = attention("time", half, packed_time, grad_mixed).reshape(-1, 3 * D)
    grad_packed = advance(grad_packed, head_job, contract_job, out_job)
    in_job = product(
        reduce_layer, normed_time, *halves(grad_packed, 1), ("m", "r", "z"), 2
    )
    grad_normed = dot_nt(grad_packed, w_in[1])
    inward, gain_one = norm_backward(after_space, gain_all[1], grad_normed)
    grad_space = swap_frames((grad_time + inward).reshape(FRAMES, -1, D)).reshape(-1, D)
    up_low = grad_space.astype(LOW)
    up_low = advance(up_low, head_job, contract_job, in_job)
    first_out_job = product(reduce_layer, mixed_space, *halves(up_low, 1), ("r", "m", "z"))
    grad_mixed = dot_nt(up_low, w_out[0]).astype(LOW)
    grad_mixed = advance(grad_mixed, first_out_job)
    grad_packed = attention("space", small, packed_space, grad_mixed)
    grad_packed = advance(
        grad_packed, head_job, contract_job, expand_job, in_job
    )
    first_in_job = product(
        reduce_layer, normed_space, *halves(grad_packed, 1), ("r", "m", "z"), 2
    )
    grad_normed = dot_nt(grad_packed, w_in[0])
    grad_normed = advance(grad_normed, first_in_job, head_job, expand_job, out_job)
    early_job = Job(reduce_deep([expand_job.result], [block]))
    inward, gain_zero = norm_backward(start, gain_all[0], grad_normed)
    grad_start = grad_space + inward
    mask_grad = jnp.sum(grad_start * space_mask[:, None], axis=0)
    chosen = (jnp.where(space_mask > 0, -1, space_codes)[:, None] == code_ids[None, :]).astype(LOW)
    start_low = grad_start.astype(LOW)
    embed_job = product(reduce_table, chosen, *halves(start_low, 1))

    gain_grads = jnp.stack([gain_zero, gain_one, gain_two, gain_three, mask_grad])
    gain_job = Job(sum_over(gain_grads, ("h", "m", "r", "z")))
    token = jnp.zeros((), WIDE)
    token = advance(token, embed_job, gain_job, head_job, in_job, out_job, first_out_job)
    late_job = Job(reduce_deep([in_job.result, out_job.result], [None, None]))
    token = advance(token, first_in_job)
    token = advance(token, embed_job, gain_job, head_job, early_job, first_out_job)
    token = advance(token, first_in_job)
    last_job = Job(reduce_deep([first_in_job.result, first_out_job.result], [None, None]))
    token = advance(token, embed_job, gain_job, early_job, late_job)
    token = advance(token, last_job, embed_job, gain_job, late_job)

    owner = jnp.int32(0)
    for axis in ALL:
        owner = owner * lax.axis_size(axis) + lax.axis_index(axis)
    width = gains.shape[1]
    gain_grads = lax.dynamic_slice_in_dim(gain_job.finish(), owner * width, width, 1)
    jobs = (early_job, late_job, last_job, contract_job, embed_job, head_job)
    lane = jnp.arange(LANES)
    small_square = jnp.pad(jnp.sum(gain_grads * gain_grads, axis=0), (0, LANES - width))
    owned = sum(job.square for job in jobs) + small_square
    sums = jnp.stack([owned, jnp.where(lane == 0, loss_part, 0.0)])
    norm_job = Job(sum_over(sums, ("h", "m", "r", "z")))
    while norm_job.flight is not None:
        token = advance(token, norm_job, *jobs)
    (up_grad,), (next_in, next_out), (first_in, first_out) = (job.finish() for job in jobs[:3])
    square_sum, loss = jnp.sum(norm_job.result, axis=1)
    norm = jnp.sqrt(square_sum)
    factor = jnp.minimum(1.0, CLIP / (norm + 1e-06))

    grads = (
        jnp.stack([first_in, next_in]),
        jnp.stack([first_out, next_out]),
        up_grad,
        contract_job.finish(),
        gain_grads,
        jnp.stack([embed_job.finish(), head_job.finish()]),
    )
    params = (attend_in, attend_out, expand, contract, gains, tables)
    firsts = (mean_in, mean_out, mean_expand, mean_contract, mean_gains, mean_tables)
    seconds = (square_in, square_out, square_expand, square_contract, square_gains, square_tables)
    rates = (RATE, RATE, RATE, RATE, RATE_SMALL, RATE)
    decays = (DECAY, DECAY, DECAY, DECAY, 0.0, DECAY)
    results = [
        adamw(p, factor * g, f, s, r, k)
        for p, g, f, s, r, k in zip(params, grads, firsts, seconds, rates, decays)
    ]
    return (loss, norm) + tuple(result[k] for k in range(3) for result in results)


def solution(mesh):
    dp, code = mesh.shape["dp"], mesh.shape["code"]
    deep = next(n for n in (4, 2, 1) if dp % n == 0)
    fine = Mesh(mesh.devices.reshape(deep, dp // deep, MICRO, code // MICRO), ALL)
    group = ("z", "r")
    weights = (
        P(None, ALL, None),
        P(None, ALL, None),
        P(ALL, None),
        P(ALL, None),
        P(None, ALL),
        P(None, ("m", "h"), None),
    )
    return jax.shard_map(
        on_device,
        mesh=fine,
        in_specs=(
            P(None, group, None, None),
            P(None, group, None, None),
            P(None, group),
            P(None, group, None),
        )
        + weights * 3,
        out_specs=(P(), P()) + weights * 3,
        check_vma=False,
    )
```

```python
import functools
from typing import NamedTuple

import jax
import jax.numpy as jnp
from jax import lax
from jax.experimental import pallas as pl
from jax.experimental.pallas import tpu as pltpu
from jax.sharding import Mesh, PartitionSpec as P

D = 1024
HEADS = 16
HEAD = 64
FRAMES = 4
SLOTS = 256
SMALL_TOKENS = 64
CLIPS = 4
DOMAINS = 4
MICRO = 2
STEP = 10


EPS = 1e-05
NEG = -1e30
BETA_ONE = 0.9
BETA_TWO = 0.95
ADAM_EPS = 1e-08
DECAY = 0.1
RATE = 0.02
RATE_SMALL = 0.2
CLIP = 0.005
LOW = jnp.bfloat16
WIDE = jnp.float32
ALL = ("z", "r", "m", "h")
GROUP = 256
LANES = 128


def shifted(part, axis, shift):
    n = lax.axis_size(axis)
    return lax.ppermute(part, axis, [((i + shift) % n, i) for i in range(n)])


def at(array, index, dim):
    return lax.dynamic_index_in_dim(array, index, dim, keepdims=False)


def sent_around(part, axis):
    return [shifted(part, axis, shift) for shift in range(1, lax.axis_size(axis))]


def placed(part, others, axis, dim):
    n = lax.axis_size(axis)
    mine = lax.axis_index(axis)
    whole = jnp.broadcast_to(
        jnp.expand_dims(part, dim), part.shape[:dim] + (n,) + part.shape[dim:]
    )
    for shift, other in zip(range(1, n), others):
        whole = lax.dynamic_update_index_in_dim(whole, other, (mine + shift) % n, dim)
    return whole


def gather_axis(part, axis, dim):
    return placed(part, sent_around(part, axis), axis, dim)


def halves(array, dim):
    size = array.shape[dim] // lax.axis_size("h")
    half = lax.axis_index("h")
    return [
        lax.dynamic_slice_in_dim(array, start * size, size, dim) for start in (half, 1 - half)
    ]


class Squared(NamedTuple):
    square: jax.Array
    flight: list


class Job:
    def __init__(self, steps):
        self.steps = steps
        self.result = self.square = None
        self.flight = next(steps)

    def resume(self, arrived):
        try:
            self.flight = self.steps.send(arrived)
        except StopIteration as stop:
            self.flight, self.result = None, stop.value
        if isinstance(self.flight, Squared):
            self.square, self.flight = self.flight

    def finish(self):
        while self.flight is not None:
            self.resume(self.flight)
        return self.result


def advance(value, *jobs):
    jobs = [job for job in jobs if job.flight is not None]
    value, flights = lax.optimization_barrier((value, [job.flight for job in jobs]))
    for job, flight in zip(jobs, flights):
        job.resume(flight)
    return value


def split_columns(array):
    cut = array.shape[-1] // (2 * LANES) * LANES
    return array[..., :cut], array[..., cut:]


def gather_deep(part):
    if lax.axis_size("z") != 4:
        others = yield sent_around(part, "z")
        return placed(part, others, "z", 0)
    above, below = yield [shifted(part, "z", 1), shifted(part, "z", 3)]
    first, second = split_columns(above)[0], split_columns(below)[1]
    first, second = yield [shifted(first, "z", 1), shifted(second, "z", 3)]
    mine = lax.axis_index("z")
    whole = jnp.broadcast_to(part[None], (4,) + part.shape)
    whole = lax.dynamic_update_index_in_dim(whole, above, (mine + 1) % 4, 0)
    whole = lax.dynamic_update_index_in_dim(whole, below, (mine + 3) % 4, 0)
    zero = jnp.int32(0)
    place = [(mine + 2) % 4] + [zero] * part.ndim
    whole = lax.dynamic_update_slice(whole, first[None], place)
    place[-1] = jnp.int32(first.shape[-1])
    return lax.dynamic_update_slice(whole, second[None], place)


def gather_flat(part, dim):
    first, second = split_columns(part)
    one, two = yield (sent_around(first, "m"), sent_around(second, "r"))
    first, second = placed(first, one, "m", dim), placed(second, two, "r", dim)
    one, two = yield (sent_around(first, "r"), sent_around(second, "m"))
    first, second = placed(first, one, "r", dim), placed(second, two, "m", dim + 1)
    return jnp.concatenate([first, second], axis=-1)


def exchanged(own):
    own = own.reshape(-1, own.shape[-1])
    (other,) = yield [shifted(own, "h", 1)]
    return (own, other)


def gather_half(part):
    whole = yield from gather_deep(part)
    whole = yield from gather_flat(whole, 1)
    return (yield from exchanged(whole))


def gather_table(part):
    others = yield sent_around(part, "m")
    part = placed(part, others, "m", 0)
    others = yield sent_around(part, "h")
    return placed(part, others, "h", 1).reshape(-1, part.shape[-1])


def by_owner(array, block):
    seen = array.reshape(array.shape[0], -1, 2, block)
    half = lax.axis_index("h")
    return [at(seen, which, 2).reshape(array.shape[0], -1) for which in (half, 1 - half)]


def gather_columns(part, block):
    mine, other = by_owner(part, block)
    (other,) = yield [shifted(other, "h", 1)]
    pair = placed(mine, [other], "h", 0)
    result = yield from gather_half(pair.reshape(-1, mine.shape[1]))
    return result


def pieces_of(total, dim, axis):
    n = lax.axis_size(axis)
    mine = lax.axis_index(axis)
    return [
        shifted(at(total, (mine + shift) % n, dim), axis, n - shift) for shift in range(1, n)
    ]


def added(total, dim, axis, pieces):
    total = at(total, lax.axis_index(axis), dim).astype(WIDE)
    for piece in pieces:
        total = total + piece.astype(WIDE)
    return total


def reduce_flat(other, own, names, order, parts=1):
    (arrived,) = yield [shifted(other, "h", 1)]
    total = (own() + arrived.astype(WIDE)).astype(LOW)
    names = list(names)
    total = total.reshape(
        tuple(lax.axis_size(name) for name in names) + (-1, total.shape[-1])
    )
    totals = jnp.split(total, parts, axis=-1)
    orders = [list(order), [order[1], order[0]] + list(order[2:])][:parts]
    left = [list(names) for _ in totals]
    for step in range(2):
        dims = [names.index(axes[step]) for names, axes in zip(left, orders)]
        steps = list(zip(totals, dims, [axes[step] for axes in orders]))
        pieces = yield [pieces_of(*each) for each in steps]
        totals = [added(*each, arrived).astype(LOW) for each, arrived in zip(steps, pieces)]
        for names, dim in zip(left, dims):
            names.pop(dim)
    return totals[0] if parts == 1 else jnp.concatenate(totals, axis=-1)


def reduce_rows(other, own, names, order, parts=1):
    total = yield from reduce_flat(other, own, names, order, parts)
    dim = [name for name in names if name not in order[:2]].index(order[2])
    pieces = yield pieces_of(total, dim, order[2])
    return added(total, dim, order[2], pieces)


def squares(total):
    total = total.reshape(-1, total.shape[-1] // LANES, LANES)
    return jnp.sum(total * total, axis=(0, 1))


def swap_rows(total, square=None):
    seen = total.reshape(2, -1, total.shape[-1])
    half = lax.axis_index("h")
    flight = [shifted(at(seen, 1 - half, 0), "h", 1)]
    (other,) = yield flight if square is None else Squared(square, flight)
    return (at(seen, half, 0), other)


def in_order(mine, other, dim):
    first = lax.axis_index("h") == 0
    return jnp.concatenate(
        [jnp.where(first, mine, other), jnp.where(first, other, mine)], axis=dim
    )


def reduce_layer(other, own, order, parts=1):
    return (yield from reduce_flat(other, own, ("z", "r", "m"), order, parts))


def reduce_deep(totals, blocks):
    ends = [0]
    for total in totals:
        ends.append(ends[-1] + total.shape[-1])
    total = totals[0] if len(totals) == 1 else jnp.concatenate(totals, axis=-1)
    pieces = yield pieces_of(total, 0, "z")
    total = added(total, 0, "z", pieces)
    pair = yield from swap_rows(total, squares(total))
    grads = []
    for start, end, block in zip(ends, ends[1:], blocks):
        mine, other = (half[:, start:end] for half in pair)
        if block is None:
            grads.append(in_order(mine, other, 1))
            continue
        rows = mine.shape[0]
        mine, other = (half.reshape(rows, -1, 1, block) for half in (mine, other))
        grads.append(in_order(mine, other, 2).reshape(rows, -1))
    return grads


def reduce_owned(other, own, order, parts):
    total = yield from reduce_rows(other, own, ("z", "r", "m"), order, parts)
    total = total.reshape(-1, total.shape[-1])
    yield Squared(squares(total), [])
    return total


def reduce_table(other, own):
    total = yield from reduce_rows(other, own, ("m", "h", "r", "z"), ("m", "r", "z"))
    square = squares(total)
    total = total.astype(LOW)
    others = yield Squared(square, sent_around(total, "z"))
    total = placed(total, others, "z", 1)
    others = yield sent_around(total, "r")
    total = placed(total, others, "r", 1)
    mine, other = yield from swap_rows(total.reshape(-1, total.shape[-1]))
    return in_order(mine, other, 1).astype(WIDE)


def sum_over(part, axes, direct=4):
    for axis in axes:
        n = lax.axis_size(axis)
        if n == direct:
            others = yield sent_around(part, axis)
            part = jnp.sum(placed(part, others, axis, 0), axis=0)
            continue
        shift = n // 2
        while shift:
            (other,) = yield [shifted(part, axis, shift)]
            part = part + other
            shift //= 2
    return part


def norm_forward(values, gain):
    return values * lax.rsqrt(jnp.mean(values * values, axis=-1, keepdims=True) + EPS) * gain


def norm_backward(values, gain, upstream):
    factor = lax.rsqrt(jnp.mean(values * values, axis=-1, keepdims=True) + EPS)
    scaled = upstream * gain
    inward = factor * scaled - values * factor**3 * jnp.mean(
        scaled * values, axis=-1, keepdims=True
    )
    gain_grad = jnp.sum(upstream * values * factor, axis=0)
    return (inward, gain_grad)


def dot_nt(left, right):
    return lax.dot_general(left, right, (((1,), (1,)), ((), ())), preferred_element_type=WIDE)


def dot_tn(left, right):
    return lax.dot_general(left, right, (((0,), (0,)), ((), ())), preferred_element_type=WIDE)


def dot_nn(left, right):
    return jnp.dot(left, right, preferred_element_type=WIDE)


def allowed_pairs(kind, scalar, count, query_dim=0):
    row = lax.broadcasted_iota(jnp.int32, (count, count), query_dim)
    col = lax.broadcasted_iota(jnp.int32, (count, count), 1 - query_dim)
    if kind == "space":
        return (scalar == 0) | (row // SMALL_TOKENS == col // SMALL_TOKENS)
    lanes = count // FRAMES
    own = FRAMES // 2
    row_frame, col_frame = row // lanes, col // lanes
    row_at = row_frame + jnp.where(scalar == 0, 0, jnp.where(row_frame < own, own, -own))
    col_at = col_frame + jnp.where(scalar == 0, 0, jnp.where(col_frame < own, own, -own))
    return (row % lanes == col % lanes) & (col_at <= row_at)


def softmax_rows(query, key, allowed):
    scores = jnp.where(allowed, dot_nt(query, key) * HEAD ** (-0.5), NEG)
    expd = jnp.exp(scores - jnp.max(scores, axis=-1, keepdims=True))
    return expd / jnp.sum(expd, axis=-1, keepdims=True)


def block_of(ref, start, kind):
    if kind == "space":
        return ref[:, pl.ds(start, LANES)]
    part = ref[:, :, pl.ds(start, LANES)]
    return part.reshape(-1, LANES)


def store_to(ref, start, kind, value):
    if kind == "space":
        ref[:, pl.ds(start, LANES)] = value
    else:
        ref[:, :, pl.ds(start, LANES)] = value.reshape(FRAMES, -1, LANES)


def forward_body(kind, scalar_ref, packed_ref, mixed_ref):
    allowed = allowed_pairs(kind, scalar_ref[0], GROUP)
    first = lax.broadcasted_iota(jnp.int32, (GROUP, LANES), 1) < HEAD

    def turn(pair, _):
        start = pl.multiple_of(pair * LANES, LANES)
        query = block_of(packed_ref, start, kind)
        key = block_of(packed_ref, pl.multiple_of(D + start, LANES), kind)
        value = block_of(packed_ref, pl.multiple_of(2 * D + start, LANES), kind)
        zero = jnp.zeros_like(query)
        one = dot_nn(softmax_rows(jnp.where(first, query, zero), key, allowed).astype(LOW), value)
        two = dot_nn(softmax_rows(jnp.where(first, zero, query), key, allowed).astype(LOW), value)
        store_to(mixed_ref, start, kind, jnp.where(first, one, two).astype(LOW))
        return 0

    lax.fori_loop(0, D // LANES, turn, 0, unroll=4)


def backward_body(kind, scalar_ref, packed_ref, up_ref, out_ref):
    allowed = allowed_pairs(kind, scalar_ref[0], GROUP, 1)
    first = lax.broadcasted_iota(jnp.int32, (GROUP, LANES), 1) < HEAD

    def turn(pair, _):
        start = pl.multiple_of(pair * LANES, LANES)
        key_at = pl.multiple_of(D + start, LANES)
        value_at = pl.multiple_of(2 * D + start, LANES)
        query = block_of(packed_ref, start, kind)
        key = block_of(packed_ref, key_at, kind)
        value = block_of(packed_ref, value_at, kind)
        up = block_of(up_ref, start, kind)
        zero = jnp.zeros_like(query)
        grads = []
        for mine in (first, ~first):
            scores = dot_nt(key, jnp.where(mine, query, zero)) * HEAD ** (-0.5)
            scores = jnp.where(allowed, scores, NEG)
            expd = jnp.exp(scores - jnp.max(scores, axis=0, keepdims=True))
            probs = expd / jnp.sum(expd, axis=0, keepdims=True)
            inner = dot_nt(value, jnp.where(mine, up, zero))
            total = jnp.sum(probs * inner, axis=0, keepdims=True)
            scores = (probs * (inner - total) * HEAD ** (-0.5)).astype(LOW)
            grads.append((dot_tn(scores, key), dot_nn(scores, query), dot_nn(probs.astype(LOW), up)))
        for place, one, two in zip((start, key_at, value_at), *grads):
            store_to(out_ref, place, kind, jnp.where(first, one, two).astype(LOW))
        return 0

    lax.fori_loop(0, D // LANES, turn, 0, unroll=2)


def attention(kind, scalar, packed, up=None):
    shape = packed.shape[:-1]
    if kind == "space":
        grid, block, where = (shape[0] // GROUP,), (GROUP,), lambda g, s: (g, 0)
    else:
        grid, block, where = (FRAMES * shape[1] // GROUP,), (FRAMES, GROUP // FRAMES), lambda g, s: (0, g, 0)
    wide = pl.BlockSpec(block + (3 * D,), where)
    narrow = pl.BlockSpec(block + (D,), where)
    body, last, ins, flops = forward_body, D, (packed,), 9e9
    if up is not None:
        body, last, flops = backward_body, 3 * D, 40e9
        ins = (packed, up.reshape(shape + (D,)))
    return pl.pallas_call(
        functools.partial(body, kind),
        out_shape=jax.ShapeDtypeStruct(shape + (last,), LOW),
        grid_spec=pltpu.PrefetchScalarGridSpec(
            num_scalar_prefetch=1,
            grid=grid,
            in_specs=[wide, narrow][: len(ins)],
            out_specs=narrow if up is None else wide,
        ),
        cost_estimate=pl.CostEstimate(
            flops=int(flops), transcendentals=4 * HEADS * GROUP * GROUP, bytes_accessed=8 << 20
        ),
    )(scalar.reshape(1).astype(jnp.int32), *ins)


def adamw(weight, grad, first, second, rate, decay):
    first_new = BETA_ONE * first + (1.0 - BETA_ONE) * grad
    second_new = BETA_TWO * second + (1.0 - BETA_TWO) * grad * grad
    unbiased_first = first_new / (1.0 - BETA_ONE**STEP)
    unbiased_second = second_new / (1.0 - BETA_TWO**STEP)
    updated = weight - rate * (
        unbiased_first / (jnp.sqrt(unbiased_second) + ADAM_EPS) + decay * weight
    )
    return (updated, first_new, second_new)


def gelu(values):
    return jax.nn.gelu(values, approximate=True)


def gelu_backward(values, upstream):
    return jax.vjp(gelu, values)[1](upstream)[0]


def swap_slots(values):
    mine, other = halves(values, 1)
    return jnp.concatenate([mine, shifted(other, "h", 1)], axis=0)


def swap_frames(values):
    half = lax.axis_index("h")
    mine, other = jnp.split(values, 2, axis=0)
    other = shifted(other, "h", 1)
    return jnp.where(
        half == 0,
        jnp.concatenate([mine, other], axis=1),
        jnp.concatenate([other, mine], axis=1),
    )


def on_device(
    tokens,
    masked,
    small_grid,
    domains,
    attend_in,
    attend_out,
    expand,
    contract,
    gains,
    tables,
    mean_in,
    mean_out,
    mean_expand,
    mean_contract,
    mean_gains,
    mean_tables,
    square_in,
    square_out,
    square_expand,
    square_contract,
    square_gains,
    square_tables,
):
    micro = lax.axis_index("m")
    half = lax.axis_index("h")
    frames = FRAMES // lax.axis_size("h")
    block = contract.shape[0]
    kinds = gains.shape[0]

    def of_micro(array):
        return at(array[:, 0], micro, 0)

    codes = of_micro(tokens)
    hidden_mask = of_micro(masked).astype(WIDE)
    small = of_micro(small_grid)
    doms = of_micro(domains)

    turned = jnp.pad(gains.T, ((0, 0), (0, LANES - kinds)))
    layers = [attend_in[0], attend_out[0], turned, attend_in[1], attend_out[1]]
    ends = [0]
    for array in layers:
        ends.append(ends[-1] + array.shape[1])
    gathered = jnp.concatenate(layers, axis=1).astype(LOW)
    gathered = lax.all_gather(gathered, ALL, axis=0, tiled=True)
    low_in, low_out = tables.astype(LOW)
    up_job = Job(gather_columns(expand.astype(LOW), block))
    down_job = Job(gather_half(contract.astype(LOW)))
    in_table_job = Job(gather_table(low_in))
    token = advance(jnp.zeros((), WIDE), up_job, down_job)
    token = advance(token, in_table_job, up_job, down_job)
    token = advance(token, in_table_job, up_job)
    table_in = in_table_job.finish()
    code_ids = jnp.arange(table_in.shape[0])

    def own_frames(array):
        return lax.dynamic_slice_in_dim(array, half * frames, frames, 0)

    space_codes = own_frames(codes).reshape(-1)
    picked = dot_nn((space_codes[:, None] == code_ids[None, :]).astype(LOW), table_in)
    token = advance(token, down_job, up_job)
    out_table_job = Job(gather_table(low_out))
    picked, token = lax.optimization_barrier((picked, token))
    gathered = advance(gathered, out_table_job)
    first_in, first_out, turned, next_in, next_out = (
        gathered[:, start:end] for start, end in zip(ends, ends[1:])
    )
    w_in, w_out = (first_in, next_in), (first_out, next_out)
    gain_all = turned.T[:kinds].astype(WIDE)

    slot_ids = jnp.arange(SLOTS)
    segment = jnp.where(small > 0, slot_ids // SMALL_TOKENS, 0)
    dom_slot = jnp.sum((segment[:, None] == jnp.arange(CLIPS)[None, :]) * doms[None, :], axis=-1)
    domain_hot = (dom_slot[:, None] == jnp.arange(DOMAINS)[None, :]).astype(WIDE)
    counts = jnp.sum(jnp.sum(hidden_mask, axis=0)[:, None] * domain_hot, axis=0)[None, :]
    counts = Job(sum_over(counts, ("r", "z"))).finish()[0]
    scale = 1.0 / (MICRO * DOMAINS * jnp.maximum(counts, 1.0))
    slot_scale = jnp.sum(domain_hot * scale[None, :], axis=1)

    def time_order(array):
        mine = halves(array, 1)[0]
        return jnp.concatenate(halves(mine, 0), axis=0).reshape(-1)

    space_mask = own_frames(hidden_mask).reshape(-1)
    time_codes = time_order(codes)
    time_weight = time_order(hidden_mask * slot_scale[None, :])

    start = jnp.where(space_mask[:, None] > 0, gain_all[4], picked)
    normed_space = norm_forward(start, gain_all[0]).astype(LOW)
    packed_space = dot_nn(normed_space, w_in[0]).astype(LOW)
    mixed_space = attention("space", small, packed_space)
    mixed_space = advance(mixed_space, down_job, up_job)
    after_space = start + dot_nn(mixed_space, w_out[0])
    after_space = swap_slots(after_space.reshape(frames, SLOTS, D)).reshape(-1, D)
    normed_time = norm_forward(after_space, gain_all[1]).astype(LOW)
    normed_time = advance(normed_time, out_table_job)
    table_out = out_table_job.finish()
    packed_time = dot_nn(normed_time, w_in[1]).astype(LOW).reshape(FRAMES, -1, 3 * D)
    mixed_time = attention("time", half, packed_time).reshape(-1, D)
    after_time = after_space + dot_nn(mixed_time, w_out[1])
    normed_ffn = norm_forward(after_time, gain_all[2]).astype(LOW)
    ups, downs = up_job.finish(), down_job.finish()
    pres = [dot_nn(normed_ffn, up) for up in ups]
    activs = [gelu(pre).astype(LOW) for pre in pres]
    after_ffn = after_time + dot_nn(activs[0], downs[0]) + dot_nn(activs[1], downs[1])
    final = norm_forward(after_ffn, gain_all[3]).astype(LOW)
    logits = dot_nt(final, table_out)
    hits = time_codes[:, None] == code_ids[None, :]
    top = jnp.max(logits, axis=1, keepdims=True)
    log_total = top + jnp.log(jnp.sum(jnp.exp(logits - top), axis=1, keepdims=True))
    target = jnp.sum(jnp.where(hits, logits, 0.0), axis=1)
    loss_part = jnp.sum(time_weight * (log_total[:, 0] - target))
    grad_logits = (time_weight[:, None] * (jnp.exp(logits - log_total) - hits)).astype(LOW)

    def product(make, left, mine, other, *rest):
        return Job(make(dot_tn(left, other).astype(LOW), lambda: dot_tn(left, mine), *rest))

    head_job = product(reduce_table, grad_logits, *halves(final, 1))
    grad_final = dot_nn(grad_logits, table_out)
    grad_ffn, gain_three = norm_backward(after_ffn, gain_all[3], grad_final)
    up_low = grad_ffn.astype(LOW)
    contract_job = Job(
        reduce_owned(
            dot_tn(activs[1], up_low).astype(LOW),
            lambda: dot_tn(activs[0], up_low),
            ("m", "r", "z"),
            2,
        )
    )
    grad_activs = [dot_nt(up_low, down) for down in downs]
    grad_pres = [gelu_backward(pre, grad).astype(LOW) for pre, grad in zip(pres, grad_activs)]
    grad_pres = advance(grad_pres, head_job, contract_job)
    expand_job = product(
        reduce_layer, normed_ffn, grad_pres[0], grad_pres[1], ("r", "m", "z"), 2
    )
    grad_normed = dot_nt(grad_pres[0], ups[0]) + dot_nt(grad_pres[1], ups[1])
    inward, gain_two = norm_backward(after_time, gain_all[2], grad_normed)
    grad_time = grad_ffn + inward
    up_low = grad_time.astype(LOW)
    up_low = advance(up_low, head_job, expand_job)
    out_job = product(reduce_layer, mixed_time, *halves(up_low, 1), ("m", "r", "z"))
    grad_mixed = dot_nt(up_low, w_out[1]).astype(LOW)
    grad_packed = attention("time", half, packed_time, grad_mixed).reshape(-1, 3 * D)
    grad_packed = advance(grad_packed, head_job, contract_job, out_job)
    in_job = product(
        reduce_layer, normed_time, *halves(grad_packed, 1), ("m", "r", "z"), 2
    )
    grad_normed = dot_nt(grad_packed, w_in[1])
    inward, gain_one = norm_backward(after_space, gain_all[1], grad_normed)
    grad_space = swap_frames((grad_time + inward).reshape(FRAMES, -1, D)).reshape(-1, D)
    up_low = grad_space.astype(LOW)
    up_low = advance(up_low, head_job, contract_job, in_job)
    first_out_job = product(reduce_layer, mixed_space, *halves(up_low, 1), ("r", "m", "z"))
    grad_mixed = dot_nt(up_low, w_out[0]).astype(LOW)
    grad_mixed = advance(grad_mixed, first_out_job)
    grad_packed = attention("space", small, packed_space, grad_mixed)
    grad_packed = advance(
        grad_packed, head_job, contract_job, expand_job, in_job
    )
    first_in_job = product(
        reduce_layer, normed_space, *halves(grad_packed, 1), ("r", "m", "z"), 2
    )
    grad_normed = dot_nt(grad_packed, w_in[0])
    grad_normed = advance(grad_normed, first_in_job, head_job, expand_job, out_job)
    early_job = Job(reduce_deep([expand_job.result], [block]))
    inward, gain_zero = norm_backward(start, gain_all[0], grad_normed)
    grad_start = grad_space + inward
    mask_grad = jnp.sum(grad_start * space_mask[:, None], axis=0)
    chosen = (jnp.where(space_mask > 0, -1, space_codes)[:, None] == code_ids[None, :]).astype(LOW)
    start_low = grad_start.astype(LOW)
    embed_job = product(reduce_table, chosen, *halves(start_low, 1))

    gain_grads = jnp.stack([gain_zero, gain_one, gain_two, gain_three, mask_grad])
    gain_job = Job(sum_over(gain_grads, ("h", "m", "r", "z")))
    token = jnp.zeros((), WIDE)
    token = advance(token, embed_job, gain_job, head_job, in_job, out_job, first_out_job)
    late_job = Job(reduce_deep([in_job.result, out_job.result], [None, None]))
    token = advance(token, first_in_job)
    token = advance(token, embed_job, gain_job, head_job, early_job, first_out_job)
    token = advance(token, first_in_job)
    last_job = Job(reduce_deep([first_in_job.result, first_out_job.result], [None, None]))
    token = advance(token, embed_job, gain_job, early_job, late_job)
    token = advance(token, last_job, embed_job, gain_job, late_job)

    owner = jnp.int32(0)
    for axis in ALL:
        owner = owner * lax.axis_size(axis) + lax.axis_index(axis)
    width = gains.shape[1]
    gain_grads = lax.dynamic_slice_in_dim(gain_job.finish(), owner * width, width, 1)
    jobs = (early_job, late_job, last_job, contract_job, embed_job, head_job)
    lane = jnp.arange(LANES)
    small_square = jnp.pad(jnp.sum(gain_grads * gain_grads, axis=0), (0, LANES - width))
    owned = sum(job.square for job in jobs) + small_square
    sums = jnp.stack([owned, jnp.where(lane == 0, loss_part, 0.0)])
    norm_job = Job(sum_over(sums, ("h", "m", "r", "z"), 0))
    while norm_job.flight is not None:
        token = advance(token, norm_job, *jobs)
    (up_grad,), (next_in, next_out), (first_in, first_out) = (job.finish() for job in jobs[:3])
    square_sum, loss = jnp.sum(norm_job.result, axis=1)
    norm = jnp.sqrt(square_sum)
    factor = jnp.minimum(1.0, CLIP / (norm + 1e-06))

    grads = (
        jnp.stack([first_in, next_in]),
        jnp.stack([first_out, next_out]),
        up_grad,
        contract_job.finish(),
        gain_grads,
        jnp.stack([embed_job.finish(), head_job.finish()]),
    )
    params = (attend_in, attend_out, expand, contract, gains, tables)
    firsts = (mean_in, mean_out, mean_expand, mean_contract, mean_gains, mean_tables)
    seconds = (square_in, square_out, square_expand, square_contract, square_gains, square_tables)
    rates = (RATE, RATE, RATE, RATE, RATE_SMALL, RATE)
    decays = (DECAY, DECAY, DECAY, DECAY, 0.0, DECAY)
    results = [
        adamw(p, factor * g, f, s, r, k)
        for p, g, f, s, r, k in zip(params, grads, firsts, seconds, rates, decays)
    ]
    return (loss, norm) + tuple(result[k] for k in range(3) for result in results)


def solution(mesh):
    dp, code = mesh.shape["dp"], mesh.shape["code"]
    deep = next(n for n in (4, 2, 1) if dp % n == 0)
    fine = Mesh(mesh.devices.reshape(deep, dp // deep, MICRO, code // MICRO), ALL)
    group = ("z", "r")
    weights = (
        P(None, ALL, None),
        P(None, ALL, None),
        P(ALL, None),
        P(ALL, None),
        P(None, ALL),
        P(None, ("m", "h"), None),
    )
    return jax.shard_map(
        on_device,
        mesh=fine,
        in_specs=(
            P(None, group, None, None),
            P(None, group, None, None),
            P(None, group),
            P(None, group, None),
        )
        + weights * 3,
        out_specs=(P(), P()) + weights * 3,
        check_vma=False,
    )
```
